32 devices in a mesh: groups: 2 (over x), tile: 16 (over z, y, core).
Axes of the slice: x: 2, y: 2, z: 4, core: 2. Of those that a mesh axis runs over, the one named last changes fastest.
Arguments:
- bands: bfloat16 [6144, 1312], P(('groups', 'tile')), parts along dimension 0, may hold values from -6 to 6
- send_table: int32 [16, 384], P('tile'), may hold values from 0 to 191, as said below
- recv_table: int32 [4, 3072], P(None, 'tile'), may hold values from 0 to 383, as said below
- regrid_weight: bfloat16 [3072, 1024], P('tile'), may hold values from 0.0049743652 to 0.25
- embed_weight: bfloat16 [1312, 384], replicated, may hold values from -0.15625 to 0.15625
- norm1_gain: float32 [2, 384], replicated, may hold values from 0.5 to 1.5
- qkv_weight: bfloat16 [2, 384, 1152], replicated, may hold values from -0.3125 to 0.3125
- rel_bias: float32 [2, 12, 225], replicated, may hold values from -6 to 400
- proj_weight: bfloat16 [2, 384, 384], replicated, may hold values from -0.3125 to 0.3125
- norm2_gain: float32 [2, 384], replicated, may hold values from 0.5 to 1.5
- up_weight: bfloat16 [2, 384, 1536], replicated, may hold values from -0.3125 to 0.3125
- down_weight: bfloat16 [2, 1536, 384], replicated, may hold values from -0.15625 to 0.15625
- unembed_weight: bfloat16 [384, 1312], replicated, may hold values from -0.3125 to 0.3125
Outputs:
- increment: float32 [6144, 1312], P(('groups', 'tile')), parts along dimension 0
The draws below stay inside these ranges and needn't reach their ends.
There are 2 independent parts, one for each index of `groups`. The reference program is written for one: setup_inputs(seed, part) draws one part's arguments, and reference() takes and returns one part's arrays. A program takes and returns all parts, laid end to end along the dimension named above; an argument that names none is the same for every part. Nothing has to cross between parts.
Inputs may be any that keep to these rules, and one draw needn't show every extreme that they name: `send_table`: row s lists 24 local block indices of device s for each receiving device in order; every local block appears exactly twice in a row. `recv_table`: slot s * 24 + c of a device is the c-th block that device s passes to it; for each l, rows 2 * l and 2 * l + 1 of a device's patches together name each of its 384 slots exactly once.
All inputs are finite; a program needn't handle non-finite values.
Results may differ from the reference program's by a relative error of at most 0.018.
Values may be sent and summed in bfloat16 or wider, within the bound.
No kernel may reach another device: no remote copies, remote signals or barrier semaphores. Data moves between devices by JAX's collectives and lax.ppermute only.
A program may use at most 128 MiB of HBM per device.

```python
import math
import jax
import jax.numpy as jnp
import numpy as np
from jax import lax

D = 384
HEADS = 12
FFH = 1536
CH = 82
PIX = 16
WIN = 8
K = 4
BLOCKS = 2
ROWS = 24
PD = 192
CAP = 24
NP = 3072
NB = 3072
NC = 128
N_TILE = 16


def draw_send_table(key, part):
    base = jax.random.fold_in(key, 11)

    def one_row(sender):
        first_half = jax.random.permutation(jax.random.fold_in(base, 2 * sender), PD)
        second_half = jax.random.permutation(jax.random.fold_in(base, 2 * sender + 1), PD)
        return jnp.concatenate([first_half, second_half]).astype(jnp.int32)
    return jax.vmap(one_row)(jnp.arange(N_TILE))


def draw_recv_table(key, part):
    base = jax.random.fold_in(key, 23)

    def one_device(device):
        levels = [jax.random.permutation(jax.random.fold_in(base, device * K + pass_index), 2 * PD) for pass_index in range(K // 2)]
        return jnp.stack(levels).reshape(K, PD).astype(jnp.int32)
    stacked = jax.vmap(one_device)(jnp.arange(N_TILE))
    return stacked.transpose(1, 0, 2).reshape(K, N_TILE * PD).astype(jnp.int32)


def draw_rel_bias(key, part):
    base = jax.random.fold_in(key, 37)
    span = 2 * WIN - 1
    table = jnp.clip(jax.random.normal(base, (BLOCKS, HEADS, span * span), jnp.float32), -6.0, 6.0)
    return table


def shard_levels(own_key, extent, pieces, low, high):
    gain = 1.0
    for dim, blocks in pieces:
        steps = jax.random.uniform(jax.random.fold_in(jax.random.fold_in(own_key, 6), dim), (blocks,), jnp.float32, low / len(pieces), high / len(pieces))
        gain = gain * jnp.repeat(jnp.exp(steps), extent[dim] // blocks).reshape((-1,) + (1,) * (len(extent) - 1 - dim))
    return gain


def bell_draw(key, dims, deviation, reach, cuts=(), kind=jnp.bfloat16):
    values = jax.random.normal(key, dims, jnp.float32) * deviation
    if len(cuts) > 0:
        values = shard_levels(key, dims, cuts, -0.22, 0.18) * values
    return jnp.clip(values, min=-reach, max=reach).astype(kind)


def setup_inputs(seed: int = 0, part: int = 0) -> dict:
    key_list = jax.random.split(jax.random.key(seed), 14)
    part_keys = jax.random.split(jax.random.fold_in(key_list[13], part), 14)
    return {
        "bands": bell_draw(part_keys[0], (NB, PIX * CH), 1.0, 6.0, ((0, 16),)),
        "send_table": draw_send_table(jax.random.fold_in(key_list[13], 71), part),
        "recv_table": draw_recv_table(jax.random.fold_in(key_list[13], 71), part),
        "regrid_weight": jnp.clip(jnp.exp(math.log(0.25) - 3.9171631 * jax.random.uniform(key_list[3], (NP, K * PIX * PIX), jnp.float32) ** shard_levels(key_list[3], (NP, K * PIX * PIX), ((0, 16),), -0.2, 0.2)), 0.0049743652, 0.25).astype(jnp.bfloat16),
        "embed_weight": bell_draw(key_list[4], (PIX * CH, D), (PIX * CH) ** -0.5, 0.15625),
        "norm1_gain": jnp.clip(1.0 + 0.1 * jax.random.normal(key_list[5], (BLOCKS, D), jnp.float32), 0.5, 1.5),
        "qkv_weight": bell_draw(key_list[6], (BLOCKS, D, 3 * D), D ** -0.5, 0.3125),
        "rel_bias": draw_rel_bias(jax.random.fold_in(key_list[13], 71), part),
        "proj_weight": bell_draw(key_list[8], (BLOCKS, D, D), D ** -0.5, 0.3125),
        "norm2_gain": jnp.clip(1.0 + 0.1 * jax.random.normal(key_list[9], (BLOCKS, D), jnp.float32), 0.5, 1.5),
        "up_weight": bell_draw(key_list[10], (BLOCKS, D, FFH), D ** -0.5, 0.3125),
        "down_weight": bell_draw(key_list[11], (BLOCKS, FFH, D), FFH ** -0.5, 0.15625),
        "unembed_weight": bell_draw(key_list[12], (D, PIX * CH), D ** -0.5, 0.3125),
    }


norm_eps = 1e-05

def offset_onehot(window_side):
    coords = np.arange(window_side * window_side)
    row_pos = coords // window_side
    col_pos = coords % window_side
    span = 2 * window_side - 1
    offset_index = (row_pos[:, None] - row_pos[None, :] + window_side - 1) * span + (col_pos[:, None] - col_pos[None, :] + window_side - 1)
    return (offset_index.reshape(-1)[:, None] == np.arange(span * span)[None, :]).astype(np.float32)

def window_bias(bias_rows):
    lookup = jnp.asarray(offset_onehot(WIN).T)
    flat_bias = jnp.dot(bias_rows, lookup, precision=lax.Precision.HIGHEST)
    return flat_bias.reshape(bias_rows.shape[0], WIN * WIN, WIN * WIN)

def layer_norm(values, gain_vector):
    average = lax.optimization_barrier(jnp.mean(values, axis=-1, keepdims=True))
    centred = values - average
    spread = lax.optimization_barrier(jnp.mean(centred * centred, axis=-1, keepdims=True))
    return centred * lax.rsqrt(spread + norm_eps) * gain_vector

def attend(token_grid, gain_vector, qkv_block, proj_block, bias_table, shifted):
    grid_rows, grid_cols, width = token_grid.shape
    head_count = bias_table.shape[0]
    head_size = width // head_count
    shift_by = WIN // 2
    if shifted:
        rolled = jnp.roll(token_grid, -shift_by, axis=0).astype(jnp.float32)
    else:
        rolled = token_grid.astype(jnp.float32)
    normed = layer_norm(rolled, gain_vector).astype(jnp.bfloat16)
    window_rows = grid_rows // WIN
    window_cols = grid_cols // WIN
    window_count = window_rows * window_cols
    windows = normed.reshape(window_rows, WIN, window_cols, WIN, width).transpose(0, 2, 1, 3, 4).reshape(window_count * WIN * WIN, width)
    packed = jnp.dot(windows, qkv_block, preferred_element_type=jnp.float32).astype(jnp.bfloat16)
    packed = packed.reshape(window_count, WIN * WIN, 3, head_count, head_size)
    query_rows = packed[:, :, 0].astype(jnp.float32)
    key_rows = packed[:, :, 1].astype(jnp.float32)
    value_rows = packed[:, :, 2].astype(jnp.float32)
    scores = jnp.einsum('wihd,wjhd->whij', query_rows, key_rows) * head_size ** (-0.5) + bias_table[None]
    if shifted:
        last_row = jnp.arange(window_count) // window_cols == window_rows - 1
        upper_half = jnp.arange(WIN * WIN) // WIN >= shift_by
        same_side = upper_half[:, None] == upper_half[None, :]
        allowed = jnp.logical_or(jnp.logical_not(last_row)[:, None, None, None], same_side[None, None])
        scores = jnp.where(allowed, scores, -1e+30)
    row_max = lax.optimization_barrier(jnp.max(scores, axis=-1, keepdims=True))
    weights_exp = jnp.exp(scores - row_max)
    probs = (weights_exp / lax.optimization_barrier(jnp.sum(weights_exp, axis=-1, keepdims=True))).astype(jnp.bfloat16)
    mixed_heads = jnp.einsum('whij,wjhd->wihd', probs.astype(jnp.float32), value_rows).astype(jnp.bfloat16)
    mixed_heads = mixed_heads.reshape(window_count * WIN * WIN, width)
    result = jnp.dot(mixed_heads, proj_block, preferred_element_type=jnp.float32).astype(jnp.bfloat16)
    result = result.reshape(window_rows, window_cols, WIN, WIN, width).transpose(0, 2, 1, 3, 4).reshape(grid_rows, grid_cols, width)
    if shifted:
        return jnp.roll(result, shift_by, axis=0)
    return result

def swin_update(state, attended, gain_vector, up_block, down_block):
    residual = state.astype(jnp.float32) + attended.astype(jnp.float32)
    normed = layer_norm(residual, gain_vector).astype(jnp.bfloat16)
    hidden = jax.nn.gelu(jnp.dot(normed, up_block, preferred_element_type=jnp.float32)).astype(jnp.bfloat16)
    return (residual + jnp.dot(hidden, down_block, preferred_element_type=jnp.float32)).astype(jnp.bfloat16)

def reference(bands, send_table, recv_table, regrid_weight, embed_weight, norm1_gain, qkv_weight, rel_bias, proj_weight, norm2_gain, up_weight, down_weight, unembed_weight):

    def sources(device):
        slot_ids = lax.dynamic_slice_in_dim(recv_table, device * PD, PD, 1)
        sender = slot_ids // CAP
        local_index = send_table[sender, device * CAP + slot_ids % CAP]
        return (sender * PD + local_index).astype(jnp.int32)

    def mixing_of(device):
        rows_here = lax.dynamic_slice_in_dim(regrid_weight, device * PD, PD, 0)
        return rows_here.astype(jnp.float32).reshape(PD, K, PIX, PIX)

    def forward_one(device):
        blocks = bands[sources(device)].astype(jnp.float32).reshape(K, PD, PIX, CH)
        mixed = jnp.einsum('pkij,kpjc->pic', mixing_of(device), blocks)
        return mixed.astype(jnp.bfloat16).reshape(PD, PIX * CH)
    devices = jnp.arange(N_TILE, dtype=jnp.int32)
    pixels = lax.map(forward_one, devices).reshape(NP, PIX * CH)
    state = jnp.dot(pixels, embed_weight, preferred_element_type=jnp.float32).astype(jnp.bfloat16)
    for block_index in range(BLOCKS):
        bias_table = window_bias(rel_bias[block_index])
        token_grid = state.reshape(N_TILE, ROWS, WIN, D).transpose(1, 0, 2, 3).reshape(ROWS, NC, D)
        if block_index % 2 == 0:
            attended = attend(token_grid, norm1_gain[block_index], qkv_weight[block_index], proj_weight[block_index], bias_table, False)
        else:
            shifted_grid = jnp.roll(token_grid, -(WIN // 2), axis=1)
            attended = jnp.roll(attend(shifted_grid, norm1_gain[block_index], qkv_weight[block_index], proj_weight[block_index], bias_table, True), WIN // 2, axis=1)
        attended = attended.reshape(ROWS, N_TILE, WIN, D).transpose(1, 0, 2, 3).reshape(NP, D)
        state = swin_update(state, attended, norm2_gain[block_index], up_weight[block_index], down_weight[block_index])
    out_pixels = jnp.dot(state, unembed_weight, preferred_element_type=jnp.float32).astype(jnp.bfloat16)

    def back_one(running, device):
        out_block = lax.dynamic_slice_in_dim(out_pixels, device * PD, PD, 0).astype(jnp.float32).reshape(PD, PIX, CH)
        contribution = jnp.einsum('pkij,pic->kpjc', mixing_of(device), out_block).reshape(K * PD, PIX * CH)
        slot_ids = lax.dynamic_slice_in_dim(recv_table, device * PD, PD, 1).reshape(-1)
        slot_sums = jnp.zeros((2 * PD, PIX * CH), jnp.float32).at[slot_ids].add(contribution)
        slot_sums = lax.optimization_barrier(slot_sums.astype(jnp.bfloat16)).astype(jnp.float32)
        slot_index = jnp.arange(2 * PD, dtype=jnp.int32)
        sender = slot_index // CAP
        local_index = send_table[sender, device * CAP + slot_index % CAP]
        owners = (sender * PD + local_index).astype(jnp.int32)
        return (running.at[owners].add(slot_sums), None)
    increment, _ = lax.scan(back_one, jnp.zeros((NB, PIX * CH), jnp.float32), devices)
    return increment
```

```python
import jax
import jax.numpy as jnp
import numpy as np
from jax import lax
from jax.experimental import pallas as pl
from jax.experimental.pallas import tpu as pltpu
from jax.sharding import PartitionSpec as P

WIN = 8
ROWS = 24
K = 4
LANES = 128
GROUP = 8

norm_eps = 1e-05
F32 = jnp.float32
BF16 = jnp.bfloat16


def iota(shape, axis):
    return lax.broadcasted_iota(jnp.int32, shape, axis)


def mm(a, b):
    return jnp.dot(a, b, preferred_element_type=F32)


def mm_tn(a, b):
    return lax.dot_general(a, b, (((0,), (0,)), ((), ())), preferred_element_type=F32)


def mm_nt(a, b):
    return lax.dot_general(a, b, (((1,), (1,)), ((), ())), preferred_element_type=F32)


def full(x):
    return pl.BlockSpec(memory_space=pltpu.VMEM)


def call(kernel, outs, args, any_args=(), scratch=(), flops=0, name=None):
    in_specs = [pl.BlockSpec(memory_space=pltpu.VMEM)] * len(args)
    in_specs += [pl.BlockSpec(memory_space=pl.ANY)] * len(any_args)
    moved = sum(int(np.prod(a.shape)) * a.dtype.itemsize for a in [*args, *any_args, *outs])
    many = len(outs) > 1
    return pl.pallas_call(
        kernel,
        out_shape=tuple(outs) if many else outs[0],
        in_specs=in_specs,
        out_specs=tuple([full(o) for o in outs]) if many else full(outs[0]),
        scratch_shapes=list(scratch),
        compiler_params=pltpu.CompilerParams(vmem_limit_bytes=48 << 20),
        cost_estimate=pl.CostEstimate(flops=int(flops), bytes_accessed=moved, transcendentals=0),
        name=name,
    )(*args, *any_args)


def sds(shape, dtype):
    return jax.ShapeDtypeStruct(shape, dtype)


def pick_kernel(bands_ref, send_ref, out_ref):
    rows, slots = bands_ref.shape[0], send_ref.shape[1]
    onehot = (iota((rows, slots), 0) == send_ref[...]).astype(F32).astype(BF16)
    out_ref[...] = mm_tn(onehot, bands_ref[...]).astype(BF16)


def spread(weights, fixed_first, pix):
    rows = weights.shape[0]
    width = pix * GROUP
    shape = (pix * pix, pix * width)
    r, c = iota(shape, 0), iota(shape, 1)
    outer, inner = c // width, (c % width) // GROUP
    if fixed_first:
        sel = (r // pix == outer) & (r % pix == inner)
    else:
        sel = (r % pix == outer) & (r // pix == inner)
    out = mm(weights, sel.astype(F32).astype(BF16))
    own = iota(out.shape, 0) % GROUP == iota(out.shape, 1) % GROUP
    return jnp.where(own, out, 0.0)


def store_spread(out_ref, value, place, pix):
    groups = value.shape[0] // GROUP
    width = pix * GROUP
    for o in range(0, pix, 2):
        lo = value[:, o * width : (o + 1) * width].reshape(groups, GROUP, width)
        hi = value[:, (o + 1) * width : (o + 2) * width].reshape(groups, GROUP, width)
        both = jnp.concatenate([lo, hi], axis=1).astype(BF16)
        out_ref[:, o * GROUP : (o + 2) * GROUP, place * width : (place + 1) * width] = both


def prep_kernel(recv_col_ref, recv_ref, weight_ref, gather_ref, mix_ref, wsend_ref, select_ref):
    kk, pd = recv_ref.shape
    slots = 2 * pd
    pixsq = weight_ref.shape[1] // kk
    pix = int(round(pixsq**0.5))
    rows = kk * pd
    gather_ref[...] = (recv_col_ref[...] == iota((rows, slots), 1)).astype(F32).astype(BF16)
    r = iota((rows, pd), 0)
    slot = (r // (2 * GROUP)) * GROUP + r % GROUP
    level = (r // GROUP) % 2
    total = None
    chosen = None
    for k in range(kk):
        hit = (recv_ref[k : k + 1, :] == slot) & (level == k // 2)
        hit = hit.astype(F32)
        w_k = weight_ref[:, k * pixsq : (k + 1) * pixsq]
        term = mm(hit.astype(BF16), w_k)
        total = term if total is None else total + term
        chosen = hit if chosen is None else chosen + hit
        store_spread(mix_ref, spread(w_k, True, pix), k, pix)
    wsend_ref[...] = total.astype(BF16)
    select_ref[...] = chosen.astype(BF16)


def prep_back_kernel(weight_ref, mix_ref):
    rows, pixsq = weight_ref.shape
    pix = int(round(pixsq**0.5))
    groups = rows // (2 * GROUP)
    w3 = weight_ref[...].astype(F32).reshape(groups, 2, GROUP, pixsq)
    for level in range(2):
        w_l = w3[:, level].reshape(groups * GROUP, pixsq).astype(BF16)
        store_spread(mix_ref, spread(w_l, False, pix), level, pix)


def layer_norm(values, gain):
    average = jnp.mean(values, axis=-1, keepdims=True)
    centred = values - average
    spread_ = jnp.mean(centred * centred, axis=-1, keepdims=True)
    return centred * lax.rsqrt(spread_ + norm_eps) * gain


def softmax_parts(scores, side):
    out = []
    for m in range(scores.shape[1] // LANES):
        part = scores[:, m * LANES : (m + 1) * LANES]
        low = iota(part.shape, 1) % LANES < side
        top_lo = jnp.max(jnp.where(low, part, -3e38), axis=-1, keepdims=True)
        top_hi = jnp.max(jnp.where(low, -3e38, part), axis=-1, keepdims=True)
        out.append(jnp.exp(part - jnp.where(low, top_lo, top_hi)))
    return jnp.concatenate(out, axis=1)


def attend_rows(query, key, value, bias, heads, blocked):
    m, d = query.shape
    size = d // heads
    span = key.shape[0]
    head_of = iota((heads * span, d), 0) // span == iota((heads * span, d), 1) // size
    mask = head_of.astype(F32).astype(BF16)
    key_all = jnp.concatenate([key] * heads, axis=0) * mask
    value_all = jnp.concatenate([value] * heads, axis=0) * mask
    scores = mm_nt(query, key_all) * size ** (-0.5) + bias
    if blocked is not None:
        scores = jnp.where(blocked, -1e30, scores)
    weights = softmax_parts(scores, span)
    weights16 = weights.astype(BF16)
    total = mm(weights16, mask)
    return (mm(weights16, value_all) / total).astype(BF16)


def feed_forward(residual, gain2, up, down):
    normed = layer_norm(residual, gain2).astype(BF16)
    hidden = jax.nn.gelu(mm(normed, up)).astype(BF16)
    return (residual + mm(hidden, down)).astype(BF16)


def start(copies):
    for c in copies:
        c.start()
    return copies


def to_vmem(pairs, sem):
    return [pltpu.make_async_copy(a, b, sem.at[i]) for i, (a, b) in enumerate(pairs)]


def lay_tiles(rows, count):
    return jnp.concatenate([rows[:, t * LANES : (t + 1) * LANES] for t in range(count)], axis=0)


def first_kernel(
    inc_ref, gather_ref, gain1_ref, gain2_ref, bias_ref,
    mix_any, embed_any, qkv_any, proj_any, up_any, down_any,
    low_ref, high_ref,
    x_ref, p_ref, pix_ref, mix_ref, embed_ref, qkv_ref, proj_ref, up_ref, down_ref, sem,
):
    copies = start(to_vmem(
        [(mix_any, mix_ref), (embed_any, embed_ref), (qkv_any, qkv_ref), (proj_any, proj_ref),
         (up_any, up_ref), (down_any, down_ref)], sem))
    slots, width = inc_ref.shape
    pix = pix_ref.shape[1] // LANES
    ch = width // pix
    pd, d = embed_ref.shape[1] and pix_ref.shape[0], embed_ref.shape[1]
    kk = p_ref.shape[0]
    groups = pd // GROUP
    heads = bias_ref.shape[1] // (WIN * WIN)
    for j in range(pix):
        lo = (ch * j // LANES) * LANES
        hi = min(lo + 2 * LANES, width)
        off = ch * j - lo
        shape = (hi - lo, LANES)
        move = (iota(shape, 0) - off == iota(shape, 1)) & (iota(shape, 1) < ch)
        move = move.astype(F32).astype(BF16)
        x_ref[:, j * LANES : (j + 1) * LANES] = mm(inc_ref[:, lo:hi], move).astype(BF16)
    for j in range(0, pix, 2):
        cols = slice(j * LANES, (j + 2) * LANES)
        got = mm(gather_ref[...], x_ref[:, cols])
        for k in range(kk):
            p_ref[k, :, cols] = got[k * pd : (k + 1) * pd]
    copies[0].wait()

    def mix_group(g, carry):
        at = pl.ds(pl.multiple_of(g * GROUP, GROUP), GROUP)
        data = jnp.concatenate([lay_tiles(p_ref[k, at, :], pix) for k in range(kk)], axis=0)
        out = mm(mix_ref[g], data.astype(BF16))
        for i in range(pix):
            pix_ref[at, i * LANES : (i + 1) * LANES] = out[i * GROUP : (i + 1) * GROUP]
        return carry

    lax.fori_loop(0, groups, mix_group, 0, unroll=4)
    copies[1].wait()
    state = mm(pix_ref[...].astype(BF16), embed_ref[...]).astype(BF16).astype(F32)
    normed = layer_norm(state, gain1_ref[...]).astype(BF16)
    copies[2].wait()
    packed = mm(normed, qkv_ref[...]).astype(BF16)
    query, key, value = packed[:, :d], packed[:, d : 2 * d], packed[:, 2 * d :]
    half = pd // 2
    win_rows = ROWS // WIN
    part = half // win_rows
    mixed = [None] * (2 * win_rows)
    for w in range(win_rows):
        def rows(v):
            return jnp.concatenate(
                [v[w * part : (w + 1) * part], v[half + w * part : half + (w + 1) * part]], axis=0)
        out = attend_rows(rows(query), rows(key), rows(value), bias_ref[...], heads, None)
        mixed[w] = out[:part]
        mixed[win_rows + w] = out[part:]
    mixed = jnp.concatenate(mixed, axis=0)
    copies[3].wait()
    attended = mm(mixed, proj_ref[...]).astype(BF16)
    residual = state + attended.astype(F32)
    copies[4].wait()
    copies[5].wait()
    new = feed_forward(residual, gain2_ref[...], up_ref[...], down_ref[...])
    low_ref[...] = new[:half]
    high_ref[...] = new[half:]


def second_kernel(
    low_ref, high_ref, left_ref, right_ref, gain1_ref, gain2_ref, bias_ref,
    select_any, qkv_any, proj_any, up_any, down_any,
    out_ref,
    select_ref, qkv_ref, proj_ref, up_ref, down_ref, sem,
):
    copies = start(to_vmem(
        [(qkv_any, qkv_ref), (proj_any, proj_ref), (up_any, up_ref), (down_any, down_ref),
         (select_any, select_ref)], sem))
    half, d = low_ref.shape
    heads = bias_ref.shape[1] // (WIN * WIN)
    shift = half * (WIN // 2) // ROWS
    turn = lambda v: jnp.concatenate([v[shift:], v[:shift]], axis=0)
    back = lambda v: jnp.concatenate([v[half - shift :], v[: half - shift]], axis=0)
    own = jnp.concatenate([turn(low_ref[...]), turn(high_ref[...])], axis=0).astype(F32)
    strips = jnp.concatenate([turn(left_ref[...]), turn(right_ref[...])], axis=0).astype(F32)
    gain1 = gain1_ref[...]
    normed = layer_norm(own, gain1).astype(BF16)
    normed_s = layer_norm(strips, gain1).astype(BF16)
    copies[0].wait()
    packed = mm(normed, qkv_ref[...]).astype(BF16)
    packed_s = mm(normed_s, qkv_ref[:, d:]).astype(BF16)
    query, key, value = packed[:, :d], packed[:, d : 2 * d], packed[:, 2 * d :]
    key_s, value_s = packed_s[:, :d], packed_s[:, d:]
    win_rows = ROWS // WIN
    part = half // win_rows
    bias = bias_ref[...]
    span = WIN * WIN
    outs = [[], []]
    for w in range(win_rows):
        near = slice(w * part, (w + 1) * part)
        far = slice(half + w * part, half + (w + 1) * part)
        for side in range(2):
            if side == 0:
                q = query[near]
                k = jnp.concatenate([key_s[near], key[near]], axis=0)
                v = jnp.concatenate([value_s[near], value[near]], axis=0)
                b = bias[part:]
            else:
                q = query[far]
                k = jnp.concatenate([key[far], key_s[far]], axis=0)
                v = jnp.concatenate([value[far], value_s[far]], axis=0)
                b = bias[:part]
            blocked = None
            if w == win_rows - 1:
                shape = (part, heads * span)
                q_up = iota(shape, 0) % part >= part // 2
                k_up = iota(shape, 1) % part >= part // 2
                blocked = q_up != k_up
            outs[side].append(attend_rows(q, k, v, b, heads, blocked))
    mixed = jnp.concatenate(outs[0] + outs[1], axis=0)
    copies[1].wait()
    attended = mm(mixed, proj_ref[...]).astype(BF16)
    residual = own + attended.astype(F32)
    copies[2].wait()
    copies[3].wait()
    new = feed_forward(residual, gain2_ref[...], up_ref[...], down_ref[...])
    state = jnp.concatenate([back(new[:half]), back(new[half:])], axis=0)
    copies[4].wait()
    out_ref[...] = mm(select_ref[...], state).astype(BF16)


def last_kernel(state_ref, send_ref, unembed_ref, mix_any, out_ref, p_ref, slot_ref, mix_ref, sem):
    copy = pltpu.make_async_copy(mix_any, mix_ref, sem.at[0])
    copy.start()
    rows, d = state_ref.shape
    width = unembed_ref.shape[1]
    pix = width // LANES
    pd, total = out_ref.shape
    ch = total // pix
    groups = rows // (2 * GROUP)
    for j in range(0, pix, 2):
        cols = slice(j * LANES, (j + 2) * LANES)
        p_ref[:, cols] = mm(state_ref[...], unembed_ref[:, cols])
    copy.wait()

    def mix_group(g, carry):
        at = pl.ds(pl.multiple_of(g * 2 * GROUP, 2 * GROUP), 2 * GROUP)
        got = p_ref[at, :]
        data = jnp.concatenate([lay_tiles(got[:GROUP], pix), lay_tiles(got[GROUP:], pix)], axis=0)
        out = mm(mix_ref[g], data.astype(BF16))
        to = pl.ds(pl.multiple_of(g * GROUP, GROUP), GROUP)
        for i in range(pix):
            slot_ref[to, i * LANES : (i + 1) * LANES] = out[i * GROUP : (i + 1) * GROUP]
        return carry

    lax.fori_loop(0, groups, mix_group, 0, unroll=4)
    onehot = (iota((pd, send_ref.shape[1]), 0) == send_ref[...]).astype(F32).astype(BF16)
    tiles = [None] * (-(-total // LANES))
    for j in range(0, pix, 2):
        both = mm(onehot, slot_ref[:, j * LANES : (j + 2) * LANES].astype(BF16))
        for jj in (j, j + 1):
            val = both[:, (jj - j) * LANES : (jj - j + 1) * LANES]
            t, off = divmod(ch * jj, LANES)
            if off:
                val = pltpu.roll(val, off, 1)
            lane = iota(val.shape, 1)
            for tt, piece in ((t, jnp.where(lane >= off, val, 0.0)), (t + 1, jnp.where(lane < off, val, 0.0))):
                if tt == t + 1 and off + ch <= LANES:
                    continue
                tiles[tt] = piece if tiles[tt] is None else tiles[tt] + piece
    for t, tile in enumerate(tiles):
        hi = min((t + 1) * LANES, total)
        out_ref[:, t * LANES : hi] = tile[:, : hi - t * LANES]


def swap(value, axis):
    return lax.all_to_all(value, axis, split_axis=0, concat_axis=0, tiled=True)


def swap_pairs(value, axis):
    count = lax.axis_size(axis)
    rows, width = value.shape
    cap = rows // (2 * count)
    if cap % GROUP == 0:
        return swap(value, axis)
    groups = rows // (2 * GROUP)
    v = value.reshape(groups, 2, GROUP, width).transpose(1, 0, 2, 3).reshape(2, count, cap, width)
    v = swap(v.transpose(1, 0, 2, 3).reshape(rows, width), axis)
    v = v.reshape(count, 2, cap, width).transpose(1, 0, 2, 3).reshape(2, groups, GROUP, width)
    return v.transpose(1, 0, 2, 3).reshape(rows, width)


def from_behind(value, axis, steps):
    count = lax.axis_size(axis)
    pairs = [(source, (source + steps) % count) for source in range(count)]
    return lax.ppermute(value, axis, pairs)


def bias_tables(rel_bias):
    blocks, heads, entries = rel_bias.shape
    span = WIN * WIN
    pos = jnp.arange(span)
    half = WIN // 2
    row = (pos % (span // 2)) // half
    col = (pos // (span // 2)) * half + pos % half
    wide = 2 * WIN - 1
    index = (row[:, None] - row[None] + WIN - 1) * wide + col[:, None] - col[None] + WIN - 1
    onehot = (jnp.arange(entries)[:, None] == index.reshape(1, -1)).astype(BF16)
    rest = rel_bias.reshape(blocks * heads, entries)
    parts = []
    for _ in range(3):
        top = lax.reduce_precision(rest, 8, 7)
        parts.append(top)
        rest = rest - top
    stacked = jnp.concatenate(parts, axis=0).astype(BF16)
    got = jnp.dot(stacked, onehot, preferred_element_type=F32)
    got = got.reshape(3, blocks, heads, span, span)
    got = (got[0] + got[1]) + got[2]
    return got.transpose(0, 2, 1, 3).reshape(blocks, span, heads * span)


def body(
    bands, send_table, recv_table, regrid_weight, embed_weight, norm1_gain, qkv_weight, rel_bias,
    proj_weight, norm2_gain, up_weight, down_weight, unembed_weight,
):
    pd, width = bands.shape
    slots = send_table.shape[1]
    kk = recv_table.shape[0]
    d = embed_weight.shape[1]
    pixsq = regrid_weight.shape[1] // kk
    pix = int(round(pixsq**0.5))
    ch = width // pix
    half_cols = WIN // 2
    heads = rel_bias.shape[1]
    wide = pix * LANES
    ffh = up_weight.shape[2]
    groups = pd // GROUP

    outgoing = call(pick_kernel, [sds((slots, width), BF16)], [bands, send_table],
                    flops=2 * slots * pd * width, name="pick")
    incoming = swap(outgoing, "tile")

    recv = recv_table.reshape(kk, ROWS, 2, half_cols).transpose(0, 2, 1, 3).reshape(kk, pd)
    weight = regrid_weight.reshape(ROWS, 2, half_cols, kk * pixsq).transpose(1, 0, 2, 3)
    weight = weight.reshape(pd, kk * pixsq)
    gather, mix, wsend, select = call(
        prep_kernel,
        [sds((kk * pd, slots), BF16), sds((groups, pix * GROUP, kk * pix * GROUP), BF16),
         sds((kk * pd, pixsq), BF16), sds((kk * pd, pd), BF16)],
        [recv.reshape(kk * pd, 1), recv, weight], flops=2e9, name="prep")
    embed_pad = jnp.pad(embed_weight.reshape(pix, ch, d), ((0, 0), (0, LANES - ch), (0, 0)))
    embed_pad = embed_pad.reshape(wide, d)
    unembed_pad = jnp.pad(unembed_weight.reshape(d, pix, ch), ((0, 0), (0, 0), (0, LANES - ch)))
    unembed_pad = unembed_pad.reshape(d, wide)
    bias = bias_tables(rel_bias)

    wback = swap_pairs(wsend, "tile")

    vm = pltpu.VMEM
    half = pd // 2
    layer_scratch = [vm((d, 3 * d), BF16), vm((d, d), BF16), vm((d, ffh), BF16), vm((ffh, d), BF16)]
    low, high = call(
        first_kernel,
        [sds((half, d), BF16)] * 2,
        [incoming, gather, norm1_gain[:1], norm2_gain[:1], bias[0]],
        [mix, embed_pad, qkv_weight[0], proj_weight[0], up_weight[0], down_weight[0]],
        [vm((slots, wide), BF16), vm((kk, pd, wide), F32), vm((pd, wide), F32), vm(mix.shape, BF16),
         vm((wide, d), BF16), *layer_scratch, pltpu.SemaphoreType.DMA((6,))],
        flops=4e9, name="first")
    right = from_behind(low, "tile", -1)
    left = from_behind(high, "tile", 1)
    mix_back = call(prep_back_kernel, [sds((slots // GROUP, pix * GROUP, 2 * pix * GROUP), BF16)], [wback],
                    flops=2e9, name="prep_back")
    sent = call(
        second_kernel,
        [sds((kk * pd, d), BF16)],
        [low, high, left, right, norm1_gain[1:], norm2_gain[1:], bias[1]],
        [select, qkv_weight[1], proj_weight[1], up_weight[1], down_weight[1]],
        [vm((kk * pd, pd), BF16), *layer_scratch, pltpu.SemaphoreType.DMA((5,))],
        flops=2e9, name="second")
    got = swap_pairs(sent, "tile")
    return call(
        last_kernel,
        [sds((pd, width), F32)],
        [got, send_table, unembed_pad],
        [mix_back],
        [vm((kk * pd, wide), F32), vm((slots, wide), F32), vm(mix_back.shape, BF16),
         pltpu.SemaphoreType.DMA((1,))],
        flops=3e9, name="last")


def solution(mesh):
    in_specs = (
        P(("groups", "tile"), None), P("tile", None), P(None, "tile"), P("tile", None),
        P(), P(), P(), P(), P(), P(), P(), P(), P(),
    )
    out_specs = P(("groups", "tile"), None)
    return jax.shard_map(body, mesh=mesh, in_specs=in_specs, out_specs=out_specs, check_vma=False)
```

```python
import functools

import jax
import jax.numpy as jnp
import numpy as np
from jax import lax
from jax.experimental import pallas as pl
from jax.experimental.pallas import tpu as pltpu
from jax.sharding import PartitionSpec as P

WIN = 8
ROWS = 24
K = 4
LANES = 128
GROUP = 8

norm_eps = 1e-05
F32 = jnp.float32
BF16 = jnp.bfloat16


def iota(shape, axis):
    return lax.broadcasted_iota(jnp.int32, shape, axis)


def mm(a, b):
    return jnp.dot(a, b, preferred_element_type=F32)


def mm_tn(a, b):
    return lax.dot_general(a, b, (((0,), (0,)), ((), ())), preferred_element_type=F32)


def mm_nt(a, b):
    return lax.dot_general(a, b, (((1,), (1,)), ((), ())), preferred_element_type=F32)


def full(x):
    return pl.BlockSpec(memory_space=pltpu.VMEM)


VMEM_LIMIT = 30 << 20


def call(kernel, outs, args, any_args=(), scratch=(), flops=0, name=None):
    in_specs = [pl.BlockSpec(memory_space=pltpu.VMEM)] * len(args)
    in_specs += [pl.BlockSpec(memory_space=pl.ANY)] * len(any_args)
    moved = sum(int(np.prod(a.shape)) * a.dtype.itemsize for a in [*args, *any_args, *outs])
    many = len(outs) > 1
    return pl.pallas_call(
        kernel,
        out_shape=tuple(outs) if many else outs[0],
        in_specs=in_specs,
        out_specs=tuple([full(o) for o in outs]) if many else full(outs[0]),
        scratch_shapes=list(scratch),
        compiler_params=pltpu.CompilerParams(vmem_limit_bytes=VMEM_LIMIT),
        cost_estimate=pl.CostEstimate(flops=int(flops), bytes_accessed=moved, transcendentals=0),
        name=name,
    )(*args, *any_args)


def sds(shape, dtype):
    return jax.ShapeDtypeStruct(shape, dtype)


def pick_kernel(me_ref, bands_ref, send_ref, *refs):
    outs, held = refs[:-1], refs[-1]
    rows, slots = bands_ref.shape[0], send_ref.shape[1]
    count, cap = held.shape[:2]
    onehot = (iota((rows, slots), 0) == send_ref[...]).astype(F32).astype(BF16)
    got = mm_tn(onehot, bands_ref[...])
    held[...] = got.reshape(count, cap, got.shape[1]).astype(BF16)
    me = me_ref[0]
    for s, out in enumerate(outs):
        for e in range(2):
            out[e] = held[me ^ (2 * s + e)]


def pick_all_kernel(bands_ref, send_ref, out_ref):
    rows, slots = bands_ref.shape[0], send_ref.shape[1]
    onehot = (iota((rows, slots), 0) == send_ref[...]).astype(F32).astype(BF16)
    out_ref[...] = mm_tn(onehot, bands_ref[...]).astype(BF16)


def relay_kernel(*refs):
    ins, out, sem = refs[:-2], refs[-2], refs[-1]
    copies = start([pltpu.make_async_copy(r.at[1], out.at[i], sem.at[i]) for i, r in enumerate(ins)])
    for c in copies:
        c.wait()


def spread(weights, fixed_first, pix):
    width = pix * GROUP
    shape = (pix * pix, pix * width)
    r, c = iota(shape, 0), iota(shape, 1)
    outer, inner = c // width, (c % width) // GROUP
    if fixed_first:
        sel = (r // pix == outer) & (r % pix == inner)
    else:
        sel = (r % pix == outer) & (r // pix == inner)
    out = mm(weights, sel.astype(F32).astype(BF16))
    own = iota(out.shape, 0) % GROUP == iota(out.shape, 1) % GROUP
    return jnp.where(own, out, 0.0)


def store_spread(out_ref, value, row0, col0, pix):
    groups = value.shape[0] // GROUP
    width = pix * GROUP
    for o in range(0, pix, 2):
        lo = value[:, o * width : (o + 1) * width].reshape(groups, GROUP, width)
        hi = value[:, (o + 1) * width : (o + 2) * width].reshape(groups, GROUP, width)
        both = jnp.concatenate([lo, hi], axis=1).astype(BF16)
        out_ref[:, row0 + o * GROUP : row0 + (o + 2) * GROUP, col0 : col0 + width] = both


def tile_move(ch, j, total):
    lo = (ch * j // LANES) * LANES
    hi = min(lo + 2 * LANES, total)
    shape = (hi - lo, LANES)
    move = (iota(shape, 0) - (ch * j - lo) == iota(shape, 1)) & (iota(shape, 1) < ch)
    return lo, hi, move.astype(F32).astype(BF16)


def prep_kernel(
    recv_ref, recv_col_ref, weight_ref, embed_ref, unembed_ref, bias_any,
    mix_ref, wsend_ref, select_ref, scatter_ref, embed_out, unembed_out,
):
    kk, pd = recv_ref.shape
    slots = 2 * pd
    pixsq = weight_ref.shape[1] // kk
    pix = int(round(pixsq**0.5))
    ch = embed_ref.shape[0] // pix
    r = iota((slots, pd), 0)
    totals = []
    for level in range(2):
        total = None
        for k in (2 * level, 2 * level + 1):
            hit = (recv_ref[k : k + 1, :] == r).astype(F32).astype(BF16)
            term = mm(hit, weight_ref[:, k * pixsq : (k + 1) * pixsq])
            total = term if total is None else total + term
        value = spread(total.astype(BF16), True, pix)
        store_spread(mix_ref, value, level * pix * GROUP, 0, pix)
        totals.append(total.reshape(slots // GROUP, GROUP, pixsq))
    wsend_ref[...] = jnp.concatenate(totals, axis=1).reshape(2 * slots, pixsq).astype(BF16)

    def chosen(shape, axis, row0, vals):
        r = iota(shape, axis) + row0
        slot = (r // (2 * GROUP)) * GROUP + r % GROUP
        level = (r // GROUP) % 2
        first = (vals(0) == slot) | (vals(1) == slot)
        second = (vals(2) == slot) | (vals(3) == slot)
        hit = (first & (level == 0)) | (second & (level == 1))
        return hit.astype(F32).astype(BF16)

    select_ref[...] = chosen((2 * slots, pd), 0, 0, lambda k: recv_ref[k : k + 1, :])
    parts, _, width = scatter_ref.shape
    for part in range(parts):
        scatter_ref[part] = chosen((pd, width), 1, part * width, lambda k: recv_col_ref[:, k : k + 1])
    for i in range(pix):
        lo, hi, move = tile_move(ch, i, embed_ref.shape[0])
        embed_out[i * LANES : (i + 1) * LANES, :] = mm_tn(move, embed_ref[lo:hi, :]).astype(BF16)
        unembed_out[:, i * LANES : (i + 1) * LANES] = mm(unembed_ref[:, lo:hi], move).astype(BF16)


def prep_back_kernel(weight_ref, mix_ref):
    rows, pixsq = weight_ref.shape
    pix = int(round(pixsq**0.5))
    groups = rows // (2 * GROUP)
    w3 = weight_ref[...].astype(F32).reshape(groups, 2, GROUP, pixsq)
    for level in range(2):
        w_l = w3[:, level].reshape(groups * GROUP, pixsq).astype(BF16)
        store_spread(mix_ref, spread(w_l, False, pix), 0, level * pix * GROUP, pix)


def layer_norm(values, gain):
    average = jnp.mean(values, axis=-1, keepdims=True)
    centred = values - average
    spread_ = jnp.mean(centred * centred, axis=-1, keepdims=True)
    return centred * lax.rsqrt(spread_ + norm_eps) * gain


def head_mask(heads, span, d):
    head_of = iota((heads * span, d), 0) // span == iota((heads * span, d), 1) // (d // heads)
    return head_of.astype(F32).astype(BF16)


def softmax_parts(scores, side):
    out = []
    for m in range(scores.shape[1] // LANES):
        part = scores[:, m * LANES : (m + 1) * LANES]
        low = iota(part.shape, 1) % LANES < side
        top_lo = jnp.max(jnp.where(low, part, -3e38), axis=-1, keepdims=True)
        top_hi = jnp.max(jnp.where(low, -3e38, part), axis=-1, keepdims=True)
        out.append(jnp.exp(part - jnp.where(low, top_lo, top_hi)))
    return jnp.concatenate(out, axis=1)


def attend_rows(query, key, value, bias, heads, mask, blocked):
    d = query.shape[1]
    key_all = jnp.concatenate([key] * heads, axis=0) * mask
    value_all = jnp.concatenate([value] * heads, axis=0) * mask
    scores = mm_nt(query, key_all) * (d // heads) ** (-0.5) + bias
    if blocked is not None:
        scores = jnp.where(blocked, -1e30, scores)
    weights = softmax_parts(scores, key.shape[0]).astype(BF16)
    return mm(weights, value_all), weights


def feed_forward(residual, gain2, up, down):
    normed = layer_norm(residual, gain2).astype(BF16)
    hidden = jax.nn.gelu(mm(normed, up)).astype(BF16)
    return (residual + mm(hidden, down)).astype(BF16)


def start(copies):
    for c in copies:
        c.start()
    return copies


def to_vmem(pairs, sem):
    return [pltpu.make_async_copy(a, b, sem.at[i]) for i, (a, b) in enumerate(pairs)]


def lay_tiles(rows, count):
    return jnp.concatenate([rows[:, t * LANES : (t + 1) * LANES] for t in range(count)], axis=0)


def wait(copies):
    for c in copies:
        c.wait()


def regrid_part(data, x_ref, c_ref, mix_ref, scatter, embed_ref, pix):
    slots, width = data.shape
    ch = width // pix
    for j in range(pix):
        lo, hi, move = tile_move(ch, j, width)
        x_ref[:slots, j * LANES : (j + 1) * LANES] = mm(data[:, lo:hi], move)

    def group(g, carry):
        at = pl.ds(pl.multiple_of(g * GROUP, GROUP), GROUP)
        tiles = lay_tiles(x_ref[at, :], pix).astype(BF16)
        out = mm(mix_ref[g], tiles)
        to = pl.ds(pl.multiple_of(g * 2 * GROUP, 2 * GROUP), 2 * GROUP)
        for i in range(pix):
            low = out[i * GROUP : (i + 1) * GROUP]
            high = out[(pix + i) * GROUP : (pix + i + 1) * GROUP]
            both = jnp.concatenate([low, high], axis=0).astype(BF16)
            c_ref[to, i * LANES : (i + 1) * LANES] = both
        return carry

    lax.fori_loop(0, slots // GROUP, group, 0, unroll=4)
    total = None
    for j in range(0, pix, 2):
        cols = slice(j * LANES, (j + 2) * LANES)
        pixels = None
        for p, sc in enumerate(scatter):
            rows = sc.shape[1]
            term = mm(sc, c_ref[p * rows : (p + 1) * rows, cols])
            pixels = term if pixels is None else pixels + term
        term = mm(pixels.astype(BF16), embed_ref[cols, :])
        total = term if total is None else total + term
    return total


def flat(ref):
    chunks, rows, width = ref.shape
    return ref[...].astype(F32).reshape(chunks * rows, width).astype(BF16)


def early_kernel(pix, fetch, parts, *refs):
    n = len(fetch)
    chunks, refs = refs[:n], refs[n:]
    mix_any, scatter_any, embed_any = refs[:3]
    refs = refs[3:]
    prior = refs[0] if len(refs) == 9 else None
    out_ref, data_ref, x_ref, c_ref, mix_ref, scatter_ref, embed_ref, sem = refs[-8:]
    at = 0
    copies = []
    for i, (ref, (index, count)) in enumerate(zip(chunks, fetch)):
        piece = ref.at[index] if count == 1 else ref
        to = data_ref.at[at] if count == 1 else data_ref.at[at : at + count]
        copies.append(pltpu.make_async_copy(piece, to, sem.at[3 + i]))
        at += count
    groups = mix_ref.shape[0]
    first = parts[0]
    copies += [
        pltpu.make_async_copy(
            mix_any.at[first * (groups // len(parts)) : first * (groups // len(parts)) + groups], mix_ref, sem.at[0]),
        pltpu.make_async_copy(scatter_any.at[first : first + len(parts)], scatter_ref, sem.at[1]),
        pltpu.make_async_copy(embed_any, embed_ref, sem.at[2]),
    ]
    start(copies)
    wait(copies)
    scatter = [scatter_ref[i] for i in range(len(parts))]
    total = regrid_part(flat(data_ref), x_ref, c_ref, mix_ref, scatter, embed_ref, pix)
    if prior is not None:
        total = total + prior[...]
    out_ref[...] = total


def first_kernel(
    pix, part, layer,
    prior_ref, gain1_ref, gain2_ref,
    data_any, mix_any, scatter_any, embed_any, bias_any, qkv_any, proj_any, up_any, down_any,
    low_ref, high_ref,
    data_ref, x_ref, c_ref, mix_ref, scatter_ref, embed_ref, bias_ref, qkv_ref, proj_ref, up_ref, down_ref, sem,
):
    groups = mix_ref.shape[0]
    copies = start(to_vmem(
        [(data_any, data_ref), (mix_any.at[part * groups : (part + 1) * groups], mix_ref),
         (scatter_any.at[part], scatter_ref), (embed_any, embed_ref), (qkv_any.at[layer], qkv_ref),
         (bias_any.at[layer], bias_ref), (proj_any.at[layer], proj_ref),
         (up_any.at[layer], up_ref), (down_any.at[layer], down_ref)], sem))
    wait(copies[:4])
    total = regrid_part(flat(data_ref), x_ref, c_ref, mix_ref, [scatter_ref[...]], embed_ref, pix)
    state = (prior_ref[...] + total).astype(BF16).astype(F32)
    pd, d = state.shape
    heads = bias_ref.shape[1] // (WIN * WIN)
    normed = layer_norm(state, gain1_ref[layer : layer + 1, :]).astype(BF16)
    copies[4].wait()
    packed = mm(normed, qkv_ref[...]).astype(BF16)
    query, key, value = packed[:, :d], packed[:, d : 2 * d], packed[:, 2 * d :]
    half = pd // 2
    win_rows = ROWS // WIN
    part_rows = half // win_rows
    copies[5].wait()
    mask = head_mask(heads, WIN * WIN, d)
    mixed = [None] * (2 * win_rows)
    weights = [None] * (2 * win_rows)
    for w in range(win_rows):
        def rows(v):
            lo, hi = w * part_rows, (w + 1) * part_rows
            return jnp.concatenate([v[lo:hi], v[half + lo : half + hi]], axis=0)
        out, wts = attend_rows(rows(query), rows(key), rows(value), bias_ref[...], heads, mask, None)
        mixed[w], mixed[win_rows + w] = out[:part_rows], out[part_rows:]
        weights[w], weights[win_rows + w] = wts[:part_rows], wts[part_rows:]
    total = mm(jnp.concatenate(weights, axis=0), mask)
    mixed = (jnp.concatenate(mixed, axis=0) / total).astype(BF16)
    copies[6].wait()
    attended = mm(mixed, proj_ref[...]).astype(BF16)
    residual = state + attended.astype(F32)
    wait(copies[7:])
    new = feed_forward(residual, gain2_ref[layer : layer + 1, :], up_ref[...], down_ref[...])
    low_ref[...] = new[:half]
    high_ref[...] = new[half:]


def second_kernel(
    layer, order,
    low_ref, high_ref, left_ref, right_ref, gain1_ref, gain2_ref,
    select_any, bias_any, qkv_any, proj_any, up_any, down_any,
    *refs,
):
    outs = refs[: len(refs) - 7]
    select_ref, bias_ref, qkv_ref, proj_ref, up_ref, down_ref, sem = refs[len(outs) :]
    copies = start(to_vmem(
        [(qkv_any.at[layer], qkv_ref), (bias_any.at[layer], bias_ref), (proj_any.at[layer], proj_ref),
         (up_any.at[layer], up_ref), (down_any.at[layer], down_ref), (select_any, select_ref)], sem))
    half, d = low_ref.shape
    heads = bias_ref.shape[1] // (WIN * WIN)
    shift = half * (WIN // 2) // ROWS
    turn = lambda v: jnp.concatenate([v[shift:], v[:shift]], axis=0)
    back = lambda v: jnp.concatenate([v[half - shift :], v[: half - shift]], axis=0)
    own = jnp.concatenate([turn(low_ref[...]), turn(high_ref[...])], axis=0).astype(F32)
    strips = jnp.concatenate([turn(left_ref[...]), turn(right_ref[...])], axis=0).astype(F32)
    gain1 = gain1_ref[layer : layer + 1, :]
    normed = layer_norm(own, gain1).astype(BF16)
    normed_s = layer_norm(strips, gain1).astype(BF16)
    copies[0].wait()
    packed = mm(normed, qkv_ref[...]).astype(BF16)
    packed_s = mm(normed_s, qkv_ref[:, d:]).astype(BF16)
    query, key, value = packed[:, :d], packed[:, d : 2 * d], packed[:, 2 * d :]
    key_s, value_s = packed_s[:, :d], packed_s[:, d:]
    win_rows = ROWS // WIN
    part = half // win_rows
    span = WIN * WIN
    copies[1].wait()
    bias = bias_ref[...]
    mask = head_mask(heads, span, d)
    outs_m, outs_w = [[], []], [[], []]
    for w in range(win_rows):
        near = slice(w * part, (w + 1) * part)
        far = slice(half + w * part, half + (w + 1) * part)
        for side in range(2):
            if side == 0:
                q = query[near]
                k = jnp.concatenate([key_s[near], key[near]], axis=0)
                v = jnp.concatenate([value_s[near], value[near]], axis=0)
                b = bias[part:]
            else:
                q = query[far]
                k = jnp.concatenate([key[far], key_s[far]], axis=0)
                v = jnp.concatenate([value[far], value_s[far]], axis=0)
                b = bias[:part]
            blocked = None
            if w == win_rows - 1:
                shape = (part, heads * span)
                q_up = iota(shape, 0) % part >= part // 2
                k_up = iota(shape, 1) % part >= part // 2
                blocked = q_up != k_up
            out, wts = attend_rows(q, k, v, b, heads, mask, blocked)
            outs_m[side].append(out)
            outs_w[side].append(wts)
    total = mm(jnp.concatenate(outs_w[0] + outs_w[1], axis=0), mask)
    mixed = (jnp.concatenate(outs_m[0] + outs_m[1], axis=0) / total).astype(BF16)
    copies[2].wait()
    attended = mm(mixed, proj_ref[...]).astype(BF16)
    residual = own + attended.astype(F32)
    wait(copies[3:5])
    new = feed_forward(residual, gain2_ref[layer : layer + 1, :], up_ref[...], down_ref[...])
    state = jnp.concatenate([back(new[:half]), back(new[half:])], axis=0)
    copies[5].wait()
    sent = mm(select_ref[...], state).astype(BF16)
    if order is None:
        outs[0][...] = sent
        return
    rows = sent.shape[0] // len(order)
    for pos, x in enumerate(order):
        outs[x // 2][x % 2] = sent[pos * rows : (pos + 1) * rows]


def back_part(rows_ref, p_ref, slot_ref, mix_ref, unembed_ref, ready):
    width = unembed_ref.shape[1]
    pix = width // LANES
    rows = rows_ref[...].reshape(-1, rows_ref.shape[-1])
    for j in range(0, pix, 2):
        cols = slice(j * LANES, (j + 2) * LANES)
        p_ref[:, cols] = mm(rows, unembed_ref[:, cols])
    wait(ready)

    def group(g, carry):
        at = pl.ds(pl.multiple_of(g * 2 * GROUP, 2 * GROUP), 2 * GROUP)
        got = p_ref[at, :]
        data = jnp.concatenate([lay_tiles(got[:GROUP], pix), lay_tiles(got[GROUP:], pix)], axis=0)
        out = mm(mix_ref[g], data.astype(BF16))
        to = pl.ds(pl.multiple_of(g * GROUP, GROUP), GROUP)
        for i in range(pix):
            slot_ref[to, i * LANES : (i + 1) * LANES] = out[i * GROUP : (i + 1) * GROUP]
        return carry

    lax.fori_loop(0, rows.shape[0] // (2 * GROUP), group, 0, unroll=4)


def fetch_rows(chunks, fetch, rows_ref, sem):
    at = 0
    copies = []
    for i, (ref, (index, count)) in enumerate(zip(chunks, fetch)):
        piece = ref.at[index] if count == 1 else ref
        to = rows_ref.at[at] if count == 1 else rows_ref.at[at : at + count]
        copies.append(pltpu.make_async_copy(piece, to, sem.at[2 + i]))
        at += count
    return copies


def back_kernel(fetch, group0, *refs):
    n = len(fetch)
    chunks = refs[:n]
    unembed_any, mix_any, out_ref, rows_ref, p_ref, slot_ref, mix_ref, unembed_ref, sem = refs[n:]
    groups = mix_ref.shape[0]
    copies = fetch_rows(chunks, fetch, rows_ref, sem)
    copies += to_vmem([(unembed_any, unembed_ref), (mix_any.at[group0 : group0 + groups], mix_ref)], sem)
    start(copies)
    wait(copies[:-1])
    back_part(rows_ref, p_ref, slot_ref, mix_ref, unembed_ref, copies[-1:])
    out_ref[...] = slot_ref[...].astype(BF16)


def last_kernel(
    fetch, group0, *refs,
):
    n = len(fetch)
    chunks, refs = refs[1 : 1 + n], (refs[0], *refs[1 + n :])
    send_ref = refs[0]
    prior = refs[1:3]
    unembed_any, mix_any, out_ref, rows_ref, p_ref, slot_ref, all_ref, mix_ref, unembed_ref, sem = refs[3:]
    groups = mix_ref.shape[0]
    copies = fetch_rows(chunks, fetch, rows_ref, sem)
    copies += to_vmem([(unembed_any, unembed_ref), (mix_any.at[group0 : group0 + groups], mix_ref)], sem)
    at = 0
    more = []
    for i, ref in enumerate(prior):
        more.append(pltpu.make_async_copy(ref, all_ref.at[at : at + ref.shape[0]], sem.at[2 + n + i]))
        at += ref.shape[0]
    start(copies + more)
    wait(copies[:-1])
    back_part(rows_ref, p_ref, slot_ref, mix_ref, unembed_ref, copies[-1:])
    all_ref[at:, :] = slot_ref[...].astype(BF16)
    wait(more)
    pix = unembed_ref.shape[1] // LANES
    pd, total = out_ref.shape
    ch = total // pix
    onehot = (iota((pd, send_ref.shape[1]), 0) == send_ref[...]).astype(F32).astype(BF16)
    tiles = [None] * (-(-total // LANES))
    for j in range(0, pix, 2):
        both = mm(onehot, all_ref[:, j * LANES : (j + 2) * LANES])
        for jj in (j, j + 1):
            val = both[:, (jj - j) * LANES : (jj - j + 1) * LANES]
            t, off = divmod(ch * jj, LANES)
            if off:
                val = pltpu.roll(val, off, 1)
            lane = iota(val.shape, 1)
            low, high = jnp.where(lane >= off, val, 0.0), jnp.where(lane < off, val, 0.0)
            for tt, piece in ((t, low), (t + 1, high)):
                if tt == t + 1 and off + ch <= LANES:
                    continue
                tiles[tt] = piece if tiles[tt] is None else tiles[tt] + piece
    for t, tile in enumerate(tiles):
        hi = min((t + 1) * LANES, total)
        out_ref[:, t * LANES : hi] = tile[:, : hi - t * LANES]


def swap(value, axis):
    return lax.all_to_all(value, axis, split_axis=0, concat_axis=0, tiled=True)


def swap_pairs(value, axis, order):
    count = lax.axis_size(axis)
    rows, width = value.shape
    cap = rows // (2 * count)
    if order is not None:
        me = lax.axis_index(axis)
        place = jnp.array([order.index(x) for x in range(count)], jnp.int32)
        chunks = value.reshape(count, 2 * cap, width)
        chunks = jnp.take(chunks, place[jnp.arange(count) ^ me], axis=0)
        chunks = swap(chunks.reshape(rows, width), axis).reshape(count, 2 * cap, width)
        return jnp.take(chunks, jnp.array(order, jnp.int32) ^ me, axis=0).reshape(rows, width)
    if cap % GROUP == 0:
        return swap(value, axis)
    groups = rows // (2 * GROUP)
    v = value.reshape(groups, 2, GROUP, width).transpose(1, 0, 2, 3).reshape(2, count, cap, width)
    v = swap(v.transpose(1, 0, 2, 3).reshape(rows, width), axis)
    v = v.reshape(count, 2, cap, width).transpose(1, 0, 2, 3).reshape(2, groups, GROUP, width)
    return v.transpose(1, 0, 2, 3).reshape(rows, width)


def flip(value, axis, bits):
    count = lax.axis_size(axis)
    return lax.ppermute(value, axis, [(source, source ^ bits) for source in range(count)])


def from_behind(value, axis, steps):
    count = lax.axis_size(axis)
    pairs = [(source, (source + steps) % count) for source in range(count)]
    return lax.ppermute(value, axis, pairs)


def bias_tables(rel_bias):
    blocks, heads, entries = rel_bias.shape
    span = WIN * WIN
    pos = jnp.arange(span)
    half = WIN // 2
    row = (pos % (span // 2)) // half
    col = (pos // (span // 2)) * half + pos % half
    wide = 2 * WIN - 1
    index = (row[:, None] - row[None] + WIN - 1) * wide + col[:, None] - col[None] + WIN - 1
    onehot = (jnp.arange(entries)[:, None] == index.reshape(1, -1)).astype(BF16)
    rest = rel_bias.reshape(blocks * heads, entries)
    parts = []
    for _ in range(3):
        top = lax.reduce_precision(rest, 8, 7)
        parts.append(top)
        rest = rest - top
    stacked = jnp.concatenate(parts, axis=0).astype(BF16)
    got = jnp.dot(stacked, onehot, preferred_element_type=F32)
    got = got.reshape(3, blocks, heads, span, span)
    got = (got[0] + got[1]) + got[2]
    return got.transpose(0, 2, 1, 3).reshape(blocks, span, heads * span)


PARTS = 4
NEAR = 4


def body(
    bands, send_table, recv_table, regrid_weight, embed_weight, norm1_gain, qkv_weight, rel_bias,
    proj_weight, norm2_gain, up_weight, down_weight, unembed_weight,
):
    pd, width = bands.shape
    slots = send_table.shape[1]
    kk = recv_table.shape[0]
    d = embed_weight.shape[1]
    pixsq = regrid_weight.shape[1] // kk
    pix = int(round(pixsq**0.5))
    half_cols = WIN // 2
    heads = rel_bias.shape[1]
    wide = pix * LANES
    ffh = up_weight.shape[2]
    count = lax.axis_size("tile")
    cap = slots // count
    direct = count == 4 * NEAR and cap % GROUP == 0
    vm = pltpu.VMEM
    dma = lambda n: pltpu.SemaphoreType.DMA((n,))
    per = slots // PARTS
    groups = per // GROUP

    me = lax.axis_index("tile").astype(jnp.int32)
    if direct:
        order = [2 * s + e for h in range(2) for e in range(2) for s in range(h * NEAR, (h + 1) * NEAR)]
        place = [order.index(x) for x in range(count)]
        other = recv_table // cap ^ me
        recv = jnp.zeros_like(recv_table)
        for x in range(count):
            recv = jnp.where(other == x, place[x], recv)
        recv = recv * cap + recv_table % cap
        send = jnp.take(send_table.reshape(count, cap), jnp.array(order, jnp.int32) ^ me, axis=0)
        send = send.reshape(1, slots)
    else:
        order, recv, send = None, recv_table, send_table

    if direct:
        smem = pl.BlockSpec(memory_space=pltpu.SMEM)
        vmem = pl.BlockSpec(memory_space=pltpu.VMEM)
        chips = count // 2
        outgoing = pl.pallas_call(
            pick_kernel,
            out_shape=[sds((2, cap, width), BF16)] * chips,
            in_specs=[smem, vmem, vmem],
            out_specs=[vmem] * chips,
            scratch_shapes=[vm((count, cap, width), BF16)],
            compiler_params=pltpu.CompilerParams(vmem_limit_bytes=VMEM_LIMIT),
            name="pick",
        )(me.reshape(1), bands, send_table)
        came = [None] * chips
        came[0] = outgoing[0]
        for s in [*range(NEAR, chips), *range(NEAR - 1, 0, -1)]:
            came[s] = flip(outgoing[s], "tile", 2 * s)
    else:
        outgoing = call(pick_all_kernel, [sds((slots, width), BF16)], [bands, send_table],
                        flops=2 * slots * pd * width, name="pick")
        incoming = swap(outgoing, "tile").reshape(PARTS, 1, per, width)

    recv = recv.reshape(kk, ROWS, 2, half_cols).transpose(0, 2, 1, 3).reshape(kk, pd)
    weight = regrid_weight.reshape(ROWS, 2, half_cols, kk * pixsq).transpose(1, 0, 2, 3)
    weight = weight.reshape(pd, kk * pixsq)
    bias = bias_tables(rel_bias)
    mix, wsend, select, scatter, embed_pad, unembed_pad = call(
        prep_kernel,
        [sds((slots // GROUP, 2 * pix * GROUP, pix * GROUP), BF16), sds((2 * slots, pixsq), BF16),
         sds((2 * slots, pd), BF16), sds((PARTS, pd, 2 * per), BF16), sds((wide, d), BF16), sds((d, wide), BF16)],
        [recv, recv.T, weight, embed_weight, unembed_weight], [bias], flops=2e9, name="prep")
    wback = swap_pairs(wsend, "tile", order)

    def relay(arrays, shape):
        n = len(arrays)
        return call(relay_kernel, [sds((n, *shape), BF16)], [], arrays, [dma(n)], name="relay")

    def early(arrays, fetch, parts, prior):
        n = len(parts)
        data = (sum(c for _, c in fetch), *arrays[0].shape[1:])
        extra = [] if prior is None else [prior]
        in_specs = [pl.BlockSpec(memory_space=pl.ANY)] * (len(arrays) + 3)
        in_specs += [pl.BlockSpec(memory_space=pltpu.VMEM)] * len(extra)
        return pl.pallas_call(
            functools.partial(early_kernel, pix, fetch, parts),
            out_shape=sds((pd, d), F32),
            in_specs=in_specs,
            out_specs=pl.BlockSpec(memory_space=pltpu.VMEM),
            scratch_shapes=[vm(data, BF16), vm((n * per, wide), F32), vm((2 * n * per, wide), BF16),
                            vm((n * groups, *mix.shape[1:]), BF16), vm((n, pd, 2 * per), BF16),
                            vm((wide, d), BF16), dma(3 + len(arrays))],
            compiler_params=pltpu.CompilerParams(vmem_limit_bytes=VMEM_LIMIT),
            cost_estimate=pl.CostEstimate(flops=int(1e9 * n), bytes_accessed=int(3e6), transcendentals=0),
            name="early",
        )(*arrays, mix, scatter, embed_pad, *extra)

    if direct:
        near_pass = flip(relay(came[:NEAR], (cap, width)), "tile", 1)
        far_pass = flip(relay(came[NEAR:], (cap, width)), "tile", 1)
        total = early([*came[:NEAR], near_pass], [(0, 1)] * NEAR + [(None, NEAR)], (0, 1), None)
        total = early(came[NEAR:], [(0, 1)] * NEAR, (2,), total)
        last_data = far_pass
    else:
        total = early([incoming[0], incoming[1]], [(0, 1)] * 2, (0, 1), None)
        total = early([incoming[2]], [(0, 1)], (2,), total)
        last_data = incoming[3]

    half = pd // 2
    layer_scratch = [vm(bias.shape[1:], F32), vm((d, 3 * d), BF16), vm((d, d), BF16), vm((d, ffh), BF16),
                     vm((ffh, d), BF16)]
    low, high = call(
        functools.partial(first_kernel, pix, PARTS - 1, 0),
        [sds((half, d), BF16)] * 2,
        [total, norm1_gain, norm2_gain],
        [last_data, mix, scatter, embed_pad, bias, qkv_weight, proj_weight, up_weight, down_weight],
        [vm(last_data.shape, BF16), vm((per, wide), F32), vm((2 * per, wide), BF16),
         vm((groups, *mix.shape[1:]), BF16), vm((pd, 2 * per), BF16), vm((wide, d), BF16), *layer_scratch, dma(9)],
        flops=4e9, name="first")
    right = from_behind(low, "tile", -1)
    left = from_behind(high, "tile", 1)
    mix_back = call(prep_back_kernel, [sds((slots // GROUP, pix * GROUP, 2 * pix * GROUP), BF16)], [wback],
                    flops=2e9, name="prep_back")
    rows = 2 * cap
    sent = call(
        functools.partial(second_kernel, 1, order),
        [sds((2, rows, d), BF16)] * (count // 2) if direct else [sds((2 * slots, d), BF16)],
        [low, high, left, right, norm1_gain, norm2_gain],
        [select, bias, qkv_weight, proj_weight, up_weight, down_weight],
        [vm((2 * slots, pd), BF16), *layer_scratch, dma(6)],
        flops=2e9, name="second")

    def back_scratch(data, n):
        return [vm(data, BF16), vm((2 * n * per, wide), F32), vm((n * per, wide), F32)]

    def back(arrays, fetch, part, n):
        data = (sum(c for _, c in fetch), *arrays[0].shape[1:])
        return call(
            functools.partial(back_kernel, fetch, part * groups),
            [sds((n * per, wide), BF16)], [], [*arrays, unembed_pad, mix_back],
            [*back_scratch(data, n), vm((n * groups, *mix_back.shape[1:]), BF16), vm((d, wide), BF16),
             dma(2 + len(arrays))],
            flops=1e9 * n, name="back")

    if direct:
        got = [sent[0]] + [None] * (count // 2 - 1)
        for s in [*range(NEAR, count // 2), *range(NEAR - 1, 0, -1)]:
            got[s] = flip(sent[s], "tile", 2 * s)
        near_pass = flip(relay(got[:NEAR], (rows, d)), "tile", 1)
        far_pass = flip(relay(got[NEAR:], (rows, d)), "tile", 1)
        slots_a = back([*got[:NEAR], near_pass], [(0, 1)] * NEAR + [(None, NEAR)], 0, 2)
        slots_b = back(got[NEAR:], [(0, 1)] * NEAR, 2, 1)
        last_data, fetch = far_pass, [(None, NEAR)]
    else:
        got = swap_pairs(sent, "tile", order).reshape(PARTS, 1, 2 * per, d)
        slots_a = back([got[0], got[1]], [(0, 1)] * 2, 0, 2)
        slots_b = back([got[2]], [(0, 1)], 2, 1)
        last_data, fetch = got[3], [(0, 1)]
    return call(
        functools.partial(last_kernel, fetch, 3 * groups),
        [sds((pd, width), F32)],
        [send],
        [last_data, slots_a, slots_b, unembed_pad, mix_back],
        [*back_scratch(last_data.shape, 1), vm((slots, wide), BF16), vm((groups, *mix_back.shape[1:]), BF16),
         vm((d, wide), BF16), dma(5)],
        flops=3e9, name="last")


def solution(mesh):
    in_specs = (
        P(("groups", "tile"), None), P("tile", None), P(None, "tile"), P("tile", None),
        P(), P(), P(), P(), P(), P(), P(), P(), P(),
    )
    out_specs = P(("groups", "tile"), None)
    return jax.shard_map(body, mesh=mesh, in_specs=in_specs, out_specs=out_specs, check_vma=False)
```

```python
import functools

import jax
import jax.numpy as jnp
import numpy as np
from jax import lax
from jax.experimental import pallas as pl
from jax.experimental.pallas import tpu as pltpu
from jax.sharding import PartitionSpec as P

WIN = 8
ROWS = 24
K = 4
LANES = 128
GROUP = 8

norm_eps = 1e-05
F32 = jnp.float32
BF16 = jnp.bfloat16


def iota(shape, axis):
    return lax.broadcasted_iota(jnp.int32, shape, axis)


def mm(a, b):
    return jnp.dot(a, b, preferred_element_type=F32)


def mm_tn(a, b):
    return lax.dot_general(a, b, (((0,), (0,)), ((), ())), preferred_element_type=F32)


def mm_nt(a, b):
    return lax.dot_general(a, b, (((1,), (1,)), ((), ())), preferred_element_type=F32)


VMEM_LIMIT = 67043328


class In:
    def __init__(self, array, shape=None, copies=None, fixed=True):
        self.array = array
        self.shape = tuple(array.shape if shape is None else shape)
        self.copies = copies or (lambda ref, to, me: [(ref, to)])
        self.fixed = fixed


def at(array, index, fixed=True):
    return In(array, array.shape[1:], lambda ref, to, me: [(ref.at[index], to)], fixed)


class Loaded:
    def __init__(self, copies, ref):
        self.copies, self.ref, self.ready = copies, ref, False

    def __call__(self):
        if not self.ready:
            for c in self.copies:
                c.wait()
            self.ready = True
        return self.ref


def call(name, kernel, ins, outs, scratch=(), me=None, flops=0):
    most = 24

    def run(*refs):
        refs = list(refs)
        my = refs.pop(0)[0] if me is not None else None
        srcs = [refs.pop(0) for _ in ins]
        dsts = [refs.pop(0) for _ in outs]
        bufs = [refs.pop(0) for _ in ins]
        held = [refs.pop(0) for _ in outs]
        in_sem, out_sem = refs.pop(0), refs.pop(0)
        loads = []
        for i, (one, s, b) in enumerate(zip(ins, srcs, bufs)):
            copies = [
                pltpu.make_async_copy(x, y, in_sem.at[i, k]) for k, (x, y) in enumerate(one.copies(s, b, my))
            ]
            for c in copies:
                c.start()
            loads.append(Loaded(copies, b))
        stores = {}

        def put(i):
            stores[i] = pltpu.make_async_copy(held[i], dsts[i], out_sem.at[i])
            stores[i].start()

        kernel(loads, held, put, refs)
        for one in loads:
            one()
        for i in range(len(outs)):
            if i not in stores:
                put(i)
        for c in stores.values():
            c.wait()

    in_specs = [] if me is None else [pl.BlockSpec(memory_space=pltpu.SMEM)]
    in_specs += [pl.BlockSpec(memory_space=pltpu.HBM if one.fixed else pl.ANY) for one in ins]
    moved = sum(int(np.prod(s.shape)) * s.array.dtype.itemsize for s in ins)
    got = pl.pallas_call(
        run,
        out_shape=list(outs),
        in_specs=in_specs,
        out_specs=[pl.BlockSpec(memory_space=pltpu.HBM)] * len(outs),
        scratch_shapes=[
            *[pltpu.VMEM(one.shape, one.array.dtype) for one in ins],
            *[pltpu.VMEM(o.shape, o.dtype) for o in outs],
            pltpu.SemaphoreType.DMA((len(ins), most)),
            pltpu.SemaphoreType.DMA((len(outs),)),
            *scratch,
        ],
        compiler_params=pltpu.CompilerParams(vmem_limit_bytes=VMEM_LIMIT),
        cost_estimate=pl.CostEstimate(flops=int(flops), bytes_accessed=moved, transcendentals=0),
        name=name,
    )(*([] if me is None else [me]), *[one.array for one in ins])
    return got if len(outs) > 1 else got[0]


def sds(shape, dtype):
    return jax.ShapeDtypeStruct(shape, dtype)


def chosen_rows(bands_ref, send_ref):
    rows, slots = bands_ref.shape[0], send_ref.shape[1]
    onehot = (iota((rows, slots), 0) == send_ref[...]).astype(F32).astype(BF16)
    return mm_tn(onehot, bands_ref[...])


def pick_kernel(loads, outs, put, scratch):
    send, bands = loads
    outs[0][...] = chosen_rows(bands(), send()).astype(BF16)


def relay_kernel(loads, outs, put, scratch):
    for i, one in enumerate(loads):
        outs[0][i] = one()[...]


def spread(weights, fixed_first, pix):
    width = pix * GROUP
    shape = (pix * pix, pix * width)
    r, c = iota(shape, 0), iota(shape, 1)
    outer, inner = c // width, (c % width) // GROUP
    if fixed_first:
        sel = (r // pix == outer) & (r % pix == inner)
    else:
        sel = (r % pix == outer) & (r // pix == inner)
    out = mm(weights, sel.astype(F32).astype(BF16))
    own = iota(out.shape, 0) % GROUP == iota(out.shape, 1) % GROUP
    return jnp.where(own, out, 0.0)


def store_spread(out_ref, value, row0, col0, pix):
    groups = value.shape[0] // GROUP
    width = pix * GROUP
    for o in range(0, pix, 2):
        lo = value[:, o * width : (o + 1) * width].reshape(groups, GROUP, width)
        hi = value[:, (o + 1) * width : (o + 2) * width].reshape(groups, GROUP, width)
        both = jnp.concatenate([lo, hi], axis=1).astype(BF16)
        out_ref[:, row0 + o * GROUP : row0 + (o + 2) * GROUP, col0 : col0 + width] = both


def tile_move(ch, j, total):
    lo = (ch * j // LANES) * LANES
    hi = min(lo + 2 * LANES, total)
    shape = (hi - lo, LANES)
    move = (iota(shape, 0) - (ch * j - lo) == iota(shape, 1)) & (iota(shape, 1) < ch)
    return lo, hi, move.astype(F32).astype(BF16)


def weights_by_slot(recv, weight, slots, level):
    pixsq = weight.shape[1] // recv.shape[0]
    r = iota((slots, recv.shape[1]), 0)
    total = None
    for k in (2 * level, 2 * level + 1):
        hit = (recv[k : k + 1, :] == r).astype(F32).astype(BF16)
        term = mm(hit, weight[:, k * pixsq : (k + 1) * pixsq])
        total = term if total is None else total + term
    return total


def prep_kernel(loads, outs, put, scratch):
    recv, weight, recv_pos, recv_ord, recv_col, embed, unembed, bias = loads
    wsend_ref, mix_ref, select_ref, scatter_ref, embed_out, unembed_out = outs
    kk, pd = recv_pos.ref.shape
    slots = 2 * pd
    pixsq = weight.ref.shape[1] // kk
    pix = int(round(pixsq**0.5))
    ch = embed.ref.shape[0] // pix
    totals = [weights_by_slot(recv(), weight(), slots, v).reshape(slots // GROUP, GROUP, pixsq) for v in range(2)]
    wsend_ref[...] = jnp.concatenate(totals, axis=1).reshape(2 * slots, pixsq).astype(BF16)
    put(0)
    for level in range(2):
        total = weights_by_slot(recv_pos(), weight(), slots, level)
        store_spread(mix_ref, spread(total.astype(BF16), True, pix), level * pix * GROUP, 0, pix)
    put(1)

    def chosen(shape, axis, row0, vals):
        r = iota(shape, axis) + row0
        slot = (r // (2 * GROUP)) * GROUP + r % GROUP
        level = (r // GROUP) % 2
        first = (vals(0) == slot) | (vals(1) == slot)
        second = (vals(2) == slot) | (vals(3) == slot)
        hit = (first & (level == 0)) | (second & (level == 1))
        return hit.astype(F32).astype(BF16)

    rows, cols = recv_ord(), recv_col()
    select_ref[...] = chosen((2 * slots, pd), 0, 0, lambda k: rows[k : k + 1, :])
    put(2)
    parts, _, width = scatter_ref.shape
    for part in range(parts):
        scatter_ref[part] = chosen((pd, width), 1, part * width, lambda k: cols[:, k : k + 1])
    put(3)
    for i in range(pix):
        lo, hi, move = tile_move(ch, i, embed.ref.shape[0])
        tile = slice(i * LANES, (i + 1) * LANES)
        embed_out[tile, :] = mm_tn(move, embed()[lo:hi, :]).astype(BF16)
        unembed_out[tile, :] = mm_tn(move, unembed()[lo:hi, :]).astype(BF16)


def prep_back_kernel(loads, outs, put, scratch):
    weight_ref, mix_ref = loads[0](), outs[0]
    rows, pixsq = weight_ref.shape
    pix = int(round(pixsq**0.5))
    groups = rows // (2 * GROUP)
    w3 = weight_ref[...].astype(F32).reshape(groups, 2, GROUP, pixsq)
    for level in range(2):
        w_l = w3[:, level].reshape(groups * GROUP, pixsq).astype(BF16)
        store_spread(mix_ref, spread(w_l, False, pix), 0, level * pix * GROUP, pix)


def layer_norm(values, gain):
    average = jnp.mean(values, axis=-1, keepdims=True)
    centred = values - average
    spread_ = jnp.mean(centred * centred, axis=-1, keepdims=True)
    return centred * lax.rsqrt(spread_ + norm_eps) * gain


def head_mask(heads, span, d):
    head_of = iota((heads * span, d), 0) // span == iota((heads * span, d), 1) // (d // heads)
    return head_of.astype(F32).astype(BF16)


def softmax_parts(scores, side):
    out = []
    for m in range(scores.shape[1] // LANES):
        part = scores[:, m * LANES : (m + 1) * LANES]
        low = iota(part.shape, 1) % LANES < side
        top_lo = jnp.max(jnp.where(low, part, -3e38), axis=-1, keepdims=True)
        top_hi = jnp.max(jnp.where(low, -3e38, part), axis=-1, keepdims=True)
        out.append(jnp.exp(part - jnp.where(low, top_lo, top_hi)))
    return jnp.concatenate(out, axis=1)


def attend_rows(query, key, value, bias, heads, mask, blocked):
    d = query.shape[1]
    key_all = jnp.concatenate([key] * heads, axis=0) * mask
    value_all = jnp.concatenate([value] * heads, axis=0) * mask
    scores = mm_nt(query, key_all) * (d // heads) ** (-0.5) + bias
    if blocked is not None:
        scores = jnp.where(blocked, -1e30, scores)
    weights = softmax_parts(scores, key.shape[0]).astype(BF16)
    return mm(weights, value_all), weights


def feed_forward(residual, gain2, up, down):
    normed = layer_norm(residual, gain2).astype(BF16)
    hidden = jax.nn.gelu(mm(normed, up)).astype(BF16)
    return (residual + mm(hidden, down)).astype(BF16)


def lay_tiles(rows, count):
    return jnp.concatenate([rows[:, t * LANES : (t + 1) * LANES] for t in range(count)], axis=0)


def joined(chunks):
    pieces = [one()[...].astype(F32).reshape(-1, one.ref.shape[-1]) for one in chunks]
    return jnp.concatenate(pieces, axis=0).astype(BF16)


def regrid_part(data, x_ref, c_ref, mix, scatter, embed, pix):
    slots, width = data.shape
    ch = width // pix
    for j in range(pix):
        lo, hi, move = tile_move(ch, j, width)
        x_ref[:, j * LANES : (j + 1) * LANES] = mm(data[:, lo:hi], move)
    mix_ref = mix()

    def group(g, carry):
        tiles = lay_tiles(x_ref[pl.ds(pl.multiple_of(g * GROUP, GROUP), GROUP), :], pix).astype(BF16)
        out = mm(mix_ref[g], tiles)
        to = pl.ds(pl.multiple_of(g * 2 * GROUP, 2 * GROUP), 2 * GROUP)
        for i in range(pix):
            low = out[i * GROUP : (i + 1) * GROUP]
            high = out[(pix + i) * GROUP : (pix + i + 1) * GROUP]
            both = jnp.concatenate([low, high], axis=0).astype(BF16)
            c_ref[to, i * LANES : (i + 1) * LANES] = both
        return carry

    lax.fori_loop(0, slots // GROUP, group, 0, unroll=4)
    scatter_ref, embed_ref = scatter(), embed()
    total = None
    for j in range(0, pix, 2):
        cols = slice(j * LANES, (j + 2) * LANES)
        pixels = mm(scatter_ref[...], c_ref[:, cols])
        term = mm(pixels.astype(BF16), embed_ref[cols, :])
        total = term if total is None else total + term
    return total


def early_kernel(pix, loads, outs, put, scratch):
    *chunks, mix, scatter, embed = loads
    outs[0][...] = regrid_part(joined(chunks), *scratch, mix, scatter, embed, pix)


def first_kernel(pix, layer, loads, outs, put, scratch):
    *chunks, mix, scatter, embed, prior, gain1, gain2, qkv, bias, proj, up, down = loads
    total = regrid_part(joined(chunks), *scratch, mix, scatter, embed, pix)
    state = (prior()[...] + total).astype(BF16).astype(F32)
    pd, d = state.shape
    heads = bias.ref.shape[1] // (WIN * WIN)
    normed = layer_norm(state, gain1()[layer : layer + 1, :]).astype(BF16)
    packed = mm(normed, qkv()[...]).astype(BF16)
    query, key, value = packed[:, :d], packed[:, d : 2 * d], packed[:, 2 * d :]
    half = pd // 2
    win_rows = ROWS // WIN
    part_rows = half // win_rows
    bias_all = bias()[...]
    mask = head_mask(heads, WIN * WIN, d)
    mixed = [None] * (2 * win_rows)
    weights = [None] * (2 * win_rows)
    for w in range(win_rows):
        def rows(v):
            lo, hi = w * part_rows, (w + 1) * part_rows
            return jnp.concatenate([v[lo:hi], v[half + lo : half + hi]], axis=0)
        out, wts = attend_rows(rows(query), rows(key), rows(value), bias_all, heads, mask, None)
        mixed[w], mixed[win_rows + w] = out[:part_rows], out[part_rows:]
        weights[w], weights[win_rows + w] = wts[:part_rows], wts[part_rows:]
    total = mm(jnp.concatenate(weights, axis=0), mask)
    mixed = (jnp.concatenate(mixed, axis=0) / total).astype(BF16)
    attended = mm(mixed, proj()[...]).astype(BF16)
    residual = state + attended.astype(F32)
    new = feed_forward(residual, gain2()[layer : layer + 1, :], up()[...], down()[...])
    outs[0][...] = new[:half]
    outs[1][...] = new[half:]


def second_kernel(layer, order, loads, outs, put, scratch):
    low, high, gain1, gain2, qkv, bias, left, right, proj, up, down, select = loads
    half, d = low.ref.shape
    heads = bias.ref.shape[1] // (WIN * WIN)
    shift = half * (WIN // 2) // ROWS
    turn = lambda v: jnp.concatenate([v[shift:], v[:shift]], axis=0)
    back = lambda v: jnp.concatenate([v[half - shift :], v[: half - shift]], axis=0)
    own = jnp.concatenate([turn(low()[...]), turn(high()[...])], axis=0).astype(F32)
    gain = gain1()[layer : layer + 1, :]
    normed = layer_norm(own, gain).astype(BF16)
    strips = jnp.concatenate([turn(left()[...]), turn(right()[...])], axis=0).astype(F32)
    normed_s = layer_norm(strips, gain).astype(BF16)
    packed = mm(normed, qkv()[...]).astype(BF16)
    packed_s = mm(normed_s, qkv()[:, d:]).astype(BF16)
    query, key, value = packed[:, :d], packed[:, d : 2 * d], packed[:, 2 * d :]
    key_s, value_s = packed_s[:, :d], packed_s[:, d:]
    win_rows = ROWS // WIN
    part = half // win_rows
    span = WIN * WIN
    bias_all = bias()[...]
    mask = head_mask(heads, span, d)
    outs_m, outs_w = [[], []], [[], []]
    for w in range(win_rows):
        near = slice(w * part, (w + 1) * part)
        far = slice(half + w * part, half + (w + 1) * part)
        for side in range(2):
            if side == 0:
                q = query[near]
                k = jnp.concatenate([key_s[near], key[near]], axis=0)
                v = jnp.concatenate([value_s[near], value[near]], axis=0)
                b = bias_all[part:]
            else:
                q = query[far]
                k = jnp.concatenate([key[far], key_s[far]], axis=0)
                v = jnp.concatenate([value[far], value_s[far]], axis=0)
                b = bias_all[:part]
            blocked = None
            if w == win_rows - 1:
                shape = (part, heads * span)
                q_up = iota(shape, 0) % part >= part // 2
                k_up = iota(shape, 1) % part >= part // 2
                blocked = q_up != k_up
            out, wts = attend_rows(q, k, v, b, heads, mask, blocked)
            outs_m[side].append(out)
            outs_w[side].append(wts)
    total = mm(jnp.concatenate(outs_w[0] + outs_w[1], axis=0), mask)
    mixed = (jnp.concatenate(outs_m[0] + outs_m[1], axis=0) / total).astype(BF16)
    attended = mm(mixed, proj()[...]).astype(BF16)
    residual = own + attended.astype(F32)
    new = feed_forward(residual, gain2()[layer : layer + 1, :], up()[...], down()[...])
    state = jnp.concatenate([back(new[:half]), back(new[half:])], axis=0)
    sent = mm(select()[...], state).astype(BF16)
    if order is None:
        outs[0][...] = sent
        return
    rows = sent.shape[0] // len(order)
    for pos, x in enumerate(order):
        outs[x // 2][x % 2] = sent[pos * rows : (pos + 1) * rows]


def back_part(chunks, mix, unembed, p_ref, slot_ref):
    rows = jnp.concatenate([one()[...].reshape(-1, one.ref.shape[-1]) for one in chunks], axis=0)
    unembed_ref = unembed()
    pix = unembed_ref.shape[0] // LANES
    for j in range(0, pix, 2):
        cols = slice(j * LANES, (j + 2) * LANES)
        p_ref[:, cols] = mm_nt(rows, unembed_ref[cols, :])
    mix_ref = mix()

    def group(g, carry):
        got = p_ref[pl.ds(pl.multiple_of(g * 2 * GROUP, 2 * GROUP), 2 * GROUP), :]
        data = jnp.concatenate([lay_tiles(got[:GROUP], pix), lay_tiles(got[GROUP:], pix)], axis=0)
        out = mm(mix_ref[g], data.astype(BF16))
        to = pl.ds(pl.multiple_of(g * GROUP, GROUP), GROUP)
        for i in range(pix):
            slot_ref[to, i * LANES : (i + 1) * LANES] = out[i * GROUP : (i + 1) * GROUP]
        return carry

    lax.fori_loop(0, rows.shape[0] // (2 * GROUP), group, 0, unroll=4)


def back_kernel(loads, outs, put, scratch):
    *chunks, unembed, mix = loads
    back_part(chunks, mix, unembed, *scratch)
    outs[0][...] = scratch[1][...].astype(BF16)


def last_kernel(loads, outs, put, scratch):
    *chunks, unembed, mix, prior, send = loads
    back_part(chunks, mix, unembed, *scratch)
    slot_ref, out_ref = scratch[1], outs[0]
    pix = unembed.ref.shape[0] // LANES
    pd, total = out_ref.shape
    ch = total // pix
    cut = prior.ref.shape[0]
    send_ref, prior_ref = send(), prior()
    onehot = (iota((pd, send_ref.shape[1]), 0) == send_ref[...]).astype(F32).astype(BF16)
    tiles = [None] * (-(-total // LANES))
    for j in range(0, pix, 2):
        cols = slice(j * LANES, (j + 2) * LANES)
        slots = jnp.concatenate([prior_ref[:, cols], slot_ref[:, cols].astype(BF16)], axis=0)
        both = mm(onehot, slots)
        for jj in (j, j + 1):
            val = both[:, (jj - j) * LANES : (jj - j + 1) * LANES]
            t, off = divmod(ch * jj, LANES)
            if off:
                val = pltpu.roll(val, off, 1)
            lane = iota(val.shape, 1)
            low, high = jnp.where(lane >= off, val, 0.0), jnp.where(lane < off, val, 0.0)
            for tt, piece in ((t, low), (t + 1, high)):
                if tt == t + 1 and off + ch <= LANES:
                    continue
                tiles[tt] = piece if tiles[tt] is None else tiles[tt] + piece
    for t, tile in enumerate(tiles):
        hi = min((t + 1) * LANES, total)
        out_ref[:, t * LANES : hi] = tile[:, : hi - t * LANES]


def swap(value, axis):
    return lax.all_to_all(value, axis, split_axis=0, concat_axis=0, tiled=True)


def swap_pairs(value, axis):
    count = lax.axis_size(axis)
    rows, width = value.shape
    cap = rows // (2 * count)
    if cap % GROUP == 0:
        return swap(value, axis)
    groups = rows // (2 * GROUP)
    v = value.reshape(groups, 2, GROUP, width).transpose(1, 0, 2, 3).reshape(2, count, cap, width)
    v = swap(v.transpose(1, 0, 2, 3).reshape(rows, width), axis)
    v = v.reshape(count, 2, cap, width).transpose(1, 0, 2, 3).reshape(2, groups, GROUP, width)
    return v.transpose(1, 0, 2, 3).reshape(rows, width)


def flip(value, axis, bits):
    count = lax.axis_size(axis)
    return lax.ppermute(value, axis, [(source, source ^ bits) for source in range(count)])


def from_behind(value, axis, steps):
    count = lax.axis_size(axis)
    pairs = [(source, (source + steps) % count) for source in range(count)]
    return lax.ppermute(value, axis, pairs)


def bias_tables(rel_bias):
    blocks, heads, entries = rel_bias.shape
    span = WIN * WIN
    pos = jnp.arange(span)
    half = WIN // 2
    row = (pos % (span // 2)) // half
    col = (pos // (span // 2)) * half + pos % half
    wide = 2 * WIN - 1
    index = (row[:, None] - row[None] + WIN - 1) * wide + col[:, None] - col[None] + WIN - 1
    onehot = (jnp.arange(entries)[:, None] == index.reshape(1, -1)).astype(BF16)
    rest = rel_bias.reshape(blocks * heads, entries)
    parts = []
    for _ in range(3):
        top = lax.reduce_precision(rest, 8, 7)
        parts.append(top)
        rest = rest - top
    stacked = jnp.concatenate(parts, axis=0).astype(BF16)
    got = jnp.dot(stacked, onehot, preferred_element_type=F32)
    got = got.reshape(3, blocks, heads, span, span)
    got = (got[0] + got[1]) + got[2]
    return got.transpose(0, 2, 1, 3).reshape(blocks, span, heads * span)


STAGES = 2
NEAR = 4


def body(
    bands, send_table, recv_table, regrid_weight, embed_weight, norm1_gain, qkv_weight, rel_bias,
    proj_weight, norm2_gain, up_weight, down_weight, unembed_weight,
):
    pd, width = bands.shape
    slots = send_table.shape[1]
    kk = recv_table.shape[0]
    d = embed_weight.shape[1]
    pixsq = regrid_weight.shape[1] // kk
    pix = int(round(pixsq**0.5))
    half_cols = WIN // 2
    wide = pix * LANES
    count = lax.axis_size("tile")
    cap = slots // count
    chips = count // 2
    direct = chips == 2 * NEAR and cap % GROUP == 0
    vm = pltpu.VMEM
    per = slots // STAGES
    groups = per // GROUP
    me = lax.axis_index("tile").astype(jnp.int32)

    if direct:
        order = [2 * s + e for h in range(2) for e in range(2) for s in range(h * NEAR, (h + 1) * NEAR)]
        place = [order.index(x) for x in range(count)]
        turns = [*range(NEAR, chips), *range(NEAR - 1, 0, -1)]

        def pick_direct(my_ref, bands_ref, send_ref, *refs):
            outs, held, tabs, rows, sem = refs[:chips], refs[chips], refs[-3], refs[-2], refs[-1]
            my = my_ref[0]
            loads = [pltpu.make_async_copy(send_ref, tabs, sem.at[0]), pltpu.make_async_copy(bands_ref, rows, sem.at[1])]
            for c in loads:
                c.start()
            for c in loads:
                c.wait()
            got = chosen_rows(rows, tabs)
            held[...] = got.reshape(count, cap, width).astype(BF16)
            stores = []
            for n, s in enumerate([*turns, 0]):
                for e in range(2):
                    c = pltpu.make_async_copy(held.at[my ^ (2 * s + e)], outs[s].at[e], sem.at[2 + 2 * n + e])
                    c.start()
                    stores.append(c)
            for c in stores:
                c.wait()

        hbm = pl.BlockSpec(memory_space=pltpu.HBM)
        outgoing = pl.pallas_call(
            pick_direct,
            out_shape=[sds((2, cap, width), BF16)] * chips,
            in_specs=[pl.BlockSpec(memory_space=pltpu.SMEM), hbm, hbm],
            out_specs=[hbm] * chips,
            scratch_shapes=[vm((count, cap, width), BF16), vm((1, slots), jnp.int32), vm((pd, width), BF16),
                            pltpu.SemaphoreType.DMA((2 + count,))],
            compiler_params=pltpu.CompilerParams(vmem_limit_bytes=VMEM_LIMIT),
            name="pick",
        )(me.reshape(1), bands, send_table)
        came = [outgoing[0]] + [None] * (chips - 1)
        for s in turns:
            came[s] = flip(outgoing[s], "tile", 2 * s)
        other = recv_table // cap ^ me
        recv_pos = jnp.zeros_like(recv_table)
        for x in range(count):
            recv_pos = jnp.where(other == x, place[x], recv_pos)
        recv_pos = recv_pos * cap + recv_table % cap
        send = jnp.take(send_table.reshape(count, cap), jnp.array(order, jnp.int32) ^ me, axis=0)
        send = send.reshape(1, slots)
    else:
        order, recv_pos, send = None, recv_table, send_table
        outgoing = call("pick", pick_kernel, [In(send_table), In(bands)], [sds((slots, width), BF16)])
        incoming = swap(outgoing, "tile").reshape(STAGES, per, width)

    recv_ord = recv_pos.reshape(kk, ROWS, 2, half_cols).transpose(0, 2, 1, 3).reshape(kk, pd)
    bias = bias_tables(rel_bias)
    wsend, mix, select, scatter, embed_pad, unembed_pad = call(
        "prep", prep_kernel,
        [In(recv_table), In(regrid_weight), In(recv_pos), In(recv_ord), In(recv_ord.T), In(embed_weight),
         In(unembed_weight.T), In(bias, (1, *bias.shape[1:]), lambda ref, to, me: [(ref.at[0:1], to)])],
        [sds((2 * slots, pixsq), BF16), sds((slots // GROUP, 2 * pix * GROUP, pix * GROUP), BF16),
         sds((2 * slots, pd), BF16), sds((STAGES, pd, 2 * per), BF16), sds((wide, d), BF16), sds((wide, d), BF16)],
        flops=4e9)
    wback = swap_pairs(wsend, "tile")

    def relay(arrays):
        shape = (len(arrays), *arrays[0].shape[1:])
        return call("relay", relay_kernel, [at(x, 1, False) for x in arrays], [sds(shape, BF16)])

    def mix_rows(stage):
        return In(mix, (groups, *mix.shape[1:]),
                  lambda ref, to, me: [(ref.at[stage * groups : (stage + 1) * groups], to)])

    if direct:
        near_pass = flip(relay(came[:NEAR]), "tile", 1)
        near = [at(x, 0, False) for x in came[:NEAR]] + [In(near_pass, fixed=False)]
        far_pass = flip(relay(came[NEAR:]), "tile", 1)
        far = [at(x, 0, False) for x in came[NEAR:]] + [In(far_pass, fixed=False)]
    else:
        near, far = [at(incoming, 0)], [at(incoming, 1)]
    regrid_scratch = [vm((per, wide), F32), vm((2 * per, wide), BF16)]
    total = call("early", functools.partial(early_kernel, pix),
                 [*near, mix_rows(0), at(scatter, 0), In(embed_pad)], [sds((pd, d), F32)], regrid_scratch, flops=2e9)

    def layer(n):
        return [In(norm1_gain), In(norm2_gain), at(qkv_weight, n), at(bias, n)], [
            at(proj_weight, n), at(up_weight, n), at(down_weight, n)]

    half = pd // 2
    ins_a, ins_b = layer(0)
    low, high = call(
        "first", functools.partial(first_kernel, pix, 0),
        [*far, mix_rows(1), at(scatter, 1), In(embed_pad), In(total), *ins_a, *ins_b],
        [sds((half, d), BF16)] * 2, regrid_scratch, flops=4e9)
    right = from_behind(low, "tile", -1)
    left = from_behind(high, "tile", 1)
    mix_back = call("prep_back", prep_back_kernel, [In(wback, fixed=False)],
                    [sds((slots // GROUP, pix * GROUP, 2 * pix * GROUP), BF16)], flops=2e9)
    ins_a, ins_b = layer(1)
    rows = 2 * cap
    sent = call(
        "second", functools.partial(second_kernel, 1, order),
        [In(low), In(high), *ins_a, In(left, fixed=False), In(right, fixed=False), *ins_b, In(select)],
        [sds((2, rows, d), BF16)] * chips if direct else [sds((2 * slots, d), BF16)], flops=2e9)

    def back_rows(stage):
        shape = (groups, *mix_back.shape[1:])
        if not direct:
            return In(mix_back, shape, lambda ref, to, me: [(ref.at[stage * groups : (stage + 1) * groups], to)])
        size = cap // GROUP
        near_by = order[stage * 2 * NEAR : (stage + 1) * 2 * NEAR]
        return In(mix_back, shape, lambda ref, to, me: [
            (ref.at[pl.ds((me ^ x) * size, size)], to.at[i * size : (i + 1) * size]) for i, x in enumerate(near_by)])

    back_scratch = [vm((2 * per, wide), F32), vm((per, wide), F32)]
    if direct:
        got = [sent[0]] + [None] * (chips - 1)
        for s in turns:
            got[s] = flip(sent[s], "tile", 2 * s)
        near_pass = flip(relay(got[:NEAR]), "tile", 1)
        near = [at(x, 0, False) for x in got[:NEAR]] + [In(near_pass, fixed=False)]
        far_pass = flip(relay(got[NEAR:]), "tile", 1)
        far = [at(x, 0, False) for x in got[NEAR:]] + [In(far_pass, fixed=False)]
    else:
        got = swap_pairs(sent, "tile").reshape(STAGES, 2 * per, d)
        near, far = [at(got, 0)], [at(got, 1)]
    my = me.reshape(1) if direct else None
    prior = call("back", back_kernel, [*near, In(unembed_pad), back_rows(0)], [sds((per, wide), BF16)],
                 back_scratch, my, flops=2e9)
    return call("last", last_kernel, [*far, In(unembed_pad), back_rows(1), In(prior), In(send)],
                [sds((pd, width), F32)], back_scratch, my, flops=3e9)


def solution(mesh):
    in_specs = (
        P(("groups", "tile"), None), P("tile", None), P(None, "tile"), P("tile", None),
        P(), P(), P(), P(), P(), P(), P(), P(), P(),
    )
    out_specs = P(("groups", "tile"), None)
    return jax.shard_map(body, mesh=mesh, in_specs=in_specs, out_specs=out_specs, check_vma=False)
```

```python
import functools

import jax
import jax.numpy as jnp
import numpy as np
from jax import lax
from jax.experimental import pallas as pl
from jax.experimental.pallas import tpu as pltpu
from jax.sharding import PartitionSpec as P

WIN = 8
ROWS = 24
K = 4
LANES = 128
GROUP = 8

norm_eps = 1e-05
F32 = jnp.float32
BF16 = jnp.bfloat16


def iota(shape, axis):
    return lax.broadcasted_iota(jnp.int32, shape, axis)


def mm(a, b):
    return jnp.dot(a, b, preferred_element_type=F32)


def mm_tn(a, b):
    return lax.dot_general(a, b, (((0,), (0,)), ((), ())), preferred_element_type=F32)


def mm_nt(a, b):
    return lax.dot_general(a, b, (((1,), (1,)), ((), ())), preferred_element_type=F32)


VMEM_LIMIT = 16 << 20


class In:
    def __init__(self, array, index=None):
        self.array = array
        self.index = index


def at(array, index):
    return In(array, index)


class Loaded:
    def __init__(self, ref):
        self.ref = ref

    def __call__(self):
        return self.ref


def call(name, kernel, ins, outs, scratch=(), table=None, flops=0, after=()):
    def run(*refs):
        refs = list(refs)
        lead = [refs.pop(0)] if table is not None else []
        loads = []
        for one in ins:
            ref = refs.pop(0)
            loads.append(Loaded(ref if one.index is None else ref.at[one.index]))
        del refs[: len(after)]
        held = [refs.pop(0) for _ in outs]
        kernel(*lead, loads, held, refs)

    vmem = pl.BlockSpec(memory_space=pltpu.VMEM)
    in_specs = [] if table is None else [pl.BlockSpec(memory_space=pltpu.SMEM)]
    moved = sum(int(np.prod(s.array.shape)) * s.array.dtype.itemsize for s in ins)
    got = pl.pallas_call(
        run,
        out_shape=list(outs),
        in_specs=in_specs + [vmem] * len(ins) + [pl.BlockSpec(memory_space=pl.ANY)] * len(after),
        out_specs=[vmem] * len(outs),
        scratch_shapes=list(scratch),
        compiler_params=pltpu.CompilerParams(vmem_limit_bytes=VMEM_LIMIT),
        cost_estimate=pl.CostEstimate(flops=int(flops), bytes_accessed=moved, transcendentals=0),
        name=name,
    )(*([] if table is None else [table]), *[one.array for one in ins], *after)
    return got if len(outs) > 1 else got[0]


def sds(shape, dtype):
    return jax.ShapeDtypeStruct(shape, dtype)


def chosen_rows(bands_ref, send_ref):
    rows, slots = bands_ref.shape[0], send_ref.shape[1]
    onehot = (iota((rows, slots), 0) == send_ref[...]).astype(F32).astype(BF16)
    return mm_tn(onehot, bands_ref[...])


def pick_kernel(loads, outs, scratch):
    send, bands = loads
    outs[0][...] = chosen_rows(bands(), send()).astype(BF16)


def pick_direct_kernel(count, my_ref, loads, outs, scratch):
    send, bands = loads
    held = scratch[0]
    held[...] = chosen_rows(bands(), send()).reshape(held.shape).astype(BF16)
    for s, out in enumerate(outs):
        for e in range(2):
            out[e] = held[my_ref[0] ^ (2 * s + e)]


def relay_kernel(loads, outs, scratch):
    for i, one in enumerate(loads):
        outs[0][i] = one()[...]


def spread(weights, fixed_first, pix):
    width = pix * GROUP
    shape = (pix * pix, pix * width)
    r, c = iota(shape, 0), iota(shape, 1)
    outer, inner = c // width, (c % width) // GROUP
    if fixed_first:
        sel = (r // pix == outer) & (r % pix == inner)
    else:
        sel = (r % pix == outer) & (r // pix == inner)
    out = mm(weights, sel.astype(F32).astype(BF16))
    own = iota(out.shape, 0) % GROUP == iota(out.shape, 1) % GROUP
    return jnp.where(own, out, 0.0)


def store_spread(out_ref, value, row0, col0, pix):
    groups = value.shape[0] // GROUP
    width = pix * GROUP
    for o in range(0, pix, 2):
        lo = value[:, o * width : (o + 1) * width].reshape(groups, GROUP, width)
        hi = value[:, (o + 1) * width : (o + 2) * width].reshape(groups, GROUP, width)
        both = jnp.concatenate([lo, hi], axis=1).astype(BF16)
        out_ref[:, row0 + o * GROUP : row0 + (o + 2) * GROUP, col0 : col0 + width] = both


def tile_move(ch, j, total):
    lo = (ch * j // LANES) * LANES
    hi = min(lo + 2 * LANES, total)
    shape = (hi - lo, LANES)
    move = (iota(shape, 0) - (ch * j - lo) == iota(shape, 1)) & (iota(shape, 1) < ch)
    return lo, hi, move.astype(F32).astype(BF16)


def weights_by_slot(recv, weight, slots, level):
    pixsq = weight.shape[1] // recv.shape[0]
    r = iota((slots, recv.shape[1]), 0)
    total = None
    for k in (2 * level, 2 * level + 1):
        hit = (recv[k : k + 1, :] == r).astype(F32).astype(BF16)
        term = mm(hit, weight[:, k * pixsq : (k + 1) * pixsq])
        total = term if total is None else total + term
    return total


def over(values, size):
    return jnp.floor((values.astype(F32) + 0.5) * (1.0 / size)).astype(jnp.int32)


def bias_rows(rel_ref, tab_ref, out_ref):
    blocks, heads, entries = rel_ref.shape
    span = WIN * WIN
    half = WIN // 2

    def row_col(pos):
        side = pos // (span // 2)
        return (pos % (span // 2)) // half, side * half + pos % half

    shape = (span, LANES)
    ra, ca = row_col(iota(shape, 0))
    rb, cb = row_col(iota(shape, 1) % span)
    index = (ra - rb + WIN - 1) * (2 * WIN - 1) + ca - cb + WIN - 1
    low = jnp.minimum(index, LANES - 1)
    high = jnp.maximum(index - LANES, 0)
    first = iota(shape, 1) < span
    for b in range(blocks):
        tab_ref[:, :entries] = rel_ref[b]
        for m in range(heads // 2):
            both = []
            for h in (2 * m, 2 * m + 1):
                lo = jnp.broadcast_to(tab_ref[h : h + 1, :LANES], shape)
                hi = jnp.broadcast_to(tab_ref[h : h + 1, LANES:], shape)
                got_lo = jnp.take_along_axis(lo, low, axis=1, mode="promise_in_bounds")
                got_hi = jnp.take_along_axis(hi, high, axis=1, mode="promise_in_bounds")
                both.append(jnp.where(index < LANES, got_lo, got_hi))
            out_ref[b, :, m * LANES : (m + 1) * LANES] = jnp.where(first, both[0], both[1])


def weights_kernel(loads, outs, scratch):
    recv, weight = (one() for one in loads)
    slots = 2 * recv.shape[1]
    pixsq = weight.shape[1] // recv.shape[0]
    totals = [weights_by_slot(recv, weight, slots, v).reshape(slots // GROUP, GROUP, pixsq) for v in range(2)]
    outs[0][...] = jnp.concatenate(totals, axis=1).reshape(2 * slots, pixsq).astype(BF16)


def split_slots(recv, cap, me):
    slot = recv[...]
    sender = over(slot, cap)
    inner = slot - sender * cap
    return sender ^ me, inner


def patch_turn(pd):
    half = WIN // 2
    r, c = iota((pd, pd), 0), iota((pd, pd), 1)
    side, rest = r // (ROWS * half), r % (ROWS * half)
    return ((rest // half) * WIN + side * half + rest % half == c).astype(F32).astype(BF16)


def chosen(shape, axis, row0, vals):
    r = iota(shape, axis) + row0
    slot = (r // (2 * GROUP)) * GROUP + r % GROUP
    level = (r // GROUP) % 2
    first = (vals(0) == slot) | (vals(1) == slot)
    second = (vals(2) == slot) | (vals(3) == slot)
    hit = (first & (level == 0)) | (second & (level == 1))
    return hit.astype(F32).astype(BF16)


def prep_kernel(cap, me_ref, loads, outs, scratch):
    recv, weight, embed, rel = (one() for one in loads)
    mix_ref, scatter_ref, embed_out, bias_ref = outs
    kk, pd = recv.shape
    slots = 2 * pd
    pixsq = weight.shape[1] // kk
    pix = int(round(pixsq**0.5))
    ch = embed.shape[0] // pix
    sender, inner = split_slots(recv, cap, me_ref[0])
    slot = sender * cap + inner
    for level in range(2):
        total = weights_by_slot(slot, weight, slots, level)
        store_spread(mix_ref, spread(total.astype(BF16), True, pix), level * pix * GROUP, 0, pix)
    turn = patch_turn(pd)
    parts = [v.astype(F32).astype(BF16) for v in (sender, inner)]
    cols = (mm_nt(turn, parts[0]) * cap + mm_nt(turn, parts[1])).astype(jnp.int32)
    stages, _, width = scatter_ref.shape
    for stage in range(stages):
        scatter_ref[stage] = chosen((pd, width), 1, stage * width, lambda k: cols[:, k : k + 1])
    for i in range(pix):
        lo, hi, move = tile_move(ch, i, embed.shape[0])
        embed_out[i * LANES : (i + 1) * LANES, :] = mm_tn(move, embed[lo:hi, :]).astype(BF16)
    bias_rows(rel, scratch[0], bias_ref)


def prep_back_kernel(cap, me_ref, loads, outs, scratch):
    weight_ref, recv, unembed = (one() for one in loads)
    mix_ref, select_ref, unembed_out = outs
    rows, pixsq = weight_ref.shape
    pix = int(round(pixsq**0.5))
    ch = unembed.shape[0] // pix
    groups = rows // (2 * GROUP)
    w3 = weight_ref[...].astype(F32).reshape(groups, 2, GROUP, pixsq)
    for level in range(2):
        w_l = w3[:, level].reshape(groups * GROUP, pixsq).astype(BF16)
        store_spread(mix_ref, spread(w_l, False, pix), 0, level * pix * GROUP, pix)
    pd = recv.shape[1]
    turn = patch_turn(pd)
    parts = [v.astype(F32).astype(BF16) for v in split_slots(recv, cap, me_ref[0])]
    slot = (mm_nt(parts[0], turn) * cap + mm_nt(parts[1], turn)).astype(jnp.int32)
    select_ref[...] = chosen((rows, pd), 0, 0, lambda k: slot[k : k + 1, :])
    for i in range(pix):
        lo, hi, move = tile_move(ch, i, unembed.shape[0])
        unembed_out[i * LANES : (i + 1) * LANES, :] = mm_tn(move, unembed[lo:hi, :]).astype(BF16)


def layer_norm(values, gain):
    average = jnp.mean(values, axis=-1, keepdims=True)
    centred = values - average
    spread_ = jnp.mean(centred * centred, axis=-1, keepdims=True)
    return centred * lax.rsqrt(spread_ + norm_eps) * gain


def head_mask(heads, span, d):
    head_of = iota((heads * span, d), 0) // span == iota((heads * span, d), 1) // (d // heads)
    return head_of.astype(F32).astype(BF16)


def softmax_parts(scores, side):
    out = []
    for m in range(scores.shape[1] // LANES):
        part = scores[:, m * LANES : (m + 1) * LANES]
        low = iota(part.shape, 1) % LANES < side
        top_lo = jnp.max(jnp.where(low, part, -3e38), axis=-1, keepdims=True)
        top_hi = jnp.max(jnp.where(low, -3e38, part), axis=-1, keepdims=True)
        out.append(jnp.exp(part - jnp.where(low, top_lo, top_hi)))
    return jnp.concatenate(out, axis=1)


def attend_rows(query, key, value, bias, heads, mask, blocked):
    d = query.shape[1]
    key_all = jnp.concatenate([key] * heads, axis=0) * mask
    value_all = jnp.concatenate([value] * heads, axis=0) * mask
    scores = mm_nt(query, key_all) * (d // heads) ** (-0.5) + bias
    if blocked is not None:
        scores = jnp.where(blocked, -1e30, scores)
    weights = softmax_parts(scores, key.shape[0]).astype(BF16)
    return mm(weights, value_all), weights


def feed_forward(residual, gain2, up, down):
    normed = layer_norm(residual, gain2).astype(BF16)
    hidden = jax.nn.gelu(mm(normed, up)).astype(BF16)
    return (residual + mm(hidden, down)).astype(BF16)


def lay_tiles(rows, count):
    return jnp.concatenate([rows[:, t * LANES : (t + 1) * LANES] for t in range(count)], axis=0)


def joined(chunks):
    pieces = [one()[...].astype(F32).reshape(-1, one.ref.shape[-1]) for one in chunks]
    return jnp.concatenate(pieces, axis=0).astype(BF16)


def regrid_part(data, x_ref, c_ref, mix, scatter, embed, pix):
    slots, width = data.shape
    ch = width // pix
    for j in range(pix):
        lo, hi, move = tile_move(ch, j, width)
        x_ref[:, j * LANES : (j + 1) * LANES] = mm(data[:, lo:hi], move)
    mix_ref = mix()

    def group(g, carry):
        tiles = lay_tiles(x_ref[pl.ds(pl.multiple_of(g * GROUP, GROUP), GROUP), :], pix).astype(BF16)
        out = mm(mix_ref[g], tiles)
        to = pl.ds(pl.multiple_of(g * 2 * GROUP, 2 * GROUP), 2 * GROUP)
        for i in range(pix):
            low = out[i * GROUP : (i + 1) * GROUP]
            high = out[(pix + i) * GROUP : (pix + i + 1) * GROUP]
            both = jnp.concatenate([low, high], axis=0).astype(BF16)
            c_ref[to, i * LANES : (i + 1) * LANES] = both
        return carry

    lax.fori_loop(0, slots // GROUP, group, 0, unroll=4)
    scatter_ref, embed_ref = scatter(), embed()
    total = None
    for j in range(0, pix, 2):
        cols = slice(j * LANES, (j + 2) * LANES)
        pixels = mm(scatter_ref[...], c_ref[:, cols])
        term = mm(pixels.astype(BF16), embed_ref[cols, :])
        total = term if total is None else total + term
    return total


def early_kernel(pix, loads, outs, scratch):
    *chunks, mix, scatter, embed = loads
    outs[0][...] = regrid_part(joined(chunks), *scratch, mix, scatter, embed, pix)


def first_kernel(pix, layer, loads, outs, scratch):
    *chunks, mix, scatter, embed, prior, gain1, gain2, qkv, bias, proj, up, down = loads
    total = regrid_part(joined(chunks), *scratch, mix, scatter, embed, pix)
    state = (prior()[...] + total).astype(BF16).astype(F32)
    pd, d = state.shape
    heads = bias.ref.shape[1] // (WIN * WIN)
    normed = layer_norm(state, gain1()[layer : layer + 1, :]).astype(BF16)
    packed = mm(normed, qkv()[...]).astype(BF16)
    query, key, value = packed[:, :d], packed[:, d : 2 * d], packed[:, 2 * d :]
    half = pd // 2
    win_rows = ROWS // WIN
    part_rows = half // win_rows
    bias_all = bias()[...]
    mask = head_mask(heads, WIN * WIN, d)
    mixed = [None] * (2 * win_rows)
    weights = [None] * (2 * win_rows)
    for w in range(win_rows):
        def rows(v):
            lo, hi = w * part_rows, (w + 1) * part_rows
            return jnp.concatenate([v[lo:hi], v[half + lo : half + hi]], axis=0)
        out, wts = attend_rows(rows(query), rows(key), rows(value), bias_all, heads, mask, None)
        mixed[w], mixed[win_rows + w] = out[:part_rows], out[part_rows:]
        weights[w], weights[win_rows + w] = wts[:part_rows], wts[part_rows:]
    total = mm(jnp.concatenate(weights, axis=0), mask)
    mixed = (jnp.concatenate(mixed, axis=0) / total).astype(BF16)
    attended = mm(mixed, proj()[...]).astype(BF16)
    residual = state + attended.astype(F32)
    new = feed_forward(residual, gain2()[layer : layer + 1, :], up()[...], down()[...])
    outs[0][...] = new[:half]
    outs[1][...] = new[half:]


def second_kernel(layer, loads, outs, scratch):
    low, high, gain1, gain2, qkv, bias, left, right, proj, up, down, select = loads
    half, d = low.ref.shape
    heads = bias.ref.shape[1] // (WIN * WIN)
    shift = half * (WIN // 2) // ROWS
    turn = lambda v: jnp.concatenate([v[shift:], v[:shift]], axis=0)
    back = lambda v: jnp.concatenate([v[half - shift :], v[: half - shift]], axis=0)
    own = jnp.concatenate([turn(low()[...]), turn(high()[...])], axis=0).astype(F32)
    gain = gain1()[layer : layer + 1, :]
    normed = layer_norm(own, gain).astype(BF16)
    strips = jnp.concatenate([turn(left()[...]), turn(right()[...])], axis=0).astype(F32)
    normed_s = layer_norm(strips, gain).astype(BF16)
    packed = mm(normed, qkv()[...]).astype(BF16)
    packed_s = mm(normed_s, qkv()[:, d:]).astype(BF16)
    query, key, value = packed[:, :d], packed[:, d : 2 * d], packed[:, 2 * d :]
    key_s, value_s = packed_s[:, :d], packed_s[:, d:]
    win_rows = ROWS // WIN
    part = half // win_rows
    span = WIN * WIN
    bias_all = bias()[...]
    mask = head_mask(heads, span, d)
    outs_m, outs_w = [[], []], [[], []]
    for w in range(win_rows):
        near = slice(w * part, (w + 1) * part)
        far = slice(half + w * part, half + (w + 1) * part)
        for side in range(2):
            if side == 0:
                q = query[near]
                k = jnp.concatenate([key_s[near], key[near]], axis=0)
                v = jnp.concatenate([value_s[near], value[near]], axis=0)
                b = bias_all[part:]
            else:
                q = query[far]
                k = jnp.concatenate([key[far], key_s[far]], axis=0)
                v = jnp.concatenate([value[far], value_s[far]], axis=0)
                b = bias_all[:part]
            blocked = None
            if w == win_rows - 1:
                shape = (part, heads * span)
                q_up = iota(shape, 0) % part >= part // 2
                k_up = iota(shape, 1) % part >= part // 2
                blocked = q_up != k_up
            out, wts = attend_rows(q, k, v, b, heads, mask, blocked)
            outs_m[side].append(out)
            outs_w[side].append(wts)
    total = mm(jnp.concatenate(outs_w[0] + outs_w[1], axis=0), mask)
    mixed = (jnp.concatenate(outs_m[0] + outs_m[1], axis=0) / total).astype(BF16)
    attended = mm(mixed, proj()[...]).astype(BF16)
    residual = own + attended.astype(F32)
    new = feed_forward(residual, gain2()[layer : layer + 1, :], up()[...], down()[...])
    state = jnp.concatenate([back(new[:half]), back(new[half:])], axis=0)
    sent = mm(select()[...], state).astype(BF16)
    if len(outs) == 1:
        outs[0][...] = sent
        return
    rows = sent.shape[0] // (2 * len(outs))
    for x in range(2 * len(outs)):
        outs[x // 2][x % 2] = sent[x * rows : (x + 1) * rows]


def back_part(size, first, me_ref, chunks, mix, unembed, p_ref, slot_ref):
    rows = jnp.concatenate([one()[...].reshape(-1, one.ref.shape[-1]) for one in chunks], axis=0)
    unembed_ref = unembed()
    pix = unembed_ref.shape[0] // LANES
    for j in range(0, pix, 2):
        cols = slice(j * LANES, (j + 2) * LANES)
        p_ref[:, cols] = mm_nt(rows, unembed_ref[cols, :])
    mix_ref = mix()

    def group(g, carry):
        got = p_ref[pl.ds(pl.multiple_of(g * 2 * GROUP, 2 * GROUP), 2 * GROUP), :]
        data = jnp.concatenate([lay_tiles(got[:GROUP], pix), lay_tiles(got[GROUP:], pix)], axis=0)
        where = first + g
        if size is not None:
            chunk = lax.div(where, size)
            where = (chunk ^ me_ref[0]) * size + where - chunk * size
        out = mm(mix_ref[where], data.astype(BF16))
        to = pl.ds(pl.multiple_of(g * GROUP, GROUP), GROUP)
        for i in range(pix):
            slot_ref[to, i * LANES : (i + 1) * LANES] = out[i * GROUP : (i + 1) * GROUP]
        return carry

    lax.fori_loop(0, rows.shape[0] // (2 * GROUP), group, 0, unroll=4)


def back_kernel(size, first, me_ref, loads, outs, scratch):
    *chunks, unembed, mix = loads
    back_part(size, first, me_ref, chunks, mix, unembed, *scratch)
    outs[0][...] = scratch[1][...].astype(BF16)


def last_kernel(size, first, me_ref, loads, outs, scratch):
    *chunks, unembed, mix, prior, send = loads
    back_part(size, first, me_ref, chunks, mix, unembed, *scratch)
    slot_ref, out_ref = scratch[1], outs[0]
    pix = unembed.ref.shape[0] // LANES
    pd, total = out_ref.shape
    ch = total // pix
    cut = prior.ref.shape[0]
    prior_ref = prior()
    owner = jnp.broadcast_to(send()[...], (GROUP, send.ref.shape[1]))
    if size is not None:
        cap = size * GROUP
        count = owner.shape[1] // cap
        chunk = over(iota(owner.shape, 1), cap)
        for bit in range(count.bit_length() - 1):
            gap = cap << bit
            up = pltpu.roll(owner, owner.shape[1] - gap, 1)
            down = pltpu.roll(owner, gap, 1)
            swapped = jnp.where((chunk >> bit) & 1 == 0, up, down)
            owner = jnp.where((me_ref[0] >> bit) & 1 == 1, swapped, owner)
    onehot = (iota((pd, owner.shape[1]), 0) == owner[:1]).astype(F32).astype(BF16)
    tiles = [None] * (-(-total // LANES))
    for j in range(0, pix, 2):
        cols = slice(j * LANES, (j + 2) * LANES)
        slots = jnp.concatenate([prior_ref[:, cols], slot_ref[:, cols].astype(BF16)], axis=0)
        both = mm(onehot, slots)
        for jj in (j, j + 1):
            val = both[:, (jj - j) * LANES : (jj - j + 1) * LANES]
            t, off = divmod(ch * jj, LANES)
            if off:
                val = pltpu.roll(val, off, 1)
            lane = iota(val.shape, 1)
            low, high = jnp.where(lane >= off, val, 0.0), jnp.where(lane < off, val, 0.0)
            for tt, piece in ((t, low), (t + 1, high)):
                if tt == t + 1 and off + ch <= LANES:
                    continue
                tiles[tt] = piece if tiles[tt] is None else tiles[tt] + piece
    for t, tile in enumerate(tiles):
        hi = min((t + 1) * LANES, total)
        out_ref[:, t * LANES : hi] = tile[:, : hi - t * LANES]


def swap(value, axis):
    return lax.all_to_all(value, axis, split_axis=0, concat_axis=0, tiled=True)


def swap_pairs(value, axis):
    count = lax.axis_size(axis)
    rows, width = value.shape
    cap = rows // (2 * count)
    if cap % GROUP == 0:
        return swap(value, axis)
    groups = rows // (2 * GROUP)
    v = value.reshape(groups, 2, GROUP, width).transpose(1, 0, 2, 3).reshape(2, count, cap, width)
    v = swap(v.transpose(1, 0, 2, 3).reshape(rows, width), axis)
    v = v.reshape(count, 2, cap, width).transpose(1, 0, 2, 3).reshape(2, groups, GROUP, width)
    return v.transpose(1, 0, 2, 3).reshape(rows, width)


def flip(value, axis, bits):
    count = lax.axis_size(axis)
    return lax.ppermute(value, axis, [(source, source ^ bits) for source in range(count)])


def from_behind(value, axis, steps):
    count = lax.axis_size(axis)
    pairs = [(source, (source + steps) % count) for source in range(count)]
    return lax.ppermute(value, axis, pairs)


STAGES = 2
NEAR = 4


def body(
    bands, send_table, recv_table, regrid_weight, embed_weight, norm1_gain, qkv_weight, rel_bias,
    proj_weight, norm2_gain, up_weight, down_weight, unembed_weight,
):
    pd, width = bands.shape
    slots = send_table.shape[1]
    kk = recv_table.shape[0]
    d = embed_weight.shape[1]
    pixsq = regrid_weight.shape[1] // kk
    pix = int(round(pixsq**0.5))
    wide = pix * LANES
    count = lax.axis_size("tile")
    cap = slots // count
    chips = count // 2
    direct = chips == 2 * NEAR and cap % GROUP == 0
    vm = pltpu.VMEM
    per = slots // STAGES
    groups = per // GROUP
    my = lax.axis_index("tile").astype(jnp.int32).reshape(1)
    if not direct:
        my = my * 0

    if direct:
        turns = [*range(NEAR, chips), *range(NEAR - 1, 0, -1)]

        outgoing = call("pick", functools.partial(pick_direct_kernel, count), [In(send_table), In(bands)],
                        [sds((2, cap, width), BF16)] * chips, [vm((count, cap, width), BF16)], my)
        came = [outgoing[0]] + [None] * (chips - 1)
        for s in turns:
            came[s] = flip(outgoing[s], "tile", 2 * s)
    else:
        outgoing = call("pick", pick_kernel, [In(send_table), In(bands)], [sds((slots, width), BF16)])
        incoming = swap(outgoing, "tile").reshape(STAGES, per, width)

    heads = rel_bias.shape[1]
    span = WIN * WIN
    wsend = call("weights", weights_kernel, [In(recv_table), In(regrid_weight)], [sds((2 * slots, pixsq), BF16)],
                 flops=2e8)
    wback = swap_pairs(wsend, "tile")
    mix, scatter, embed_pad, bias = call(
        "prep", functools.partial(prep_kernel, cap),
        [In(recv_table), In(regrid_weight), In(embed_weight), In(rel_bias)],
        [sds((slots // GROUP, 2 * pix * GROUP, pix * GROUP), BF16), sds((STAGES, pd, 2 * per), BF16),
         sds((wide, d), BF16), sds((rel_bias.shape[0], span, heads * span), F32)],
        [vm((heads, 2 * LANES), F32)], my, flops=4e9, after=[wsend])

    def relay(arrays, after=()):
        shape = (len(arrays), *arrays[0].shape[1:])
        return call("relay", relay_kernel, [at(x, 1) for x in arrays], [sds(shape, BF16)], after=after)

    def mix_rows(stage):
        return In(mix, slice(stage * groups, (stage + 1) * groups))

    regrid_scratch = [vm((per, wide), F32), vm((2 * per, wide), BF16)]
    if direct:
        near_pass = flip(relay(came[:NEAR], [wsend]), "tile", 1)
        near = [y for i, x in enumerate(came[:NEAR]) for y in (at(x, 0), at(near_pass, i))]
    else:
        near, far = [at(incoming, 0)], [at(incoming, 1)]
    total = call("early", functools.partial(early_kernel, pix),
                 [*near, mix_rows(0), at(scatter, 0), In(embed_pad)], [sds((pd, d), F32)], regrid_scratch, flops=2e9)
    if direct:
        far_pass = flip(relay(came[NEAR:], [total]), "tile", 1)
        far = [y for i, x in enumerate(came[NEAR:]) for y in (at(x, 0), at(far_pass, i))]

    def layer(n):
        return [In(norm1_gain), In(norm2_gain), at(qkv_weight, n), at(bias, n)], [
            at(proj_weight, n), at(up_weight, n), at(down_weight, n)]

    half = pd // 2
    ins_a, ins_b = layer(0)
    low, high = call(
        "first", functools.partial(first_kernel, pix, 0),
        [*far, mix_rows(1), at(scatter, 1), In(embed_pad), In(total), *ins_a, *ins_b],
        [sds((half, d), BF16)] * 2, regrid_scratch, flops=4e9)
    right = from_behind(low, "tile", -1)
    left = from_behind(high, "tile", 1)
    mix_back, select, unembed_pad = call(
        "prep_back", functools.partial(prep_back_kernel, cap), [In(wback), In(recv_table), In(unembed_weight.T)],
        [sds((slots // GROUP, pix * GROUP, 2 * pix * GROUP), BF16), sds((2 * slots, pd), BF16), sds((wide, d), BF16)],
        (), my, flops=2e9, after=[low])
    ins_a, ins_b = layer(1)
    rows = 2 * cap
    sent = call(
        "second", functools.partial(second_kernel, 1),
        [In(low), In(high), *ins_a, In(left), In(right), *ins_b, In(select)],
        [sds((2, rows, d), BF16)] * chips if direct else [sds((2 * slots, d), BF16)], flops=2e9, after=[mix_back])

    size = cap // GROUP if direct else None
    back_scratch = [vm((2 * per, wide), F32), vm((per, wide), F32)]
    if direct:
        got = [sent[0]] + [None] * (chips - 1)
        for s in turns:
            got[s] = flip(sent[s], "tile", 2 * s)
        near_pass = flip(relay(got[:NEAR]), "tile", 1)
        near = [y for i, x in enumerate(got[:NEAR]) for y in (at(x, 0), at(near_pass, i))]
    else:
        got = swap_pairs(sent, "tile").reshape(STAGES, 2 * per, d)
        near, far = [at(got, 0)], [at(got, 1)]
    prior = call("back", functools.partial(back_kernel, size, 0), [*near, In(unembed_pad), In(mix_back)],
                 [sds((per, wide), BF16)], back_scratch, my, flops=2e9)
    if direct:
        far_pass = flip(relay(got[NEAR:], [prior]), "tile", 1)
        far = [y for i, x in enumerate(got[NEAR:]) for y in (at(x, 0), at(far_pass, i))]
    return call("last", functools.partial(last_kernel, size, groups), [*far, In(unembed_pad), In(mix_back), In(prior), In(send_table)],
                [sds((pd, width), F32)], back_scratch, my, flops=3e9)


def solution(mesh):
    in_specs = (
        P(("groups", "tile"), None), P("tile", None), P(None, "tile"), P("tile", None),
        P(), P(), P(), P(), P(), P(), P(), P(), P(),
    )
    out_specs = P(("groups", "tile"), None)
    return jax.shard_map(body, mesh=mesh, in_specs=in_specs, out_specs=out_specs, check_vma=False)
```

```python
import functools

import jax
import jax.numpy as jnp
import numpy as np
from jax import lax
from jax.experimental import pallas as pl
from jax.experimental.pallas import tpu as pltpu
from jax.sharding import PartitionSpec as P


WIN = 8
ROWS = 24
LANES = 128
GROUP = 8

norm_eps = 1e-05
F32 = jnp.float32
BF16 = jnp.bfloat16


def iota(shape, axis):
    return lax.broadcasted_iota(jnp.int32, shape, axis)


def mm(a, b):
    return jnp.dot(a, b, preferred_element_type=F32)


def mm_tn(a, b):
    return lax.dot_general(a, b, (((0,), (0,)), ((), ())), preferred_element_type=F32)


def mm_nt(a, b):
    return lax.dot_general(a, b, (((1,), (1,)), ((), ())), preferred_element_type=F32)


VMEM_LIMIT = 16 << 20


class In:
    def __init__(self, array, index=None):
        self.array = array
        self.index = index


def at(array, index):
    return In(array, index)


class Loaded:
    def __init__(self, ref):
        self.ref = ref

    def __call__(self):
        return self.ref


def call(kernel, ins, outs, scratch=(), table=None, flops=0, after=()):
    def run(*refs):
        refs = list(refs)
        lead = [refs.pop(0)] if table is not None else []
        loads = []
        for one in ins:
            ref = refs.pop(0)
            loads.append(Loaded(ref if one.index is None else ref.at[one.index]))
        del refs[: len(after)]
        held = [refs.pop(0) for _ in outs]
        kernel(*lead, loads, held, refs)

    vmem = pl.BlockSpec(memory_space=pltpu.VMEM)
    in_specs = [] if table is None else [pl.BlockSpec(memory_space=pltpu.SMEM)]
    moved = sum(int(np.prod(s.array.shape)) * s.array.dtype.itemsize for s in ins)
    got = pl.pallas_call(
        run,
        out_shape=list(outs),
        in_specs=in_specs + [vmem] * len(ins) + [pl.BlockSpec(memory_space=pl.ANY)] * len(after),
        out_specs=[vmem] * len(outs),
        scratch_shapes=list(scratch),
        compiler_params=pltpu.CompilerParams(vmem_limit_bytes=VMEM_LIMIT),
        cost_estimate=pl.CostEstimate(flops=int(flops), bytes_accessed=moved, transcendentals=0),
    )(*([] if table is None else [table]), *[one.array for one in ins], *after)
    return got if len(outs) > 1 else got[0]


def sds(shape, dtype):
    return jax.ShapeDtypeStruct(shape, dtype)


def chosen_rows(bands_ref, send_ref):
    rows, slots = bands_ref.shape[0], send_ref.shape[1]
    onehot = (iota((rows, slots), 0) == send_ref[...]).astype(F32).astype(BF16)
    return mm_tn(onehot, bands_ref[...])


def pick_kernel(loads, outs, scratch):
    send, bands = loads
    outs[0][...] = chosen_rows(bands(), send()).astype(BF16)


def pick_direct_kernel(my_ref, loads, outs, scratch):
    send, bands = loads
    held = scratch[0]
    held[...] = chosen_rows(bands(), send()).reshape(held.shape).astype(BF16)
    for s, out in enumerate(outs):
        for e in range(2):
            out[e] = held[my_ref[0] ^ (2 * s + e)]


def relay_kernel(loads, outs, scratch):
    for i, one in enumerate(loads):
        outs[0][i] = one()[...]


def spread(weights, fixed_first, pix):
    width = pix * GROUP
    shape = (pix * pix, pix * width)
    r, c = iota(shape, 0), iota(shape, 1)
    outer, inner = c // width, (c % width) // GROUP
    if fixed_first:
        sel = (r // pix == outer) & (r % pix == inner)
    else:
        sel = (r % pix == outer) & (r // pix == inner)
    out = mm(weights, sel.astype(F32).astype(BF16))
    own = iota(out.shape, 0) % GROUP == iota(out.shape, 1) % GROUP
    return jnp.where(own, out, 0.0)


def store_spread(out_ref, value, row0, col0, pix):
    groups = value.shape[0] // GROUP
    width = pix * GROUP
    for o in range(0, pix, 2):
        lo = value[:, o * width : (o + 1) * width].reshape(groups, GROUP, width)
        hi = value[:, (o + 1) * width : (o + 2) * width].reshape(groups, GROUP, width)
        both = jnp.concatenate([lo, hi], axis=1).astype(BF16)
        out_ref[:, row0 + o * GROUP : row0 + (o + 2) * GROUP, col0 : col0 + width] = both


def tile_move(ch, j, total):
    lo = (ch * j // LANES) * LANES
    hi = min(lo + 2 * LANES, total)
    shape = (hi - lo, LANES)
    move = (iota(shape, 0) - (ch * j - lo) == iota(shape, 1)) & (iota(shape, 1) < ch)
    return lo, hi, move.astype(F32).astype(BF16)


def weights_by_slot(recv, weight, slots, level):
    pixsq = weight.shape[1] // recv.shape[0]
    r = iota((slots, recv.shape[1]), 0)
    total = None
    for k in (2 * level, 2 * level + 1):
        hit = (recv[k : k + 1, :] == r).astype(F32).astype(BF16)
        term = mm(hit, weight[:, k * pixsq : (k + 1) * pixsq])
        total = term if total is None else total + term
    return total


def over(values, size):
    return jnp.floor((values.astype(F32) + 0.5) * (1.0 / size)).astype(jnp.int32)


def bias_rows(rel_ref, tab_ref, out_ref):
    heads, blocks, entries = rel_ref.shape
    span = WIN * WIN
    half = WIN // 2

    def row_col(pos):
        side = pos // (span // 2)
        return (pos % (span // 2)) // half, side * half + pos % half

    shape = (span, LANES)
    ra, ca = row_col(iota(shape, 0))
    rb, cb = row_col(iota(shape, 1) % span)
    index = (ra - rb + WIN - 1) * (2 * WIN - 1) + ca - cb + WIN - 1
    low = jnp.minimum(index, LANES - 1)
    high = jnp.maximum(index - LANES, 0)
    first = iota(shape, 1) < span
    for b in range(blocks):
        for h in range(heads):
            tab_ref[h : h + 1, :entries] = rel_ref[h, b : b + 1, :]
        for m in range(heads // 2):
            both = []
            for h in (2 * m, 2 * m + 1):
                lo = jnp.broadcast_to(tab_ref[h : h + 1, :LANES], shape)
                hi = jnp.broadcast_to(tab_ref[h : h + 1, LANES:], shape)
                got_lo = jnp.take_along_axis(lo, low, axis=1, mode="promise_in_bounds")
                got_hi = jnp.take_along_axis(hi, high, axis=1, mode="promise_in_bounds")
                both.append(jnp.where(index < LANES, got_lo, got_hi))
            out_ref[b, :, m * LANES : (m + 1) * LANES] = jnp.where(first, both[0], both[1])


def weights_kernel(loads, outs, scratch):
    recv, weight = (one() for one in loads)
    slots = 2 * recv.shape[1]
    pixsq = weight.shape[1] // recv.shape[0]
    totals = [weights_by_slot(recv, weight, slots, v).reshape(slots // GROUP, GROUP, pixsq) for v in range(2)]
    outs[0][...] = jnp.concatenate(totals, axis=1).reshape(2 * slots, pixsq).astype(BF16)


def split_slots(recv, cap, me):
    slot = recv[...]
    sender = over(slot, cap)
    inner = slot - sender * cap
    return sender ^ me, inner


def patch_turn(pd):
    half = WIN // 2
    r, c = iota((pd, pd), 0), iota((pd, pd), 1)
    side, rest = r // (ROWS * half), r % (ROWS * half)
    return ((rest // half) * WIN + side * half + rest % half == c).astype(F32).astype(BF16)


def chosen(shape, axis, row0, vals):
    r = iota(shape, axis) + row0
    slot = (r // (2 * GROUP)) * GROUP + r % GROUP
    level = (r // GROUP) % 2
    first = (vals(0) == slot) | (vals(1) == slot)
    second = (vals(2) == slot) | (vals(3) == slot)
    hit = (first & (level == 0)) | (second & (level == 1))
    return hit.astype(F32).astype(BF16)


def prep_kernel(cap, me_ref, loads, outs, scratch):
    recv, weight, embed, rel = (one() for one in loads)
    mix_ref, scatter_ref, embed_out, bias_ref, select_ref = outs
    kk, pd = recv.shape
    slots = 2 * pd
    pixsq = weight.shape[1] // kk
    pix = int(round(pixsq**0.5))
    ch = embed.shape[0] // pix
    sender, inner = split_slots(recv, cap, me_ref[0])
    slot = sender * cap + inner
    for level in range(2):
        total = weights_by_slot(slot, weight, slots, level)
        store_spread(mix_ref, spread(total.astype(BF16), True, pix), level * pix * GROUP, 0, pix)
    turn = patch_turn(pd)
    parts = [v.astype(F32).astype(BF16) for v in (sender, inner)]
    cols = (mm_nt(turn, parts[0]) * cap + mm_nt(turn, parts[1])).astype(jnp.int32)
    rows = (mm_nt(parts[0], turn) * cap + mm_nt(parts[1], turn)).astype(jnp.int32)
    select_ref[...] = chosen((2 * slots, pd), 0, 0, lambda k: rows[k : k + 1, :])
    stages, _, width = scatter_ref.shape
    for stage in range(stages):
        scatter_ref[stage] = chosen((pd, width), 1, stage * width, lambda k: cols[:, k : k + 1])
    for i in range(pix):
        lo, hi, move = tile_move(ch, i, embed.shape[0])
        embed_out[i * LANES : (i + 1) * LANES, :] = mm_tn(move, embed[lo:hi, :]).astype(BF16)
    bias_rows(rel, scratch[0], bias_ref)


def prep_back_kernel(loads, outs, scratch):
    weight_ref, unembed = (one() for one in loads)
    mix_ref, unembed_out = outs
    rows, pixsq = weight_ref.shape
    pix = int(round(pixsq**0.5))
    ch = unembed.shape[0] // pix
    groups = rows // (2 * GROUP)
    w3 = weight_ref[...].astype(F32).reshape(groups, 2, GROUP, pixsq)
    for level in range(2):
        w_l = w3[:, level].reshape(groups * GROUP, pixsq).astype(BF16)
        store_spread(mix_ref, spread(w_l, False, pix), 0, level * pix * GROUP, pix)
    for i in range(pix):
        lo, hi, move = tile_move(ch, i, unembed.shape[0])
        unembed_out[i * LANES : (i + 1) * LANES, :] = mm_tn(move, unembed[lo:hi, :]).astype(BF16)


def layer_norm(values, gain):
    average = jnp.mean(values, axis=-1, keepdims=True)
    centred = values - average
    spread_ = jnp.mean(centred * centred, axis=-1, keepdims=True)
    return centred * lax.rsqrt(spread_ + norm_eps) * gain


def head_mask(heads, span, d):
    head_of = iota((heads * span, d), 0) // span == iota((heads * span, d), 1) // (d // heads)
    return head_of.astype(F32).astype(BF16)


def softmax_parts(scores, side):
    out = []
    for m in range(scores.shape[1] // LANES):
        part = scores[:, m * LANES : (m + 1) * LANES]
        low = iota(part.shape, 1) % LANES < side
        top_lo = jnp.max(jnp.where(low, part, -3e38), axis=-1, keepdims=True)
        top_hi = jnp.max(jnp.where(low, -3e38, part), axis=-1, keepdims=True)
        out.append(jnp.exp(part - jnp.where(low, top_lo, top_hi)))
    return jnp.concatenate(out, axis=1)


def attend_rows(query, key, value, bias, heads, mask, blocked):
    d = query.shape[1]
    key_all = jnp.concatenate([key] * heads, axis=0) * mask
    value_all = jnp.concatenate([value] * heads, axis=0) * mask
    scores = mm_nt(query, key_all) * (d // heads) ** (-0.5) + bias
    if blocked is not None:
        scores = jnp.where(blocked, -1e30, scores)
    weights = softmax_parts(scores, key.shape[0]).astype(BF16)
    return mm(weights, value_all), weights


def feed_forward(residual, gain2, up, down):
    normed = layer_norm(residual, gain2).astype(BF16)
    hidden = jax.nn.gelu(mm(normed, up)).astype(BF16)
    return (residual + mm(hidden, down)).astype(BF16)


def lay_tiles(rows, count):
    return jnp.concatenate([rows[:, t * LANES : (t + 1) * LANES] for t in range(count)], axis=0)


def joined(chunks):
    pieces = [one()[...].astype(F32).reshape(-1, one.ref.shape[-1]) for one in chunks]
    return jnp.concatenate(pieces, axis=0).astype(BF16)


def regrid_part(data, x_ref, c_ref, mix, scatter, embed, pix):
    slots, width = data.shape
    ch = width // pix
    for j in range(pix):
        lo, hi, move = tile_move(ch, j, width)
        x_ref[:, j * LANES : (j + 1) * LANES] = mm(data[:, lo:hi], move)
    mix_ref = mix()

    def group(g, carry):
        tiles = lay_tiles(x_ref[pl.ds(pl.multiple_of(g * GROUP, GROUP), GROUP), :], pix).astype(BF16)
        out = mm(mix_ref[g], tiles)
        to = pl.ds(pl.multiple_of(g * 2 * GROUP, 2 * GROUP), 2 * GROUP)
        for i in range(pix):
            low = out[i * GROUP : (i + 1) * GROUP]
            high = out[(pix + i) * GROUP : (pix + i + 1) * GROUP]
            both = jnp.concatenate([low, high], axis=0).astype(BF16)
            c_ref[to, i * LANES : (i + 1) * LANES] = both
        return carry

    lax.fori_loop(0, slots // GROUP, group, 0, unroll=4)
    scatter_ref, embed_ref = scatter(), embed()
    total = None
    for j in range(0, pix, 2):
        cols = slice(j * LANES, (j + 2) * LANES)
        pixels = mm(scatter_ref[...], c_ref[:, cols])
        term = mm(pixels.astype(BF16), embed_ref[cols, :])
        total = term if total is None else total + term
    return total


def early_kernel(pix, loads, outs, scratch):
    *chunks, mix, scatter, embed = loads
    outs[0][...] = regrid_part(joined(chunks), *scratch, mix, scatter, embed, pix)


def first_kernel(pix, layer, loads, outs, scratch):
    *chunks, mix, scatter, embed, prior, gain1, gain2, qkv, bias, proj, up, down = loads
    total = regrid_part(joined(chunks), *scratch, mix, scatter, embed, pix)
    state = (prior()[...] + total).astype(BF16).astype(F32)
    pd, d = state.shape
    heads = bias.ref.shape[1] // (WIN * WIN)
    normed = layer_norm(state, gain1()[layer : layer + 1, :]).astype(BF16)
    packed = mm(normed, qkv()[...]).astype(BF16)
    query, key, value = packed[:, :d], packed[:, d : 2 * d], packed[:, 2 * d :]
    half = pd // 2
    win_rows = ROWS // WIN
    part_rows = half // win_rows
    bias_all = bias()[...]
    mask = head_mask(heads, WIN * WIN, d)
    mixed = [None] * (2 * win_rows)
    weights = [None] * (2 * win_rows)
    for w in range(win_rows):
        def rows(v):
            lo, hi = w * part_rows, (w + 1) * part_rows
            return jnp.concatenate([v[lo:hi], v[half + lo : half + hi]], axis=0)

        out, wts = attend_rows(rows(query), rows(key), rows(value), bias_all, heads, mask, None)
        mixed[w], mixed[win_rows + w] = out[:part_rows], out[part_rows:]
        weights[w], weights[win_rows + w] = wts[:part_rows], wts[part_rows:]
    total = mm(jnp.concatenate(weights, axis=0), mask)
    mixed = (jnp.concatenate(mixed, axis=0) / total).astype(BF16)
    attended = mm(mixed, proj()[...]).astype(BF16)
    residual = state + attended.astype(F32)
    new = feed_forward(residual, gain2()[layer : layer + 1, :], up()[...], down()[...])
    outs[0][...] = new[:half]
    outs[1][...] = new[half:]


def second_kernel(layer, loads, outs, scratch):
    low, high, gain1, gain2, qkv, bias, left, right, proj, up, down, select = loads
    half, d = low.ref.shape
    heads = bias.ref.shape[1] // (WIN * WIN)
    shift = half * (WIN // 2) // ROWS
    turn = lambda v: jnp.concatenate([v[shift:], v[:shift]], axis=0)
    back = lambda v: jnp.concatenate([v[half - shift :], v[: half - shift]], axis=0)
    own = jnp.concatenate([turn(low()[...]), turn(high()[...])], axis=0).astype(F32)
    gain = gain1()[layer : layer + 1, :]
    normed = layer_norm(own, gain).astype(BF16)
    strips = jnp.concatenate([turn(left()[...]), turn(right()[...])], axis=0).astype(F32)
    normed_s = layer_norm(strips, gain).astype(BF16)
    packed = mm(normed, qkv()[...]).astype(BF16)
    packed_s = mm(normed_s, qkv()[:, d:]).astype(BF16)
    query, key, value = packed[:, :d], packed[:, d : 2 * d], packed[:, 2 * d :]
    key_s, value_s = packed_s[:, :d], packed_s[:, d:]
    win_rows = ROWS // WIN
    part = half // win_rows
    span = WIN * WIN
    bias_all = bias()[...]
    mask = head_mask(heads, span, d)
    outs_m, outs_w = [[], []], [[], []]
    for w in range(win_rows):
        near = slice(w * part, (w + 1) * part)
        far = slice(half + w * part, half + (w + 1) * part)
        for side in range(2):
            if side == 0:
                q = query[near]
                k = jnp.concatenate([key_s[near], key[near]], axis=0)
                v = jnp.concatenate([value_s[near], value[near]], axis=0)
                b = bias_all[part:]
            else:
                q = query[far]
                k = jnp.concatenate([key[far], key_s[far]], axis=0)
                v = jnp.concatenate([value[far], value_s[far]], axis=0)
                b = bias_all[:part]
            blocked = None
            if w == win_rows - 1:
                shape = (part, heads * span)
                q_up = iota(shape, 0) % part >= part // 2
                k_up = iota(shape, 1) % part >= part // 2
                blocked = q_up != k_up
            out, wts = attend_rows(q, k, v, b, heads, mask, blocked)
            outs_m[side].append(out)
            outs_w[side].append(wts)
    total = mm(jnp.concatenate(outs_w[0] + outs_w[1], axis=0), mask)
    mixed = (jnp.concatenate(outs_m[0] + outs_m[1], axis=0) / total).astype(BF16)
    attended = mm(mixed, proj()[...]).astype(BF16)
    residual = own + attended.astype(F32)
    new = feed_forward(residual, gain2()[layer : layer + 1, :], up()[...], down()[...])
    state = jnp.concatenate([back(new[:half]), back(new[half:])], axis=0)
    sent = mm(select()[...], state).astype(BF16)
    if len(outs) == 1:
        outs[0][...] = sent
        return
    rows = sent.shape[0] // (2 * len(outs))
    for x in range(2 * len(outs)):
        outs[x // 2][x % 2] = sent[x * rows : (x + 1) * rows]


def back_part(size, first, me_ref, chunks, mix, unembed, p_ref, slot_ref):
    rows = jnp.concatenate([one()[...].reshape(-1, one.ref.shape[-1]) for one in chunks], axis=0)
    unembed_ref = unembed()
    pix = unembed_ref.shape[0] // LANES
    for j in range(0, pix, 2):
        cols = slice(j * LANES, (j + 2) * LANES)
        p_ref[:, cols] = mm_nt(rows, unembed_ref[cols, :])
    mix_ref = mix()

    def group(g, carry):
        got = p_ref[pl.ds(pl.multiple_of(g * 2 * GROUP, 2 * GROUP), 2 * GROUP), :]
        data = jnp.concatenate([lay_tiles(got[:GROUP], pix), lay_tiles(got[GROUP:], pix)], axis=0)
        where = first + g
        if size is not None:
            chunk = lax.div(where, size)
            where = (chunk ^ me_ref[0]) * size + where - chunk * size
        out = mm(mix_ref[where], data.astype(BF16))
        to = pl.ds(pl.multiple_of(g * GROUP, GROUP), GROUP)
        for i in range(pix):
            slot_ref[to, i * LANES : (i + 1) * LANES] = out[i * GROUP : (i + 1) * GROUP]
        return carry

    lax.fori_loop(0, rows.shape[0] // (2 * GROUP), group, 0, unroll=4)


def back_kernel(size, first, me_ref, loads, outs, scratch):
    *chunks, unembed, mix = loads
    back_part(size, first, me_ref, chunks, mix, unembed, *scratch)
    outs[0][...] = scratch[1][...].astype(BF16)


def last_kernel(size, first, me_ref, loads, outs, scratch):
    *chunks, unembed, mix, prior, send = loads
    back_part(size, first, me_ref, chunks, mix, unembed, *scratch)
    slot_ref, out_ref = scratch[1], outs[0]
    pix = unembed.ref.shape[0] // LANES
    pd, total = out_ref.shape
    ch = total // pix
    prior_ref = prior()
    owner = jnp.broadcast_to(send()[...], (GROUP, send.ref.shape[1]))
    if size is not None:
        cap = size * GROUP
        count = owner.shape[1] // cap
        chunk = over(iota(owner.shape, 1), cap)
        for bit in range(count.bit_length() - 1):
            gap = cap << bit
            up = pltpu.roll(owner, owner.shape[1] - gap, 1)
            down = pltpu.roll(owner, gap, 1)
            swapped = jnp.where((chunk >> bit) & 1 == 0, up, down)
            owner = jnp.where((me_ref[0] >> bit) & 1 == 1, swapped, owner)
    onehot = (iota((pd, owner.shape[1]), 0) == owner[:1]).astype(F32).astype(BF16)
    tiles = [None] * (-(-total // LANES))
    for j in range(0, pix, 2):
        cols = slice(j * LANES, (j + 2) * LANES)
        slots = jnp.concatenate([prior_ref[:, cols], slot_ref[:, cols].astype(BF16)], axis=0)
        both = mm(onehot, slots)
        for jj in (j, j + 1):
            val = both[:, (jj - j) * LANES : (jj - j + 1) * LANES]
            t, off = divmod(ch * jj, LANES)
            if off:
                val = pltpu.roll(val, off, 1)
            lane = iota(val.shape, 1)
            low, high = jnp.where(lane >= off, val, 0.0), jnp.where(lane < off, val, 0.0)
            for tt, piece in ((t, low), (t + 1, high)):
                if tt == t + 1 and off + ch <= LANES:
                    continue
                tiles[tt] = piece if tiles[tt] is None else tiles[tt] + piece
    for t, tile in enumerate(tiles):
        hi = min((t + 1) * LANES, total)
        out_ref[:, t * LANES : hi] = tile[:, : hi - t * LANES]


def swap(value, axis):
    return lax.all_to_all(value, axis, split_axis=0, concat_axis=0, tiled=True)


def swap_pairs(value, axis):
    count = lax.axis_size(axis)
    rows, width = value.shape
    cap = rows // (2 * count)
    if cap % GROUP == 0:
        return swap(value, axis)
    groups = rows // (2 * GROUP)
    v = value.reshape(groups, 2, GROUP, width).transpose(1, 0, 2, 3).reshape(2, count, cap, width)
    v = swap(v.transpose(1, 0, 2, 3).reshape(rows, width), axis)
    v = v.reshape(count, 2, cap, width).transpose(1, 0, 2, 3).reshape(2, groups, GROUP, width)
    return v.transpose(1, 0, 2, 3).reshape(rows, width)


def flip(value, axis, bits):
    count = lax.axis_size(axis)
    return lax.ppermute(value, axis, [(source, source ^ bits) for source in range(count)])


def from_behind(value, axis, steps):
    count = lax.axis_size(axis)
    pairs = [(source, (source + steps) % count) for source in range(count)]
    return lax.ppermute(value, axis, pairs)


STAGES = 2
NEAR = 4


def body(
    bands, send_table, recv_table, regrid_weight, embed_weight, norm1_gain, qkv_weight, rel_bias,
    proj_weight, norm2_gain, up_weight, down_weight, unembed_weight,
):
    pd, width = bands.shape
    slots = send_table.shape[1]
    kk = recv_table.shape[0]
    d = embed_weight.shape[1]
    pixsq = regrid_weight.shape[1] // kk
    pix = int(round(pixsq**0.5))
    wide = pix * LANES
    count = lax.axis_size("tile")
    cap = slots // count
    chips = count // 2
    direct = chips == 2 * NEAR and cap % GROUP == 0
    vm = pltpu.VMEM
    per = slots // STAGES
    groups = per // GROUP
    my = lax.axis_index("tile").astype(jnp.int32).reshape(1)
    if not direct:
        my = my * 0

    if direct:
        turns = [*range(NEAR, chips), *range(NEAR - 1, 0, -1)]

        outgoing = call(pick_direct_kernel, [In(send_table), In(bands)],
                        [sds((2, cap, width), BF16)] * chips, [vm((count, cap, width), BF16)], my)
        came = [outgoing[0]] + [None] * (chips - 1)
        for s in turns:
            came[s] = flip(outgoing[s], "tile", 2 * s)
    else:
        outgoing = call(pick_kernel, [In(send_table), In(bands)], [sds((slots, width), BF16)])
        incoming = swap(outgoing, "tile").reshape(STAGES, per, width)

    heads = rel_bias.shape[1]
    span = WIN * WIN
    wsend = call(weights_kernel, [In(recv_table), In(regrid_weight)], [sds((2 * slots, pixsq), BF16)],
                 flops=2e8)
    wback = swap_pairs(wsend, "tile")
    mix, scatter, embed_pad, bias, select = call(
        functools.partial(prep_kernel, cap),
        [In(recv_table), In(regrid_weight), In(embed_weight), In(rel_bias.transpose(1, 0, 2))],
        [sds((slots // GROUP, 2 * pix * GROUP, pix * GROUP), BF16), sds((STAGES, pd, 2 * per), BF16),
         sds((wide, d), BF16), sds((rel_bias.shape[0], span, heads * span), F32),
         sds((2 * slots, pd), BF16)],
        [vm((heads, 2 * LANES), F32)], my, flops=4e9, after=[wsend])

    def relay(arrays, after=()):
        shape = (len(arrays), *arrays[0].shape[1:])
        return call(relay_kernel, [at(x, 1) for x in arrays], [sds(shape, BF16)], after=after)

    def mix_rows(stage):
        return In(mix, slice(stage * groups, (stage + 1) * groups))

    regrid_scratch = [vm((per, wide), F32), vm((2 * per, wide), BF16)]
    if direct:
        near_all = relay(came[:NEAR], [wsend])
        near_pass = flip(near_all, "tile", 1)
        near = [y for i, x in enumerate(came[:NEAR]) for y in (at(x, 0), at(near_pass, i))]
    else:
        near, far = [at(incoming, 0)], [at(incoming, 1)]
    total = call(functools.partial(early_kernel, pix),
                 [*near, mix_rows(0), at(scatter, 0), In(embed_pad)], [sds((pd, d), F32)], regrid_scratch, flops=2e9)
    if direct:
        far_pass = flip(relay(came[NEAR:], [total]), "tile", 1)
        far = [y for i, x in enumerate(came[NEAR:]) for y in (at(x, 0), at(far_pass, i))]

    def layer(n):
        return [In(norm1_gain), In(norm2_gain), at(qkv_weight, n), at(bias, n)], [
            at(proj_weight, n), at(up_weight, n), at(down_weight, n)]

    half = pd // 2
    ins_a, ins_b = layer(0)
    low, high = call(
        functools.partial(first_kernel, pix, 0),
        [*far, mix_rows(1), at(scatter, 1), In(embed_pad), In(total), *ins_a, *ins_b],
        [sds((half, d), BF16)] * 2, regrid_scratch, flops=4e9)
    right = from_behind(low, "tile", -1)
    left = from_behind(high, "tile", 1)
    ins_a, ins_b = layer(1)
    rows = 2 * cap
    sent = call(
        functools.partial(second_kernel, 1),
        [In(low), In(high), *ins_a, In(left), In(right), *ins_b, In(select)],
        [sds((2, rows, d), BF16)] * chips if direct else [sds((2 * slots, d), BF16)], flops=2e9)
    one_sent = sent[0] if direct else sent
    mix_back, unembed_pad = call(
        prep_back_kernel, [In(wback), In(unembed_weight.T)],
        [sds((slots // GROUP, pix * GROUP, 2 * pix * GROUP), BF16), sds((wide, d), BF16)], flops=2e9, after=[one_sent])

    size = cap // GROUP if direct else None
    back_scratch = [vm((2 * per, wide), F32), vm((per, wide), F32)]
    if direct:
        got = [sent[0]] + [None] * (chips - 1)
        for s in turns:
            got[s] = flip(sent[s], "tile", 2 * s)
        near_pass = flip(relay(got[:NEAR]), "tile", 1)
        near = [y for i, x in enumerate(got[:NEAR]) for y in (at(x, 0), at(near_pass, i))]
    else:
        got = swap_pairs(sent, "tile").reshape(STAGES, 2 * per, d)
        near, far = [at(got, 0)], [at(got, 1)]
    prior = call(functools.partial(back_kernel, size, 0), [*near, In(unembed_pad), In(mix_back)],
                 [sds((per, wide), BF16)], back_scratch, my, flops=2e9)
    if direct:
        far_pass = flip(relay(got[NEAR:], [prior]), "tile", 1)
        far = [y for i, x in enumerate(got[NEAR:]) for y in (at(x, 0), at(far_pass, i))]
    return call(functools.partial(last_kernel, size, groups), [*far, In(unembed_pad), In(mix_back), In(prior), In(send_table)],
                [sds((pd, width), F32)], back_scratch, my, flops=3e9)


def solution(mesh):
    in_specs = (
        P(("groups", "tile"), None), P("tile", None), P(None, "tile"), P("tile", None),
        P(), P(), P(), P(), P(), P(), P(), P(), P(),
    )
    out_specs = P(("groups", "tile"), None)
    return jax.shard_map(body, mesh=mesh, in_specs=in_specs, out_specs=out_specs, check_vma=False)
```

```python
import functools

import jax
import jax.numpy as jnp
import numpy as np
from jax import lax
from jax.experimental import pallas as pl
from jax.experimental.pallas import tpu as pltpu
from jax.sharding import PartitionSpec as P


WIN = 8
ROWS = 24
LANES = 128
GROUP = 8

norm_eps = 1e-05
F32 = jnp.float32
BF16 = jnp.bfloat16


def iota(shape, axis):
    return lax.broadcasted_iota(jnp.int32, shape, axis)


def mm(a, b):
    return jnp.dot(a, b, preferred_element_type=F32)


def mm_tn(a, b):
    return lax.dot_general(a, b, (((0,), (0,)), ((), ())), preferred_element_type=F32)


def mm_nt(a, b):
    return lax.dot_general(a, b, (((1,), (1,)), ((), ())), preferred_element_type=F32)


VMEM_LIMIT = 16 << 20


class In:
    def __init__(self, array, index=None):
        self.array = array
        self.index = index


def at(array, index):
    return In(array, index)


class Loaded:
    def __init__(self, ref):
        self.ref = ref

    def __call__(self):
        return self.ref


def call(kernel, ins, outs, scratch=(), table=None, flops=0, after=()):
    def run(*refs):
        refs = list(refs)
        lead = [refs.pop(0)] if table is not None else []
        loads = []
        for one in ins:
            ref = refs.pop(0)
            loads.append(Loaded(ref if one.index is None else ref.at[one.index]))
        del refs[: len(after)]
        held = [refs.pop(0) for _ in outs]
        kernel(*lead, loads, held, refs)

    vmem = pl.BlockSpec(memory_space=pltpu.VMEM)
    in_specs = [] if table is None else [pl.BlockSpec(memory_space=pltpu.SMEM)]
    moved = sum(int(np.prod(s.array.shape)) * s.array.dtype.itemsize for s in ins)
    got = pl.pallas_call(
        run,
        out_shape=list(outs),
        in_specs=in_specs + [vmem] * len(ins) + [pl.BlockSpec(memory_space=pl.ANY)] * len(after),
        out_specs=[vmem] * len(outs),
        scratch_shapes=list(scratch),
        compiler_params=pltpu.CompilerParams(vmem_limit_bytes=VMEM_LIMIT),
        cost_estimate=pl.CostEstimate(flops=int(flops), bytes_accessed=moved, transcendentals=0),
    )(*([] if table is None else [table]), *[one.array for one in ins], *after)
    return got if len(outs) > 1 else got[0]


def sds(shape, dtype):
    return jax.ShapeDtypeStruct(shape, dtype)


def chosen_rows(bands_ref, send_ref):
    rows, slots = bands_ref.shape[0], send_ref.shape[1]
    onehot = (iota((rows, slots), 0) == send_ref[...]).astype(F32).astype(BF16)
    return mm_tn(onehot, bands_ref[...])


def pick_kernel(loads, outs, scratch):
    send, bands = loads
    outs[0][...] = chosen_rows(bands(), send()).astype(BF16)


def pick_direct_kernel(my_ref, loads, outs, scratch):
    send, bands = loads
    held = scratch[0]
    held[...] = chosen_rows(bands(), send()).reshape(held.shape).astype(BF16)
    for s, out in enumerate(outs):
        for e in range(2):
            out[e] = held[my_ref[0] ^ (2 * s + e)]


def relay_kernel(loads, outs, scratch):
    for i, one in enumerate(loads):
        outs[0][i] = one()[...]


def spread(weights, fixed_first, pix):
    width = pix * GROUP
    shape = (pix * pix, pix * width)
    r, c = iota(shape, 0), iota(shape, 1)
    outer, inner = c // width, (c % width) // GROUP
    if fixed_first:
        sel = (r // pix == outer) & (r % pix == inner)
    else:
        sel = (r % pix == outer) & (r // pix == inner)
    out = mm(weights, sel.astype(F32).astype(BF16))
    own = iota(out.shape, 0) % GROUP == iota(out.shape, 1) % GROUP
    return jnp.where(own, out, 0.0)


def store_spread(out_ref, value, row0, col0, pix):
    groups = value.shape[0] // GROUP
    width = pix * GROUP
    for o in range(0, pix, 2):
        lo = value[:, o * width : (o + 1) * width].reshape(groups, GROUP, width)
        hi = value[:, (o + 1) * width : (o + 2) * width].reshape(groups, GROUP, width)
        both = jnp.concatenate([lo, hi], axis=1).astype(BF16)
        out_ref[:, row0 + o * GROUP : row0 + (o + 2) * GROUP, col0 : col0 + width] = both


def tile_move(ch, j, total):
    lo = (ch * j // LANES) * LANES
    hi = min(lo + 2 * LANES, total)
    shape = (hi - lo, LANES)
    move = (iota(shape, 0) - (ch * j - lo) == iota(shape, 1)) & (iota(shape, 1) < ch)
    return lo, hi, move.astype(F32).astype(BF16)


def weights_by_slot(recv, weight, slots, level):
    pixsq = weight.shape[1] // recv.shape[0]
    r = iota((slots, recv.shape[1]), 0)
    total = None
    for k in (2 * level, 2 * level + 1):
        hit = (recv[k : k + 1, :] == r).astype(F32).astype(BF16)
        term = mm(hit, weight[:, k * pixsq : (k + 1) * pixsq])
        total = term if total is None else total + term
    return total


def over(values, size):
    return jnp.floor((values.astype(F32) + 0.5) * (1.0 / size)).astype(jnp.int32)


def bias_rows(rel_ref, tab_ref, out_ref):
    heads, blocks, entries = rel_ref.shape
    span = WIN * WIN
    half = WIN // 2

    def row_col(pos):
        side = pos // (span // 2)
        return (pos % (span // 2)) // half, side * half + pos % half

    shape = (span, LANES)
    ra, ca = row_col(iota(shape, 0))
    rb, cb = row_col(iota(shape, 1) % span)
    index = (ra - rb + WIN - 1) * (2 * WIN - 1) + ca - cb + WIN - 1
    low = jnp.minimum(index, LANES - 1)
    high = jnp.maximum(index - LANES, 0)
    first = iota(shape, 1) < span
    for b in range(blocks):
        for h in range(heads):
            tab_ref[h : h + 1, :entries] = rel_ref[h, b : b + 1, :]
        for m in range(heads // 2):
            both = []
            for h in (2 * m, 2 * m + 1):
                lo = jnp.broadcast_to(tab_ref[h : h + 1, :LANES], shape)
                hi = jnp.broadcast_to(tab_ref[h : h + 1, LANES:], shape)
                got_lo = jnp.take_along_axis(lo, low, axis=1, mode="promise_in_bounds")
                got_hi = jnp.take_along_axis(hi, high, axis=1, mode="promise_in_bounds")
                both.append(jnp.where(index < LANES, got_lo, got_hi))
            out_ref[b, :, m * LANES : (m + 1) * LANES] = jnp.where(first, both[0], both[1])


def weights_kernel(loads, outs, scratch):
    recv, weight = (one() for one in loads)
    slots = 2 * recv.shape[1]
    pixsq = weight.shape[1] // recv.shape[0]
    totals = [weights_by_slot(recv, weight, slots, v).reshape(slots // GROUP, GROUP, pixsq) for v in range(2)]
    outs[0][...] = jnp.concatenate(totals, axis=1).reshape(2 * slots, pixsq).astype(BF16)


def split_slots(recv, cap, me):
    slot = recv[...]
    sender = over(slot, cap)
    inner = slot - sender * cap
    return sender ^ me, inner


def patch_turn(pd):
    half = WIN // 2
    r, c = iota((pd, pd), 0), iota((pd, pd), 1)
    side, rest = r // (ROWS * half), r % (ROWS * half)
    return ((rest // half) * WIN + side * half + rest % half == c).astype(F32).astype(BF16)


def chosen(shape, axis, vals, chunk_of=None, size=1):
    r = iota(shape, axis)
    if chunk_of is not None:
        chunk = over(r, size)
        r = chunk_of(chunk) * size + r - chunk * size
    slot = (r // (2 * GROUP)) * GROUP + r % GROUP
    level = (r // GROUP) % 2
    first = (vals(0) == slot) | (vals(1) == slot)
    second = (vals(2) == slot) | (vals(3) == slot)
    hit = (first & (level == 0)) | (second & (level == 1))
    return hit.astype(F32).astype(BF16)


def prep_kernel(cap, direct, me_ref, loads, outs, scratch):
    recv, weight, embed, rel = (one() for one in loads)
    mix_ref, *scatter_refs, embed_out, bias_ref, select_ref = outs
    kk, pd = recv.shape
    slots = 2 * pd
    pixsq = weight.shape[1] // kk
    pix = int(round(pixsq**0.5))
    ch = embed.shape[0] // pix
    sender, inner = split_slots(recv, cap, me_ref[0])
    slot = sender * cap + inner
    for level in range(2):
        total = weights_by_slot(slot, weight, slots, level)
        store_spread(mix_ref, spread(total.astype(BF16), True, pix), level * pix * GROUP, 0, pix)
    turn = patch_turn(pd)
    parts = [v.astype(F32).astype(BF16) for v in (sender, inner)]
    cols = (mm_nt(turn, parts[0]) * cap + mm_nt(turn, parts[1])).astype(jnp.int32)
    rows = (mm_nt(parts[0], turn) * cap + mm_nt(parts[1], turn)).astype(jnp.int32)
    select_ref[...] = chosen((2 * slots, pd), 0, lambda k: rows[k : k + 1, :])
    for stage, ref in enumerate(scatter_refs):
        ref[...] = chosen(ref.shape, 1, lambda k: cols[:, k : k + 1],
                          functools.partial(stage_chunk, stage, direct), 2 * slots // (4 * NEAR))
    for i in range(pix):
        lo, hi, move = tile_move(ch, i, embed.shape[0])
        embed_out[i * LANES : (i + 1) * LANES, :] = mm_tn(move, embed[lo:hi, :]).astype(BF16)
    bias_rows(rel, scratch[0], bias_ref)


def prep_back_kernel(size, me_ref, loads, outs, scratch):
    weight, unembed, send = loads
    weight_ref, unembed = weight(), unembed()
    mix_ref, unembed_out, owner_ref = outs
    owner = jnp.broadcast_to(send()[...], (GROUP, send.ref.shape[1]))
    if size is not None:
        cap = size * GROUP
        count = owner.shape[1] // cap
        chunk = over(iota(owner.shape, 1), cap)
        for bit in range(count.bit_length() - 1):
            gap = cap << bit
            up = pltpu.roll(owner, owner.shape[1] - gap, 1)
            down = pltpu.roll(owner, gap, 1)
            swapped = jnp.where((chunk >> bit) & 1 == 0, up, down)
            owner = jnp.where((me_ref[0] >> bit) & 1 == 1, swapped, owner)
    owner_ref[...] = owner
    rows, pixsq = weight_ref.shape
    pix = int(round(pixsq**0.5))
    ch = unembed.shape[0] // pix
    groups = rows // (2 * GROUP)
    w3 = weight_ref[...].astype(F32).reshape(groups, 2, GROUP, pixsq)
    for level in range(2):
        w_l = w3[:, level].reshape(groups * GROUP, pixsq).astype(BF16)
        store_spread(mix_ref, spread(w_l, False, pix), 0, level * pix * GROUP, pix)
    for i in range(pix):
        lo, hi, move = tile_move(ch, i, unembed.shape[0])
        unembed_out[i * LANES : (i + 1) * LANES, :] = mm_tn(move, unembed[lo:hi, :]).astype(BF16)


def layer_norm(values, gain):
    average = jnp.mean(values, axis=-1, keepdims=True)
    centred = values - average
    spread_ = jnp.mean(centred * centred, axis=-1, keepdims=True)
    return centred * lax.rsqrt(spread_ + norm_eps) * gain


def head_mask(heads, span, d):
    head_of = iota((heads * span, d), 0) // span == iota((heads * span, d), 1) // (d // heads)
    return head_of.astype(F32).astype(BF16)


def softmax_parts(scores, side):
    out = []
    for m in range(scores.shape[1] // LANES):
        part = scores[:, m * LANES : (m + 1) * LANES]
        low = iota(part.shape, 1) % LANES < side
        top_lo = jnp.max(jnp.where(low, part, -3e38), axis=-1, keepdims=True)
        top_hi = jnp.max(jnp.where(low, -3e38, part), axis=-1, keepdims=True)
        out.append(jnp.exp(part - jnp.where(low, top_lo, top_hi)))
    return jnp.concatenate(out, axis=1)


def attend_rows(query, key, value, bias, heads, mask, blocked):
    d = query.shape[1]
    key_all = jnp.concatenate([key] * heads, axis=0) * mask
    value_all = jnp.concatenate([value] * heads, axis=0) * mask
    scores = mm_nt(query, key_all) * (d // heads) ** (-0.5) + bias
    if blocked is not None:
        scores = jnp.where(blocked, -1e30, scores)
    weights = softmax_parts(scores, key.shape[0]).astype(BF16)
    return mm(weights, value_all), weights


def feed_forward(residual, gain2, up, down):
    normed = layer_norm(residual, gain2).astype(BF16)
    hidden = jax.nn.gelu(mm(normed, up)).astype(BF16)
    return (residual + mm(hidden, down)).astype(BF16)


def lay_tiles(rows, count):
    return jnp.concatenate([rows[:, t * LANES : (t + 1) * LANES] for t in range(count)], axis=0)


def joined(chunks):
    pieces = [one()[...].astype(F32).reshape(-1, one.ref.shape[-1]) for one in chunks]
    return jnp.concatenate(pieces, axis=0).astype(BF16)


def stage_chunk(stage, direct, i):
    if not direct:
        return i + (0 if stage == 0 else NEAR)
    if stage == 0:
        return 2 * i
    return jnp.where(i < NEAR, 2 * i + 1, i + NEAR)


def regrid_part(stage, direct, data, x_ref, c_ref, mix, scatter, embed, pix):
    slots, width = data.shape
    ch = width // pix
    for j in range(pix):
        lo, hi, move = tile_move(ch, j, width)
        x_ref[:, j * LANES : (j + 1) * LANES] = mm(data[:, lo:hi], move)
    mix_ref = mix()
    size = mix_ref.shape[0] // (4 * NEAR)

    def group(g, carry):
        chunk = lax.div(g, size)
        where = stage_chunk(stage, direct, chunk) * size + g - chunk * size
        tiles = lay_tiles(x_ref[pl.ds(pl.multiple_of(g * GROUP, GROUP), GROUP), :], pix).astype(BF16)
        out = mm(mix_ref[where], tiles)
        to = pl.ds(pl.multiple_of(g * 2 * GROUP, 2 * GROUP), 2 * GROUP)
        for i in range(pix):
            low = out[i * GROUP : (i + 1) * GROUP]
            high = out[(pix + i) * GROUP : (pix + i + 1) * GROUP]
            both = jnp.concatenate([low, high], axis=0).astype(BF16)
            c_ref[to, i * LANES : (i + 1) * LANES] = both
        return carry

    lax.fori_loop(0, slots // GROUP, group, 0, unroll=4)
    scatter_ref, embed_ref = scatter(), embed()
    total = None
    for j in range(0, pix, 2):
        cols = slice(j * LANES, (j + 2) * LANES)
        pixels = mm(scatter_ref[...], c_ref[:, cols])
        term = mm(pixels.astype(BF16), embed_ref[cols, :])
        total = term if total is None else total + term
    return total


def early_kernel(pix, direct, loads, outs, scratch):
    *chunks, mix, scatter, embed = loads
    outs[0][...] = regrid_part(0, direct, joined(chunks), *scratch, mix, scatter, embed, pix)


def first_kernel(pix, direct, layer, loads, outs, scratch):
    *chunks, mix, scatter, embed, prior, gain1, gain2, qkv, bias, proj, up, down = loads
    total = regrid_part(1, direct, joined(chunks), *scratch, mix, scatter, embed, pix)
    state = (prior()[...] + total).astype(BF16).astype(F32)
    pd, d = state.shape
    heads = bias.ref.shape[1] // (WIN * WIN)
    normed = layer_norm(state, gain1()[layer : layer + 1, :]).astype(BF16)
    packed = mm(normed, qkv()[...]).astype(BF16)
    query, key, value = packed[:, :d], packed[:, d : 2 * d], packed[:, 2 * d :]
    half = pd // 2
    win_rows = ROWS // WIN
    part_rows = half // win_rows
    bias_all = bias()[...]
    mask = head_mask(heads, WIN * WIN, d)
    mixed = [None] * (2 * win_rows)
    weights = [None] * (2 * win_rows)
    for w in range(win_rows):
        def rows(v):
            lo, hi = w * part_rows, (w + 1) * part_rows
            return jnp.concatenate([v[lo:hi], v[half + lo : half + hi]], axis=0)

        out, wts = attend_rows(rows(query), rows(key), rows(value), bias_all, heads, mask, None)
        mixed[w], mixed[win_rows + w] = out[:part_rows], out[part_rows:]
        weights[w], weights[win_rows + w] = wts[:part_rows], wts[part_rows:]
    total = mm(jnp.concatenate(weights, axis=0), mask)
    mixed = (jnp.concatenate(mixed, axis=0) / total).astype(BF16)
    attended = mm(mixed, proj()[...]).astype(BF16)
    residual = state + attended.astype(F32)
    new = feed_forward(residual, gain2()[layer : layer + 1, :], up()[...], down()[...])
    outs[0][...] = new[:half]
    outs[1][...] = new[half:]


def second_kernel(layer, loads, outs, scratch):
    low, high, gain1, gain2, qkv, bias, left, right, proj, up, down, select = loads
    half, d = low.ref.shape
    heads = bias.ref.shape[1] // (WIN * WIN)
    shift = half * (WIN // 2) // ROWS
    turn = lambda v: jnp.concatenate([v[shift:], v[:shift]], axis=0)
    back = lambda v: jnp.concatenate([v[half - shift :], v[: half - shift]], axis=0)
    own = jnp.concatenate([turn(low()[...]), turn(high()[...])], axis=0).astype(F32)
    gain = gain1()[layer : layer + 1, :]
    normed = layer_norm(own, gain).astype(BF16)
    strips = jnp.concatenate([turn(left()[...]), turn(right()[...])], axis=0).astype(F32)
    normed_s = layer_norm(strips, gain).astype(BF16)
    packed = mm(normed, qkv()[...]).astype(BF16)
    packed_s = mm(normed_s, qkv()[:, d:]).astype(BF16)
    query, key, value = packed[:, :d], packed[:, d : 2 * d], packed[:, 2 * d :]
    key_s, value_s = packed_s[:, :d], packed_s[:, d:]
    win_rows = ROWS // WIN
    part = half // win_rows
    span = WIN * WIN
    bias_all = bias()[...]
    mask = head_mask(heads, span, d)
    outs_m, outs_w = [[], []], [[], []]
    for w in range(win_rows):
        near = slice(w * part, (w + 1) * part)
        far = slice(half + w * part, half + (w + 1) * part)
        for side in range(2):
            if side == 0:
                q = query[near]
                k = jnp.concatenate([key_s[near], key[near]], axis=0)
                v = jnp.concatenate([value_s[near], value[near]], axis=0)
                b = bias_all[part:]
            else:
                q = query[far]
                k = jnp.concatenate([key[far], key_s[far]], axis=0)
                v = jnp.concatenate([value[far], value_s[far]], axis=0)
                b = bias_all[:part]
            blocked = None
            if w == win_rows - 1:
                shape = (part, heads * span)
                q_up = iota(shape, 0) % part >= part // 2
                k_up = iota(shape, 1) % part >= part // 2
                blocked = q_up != k_up
            out, wts = attend_rows(q, k, v, b, heads, mask, blocked)
            outs_m[side].append(out)
            outs_w[side].append(wts)
    total = mm(jnp.concatenate(outs_w[0] + outs_w[1], axis=0), mask)
    mixed = (jnp.concatenate(outs_m[0] + outs_m[1], axis=0) / total).astype(BF16)
    attended = mm(mixed, proj()[...]).astype(BF16)
    residual = own + attended.astype(F32)
    new = feed_forward(residual, gain2()[layer : layer + 1, :], up()[...], down()[...])
    state = jnp.concatenate([back(new[:half]), back(new[half:])], axis=0)
    sent = mm(select()[...], state).astype(BF16)
    if len(outs) == 1:
        outs[0][...] = sent
        return
    rows = sent.shape[0] // (2 * len(outs))
    for x in range(2 * len(outs)):
        outs[x // 2][x % 2] = sent[x * rows : (x + 1) * rows]


def back_part(size, first, me_ref, chunks, mix, unembed, p_ref, slot_ref):
    rows = jnp.concatenate([one()[...].reshape(-1, one.ref.shape[-1]) for one in chunks], axis=0)
    unembed_ref = unembed()
    pix = unembed_ref.shape[0] // LANES
    for j in range(0, pix, 2):
        cols = slice(j * LANES, (j + 2) * LANES)
        p_ref[:, cols] = mm_nt(rows, unembed_ref[cols, :])
    mix_ref = mix()

    def group(g, carry):
        got = p_ref[pl.ds(pl.multiple_of(g * 2 * GROUP, 2 * GROUP), 2 * GROUP), :]
        data = jnp.concatenate([lay_tiles(got[:GROUP], pix), lay_tiles(got[GROUP:], pix)], axis=0)
        where = first + g
        if size is not None:
            chunk = lax.div(where, size)
            where = (chunk ^ me_ref[0]) * size + where - chunk * size
        out = mm(mix_ref[where], data.astype(BF16))
        to = pl.ds(pl.multiple_of(g * GROUP, GROUP), GROUP)
        for i in range(pix):
            slot_ref[to, i * LANES : (i + 1) * LANES] = out[i * GROUP : (i + 1) * GROUP]
        return carry

    lax.fori_loop(0, rows.shape[0] // (2 * GROUP), group, 0, unroll=4)


def back_kernel(size, first, me_ref, loads, outs, scratch):
    *chunks, unembed, mix = loads
    back_part(size, first, me_ref, chunks, mix, unembed, *scratch)
    outs[0][...] = scratch[1][...].astype(BF16)


def last_kernel(size, first, me_ref, loads, outs, scratch):
    *chunks, unembed, mix, prior, send = loads
    back_part(size, first, me_ref, chunks, mix, unembed, *scratch)
    slot_ref, out_ref = scratch[1], outs[0]
    pix = unembed.ref.shape[0] // LANES
    pd, total = out_ref.shape
    ch = total // pix
    prior_ref = prior()
    owner = send()
    onehot = (iota((pd, owner.shape[1]), 0) == owner[:1, :]).astype(F32).astype(BF16)
    tiles = [None] * (-(-total // LANES))
    for j in range(0, pix, 2):
        cols = slice(j * LANES, (j + 2) * LANES)
        slots = jnp.concatenate([prior_ref[:, cols], slot_ref[:, cols].astype(BF16)], axis=0)
        both = mm(onehot, slots)
        for jj in (j, j + 1):
            val = both[:, (jj - j) * LANES : (jj - j + 1) * LANES]
            t, off = divmod(ch * jj, LANES)
            if off:
                val = pltpu.roll(val, off, 1)
            lane = iota(val.shape, 1)
            low, high = jnp.where(lane >= off, val, 0.0), jnp.where(lane < off, val, 0.0)
            for tt, piece in ((t, low), (t + 1, high)):
                if tt == t + 1 and off + ch <= LANES:
                    continue
                tiles[tt] = piece if tiles[tt] is None else tiles[tt] + piece
    for t, tile in enumerate(tiles):
        hi = min((t + 1) * LANES, total)
        out_ref[:, t * LANES : hi] = tile[:, : hi - t * LANES]


def swap(value, axis):
    return lax.all_to_all(value, axis, split_axis=0, concat_axis=0, tiled=True)


def swap_pairs(value, axis):
    count = lax.axis_size(axis)
    rows, width = value.shape
    cap = rows // (2 * count)
    if cap % GROUP == 0:
        return swap(value, axis)
    groups = rows // (2 * GROUP)
    v = value.reshape(groups, 2, GROUP, width).transpose(1, 0, 2, 3).reshape(2, count, cap, width)
    v = swap(v.transpose(1, 0, 2, 3).reshape(rows, width), axis)
    v = v.reshape(count, 2, cap, width).transpose(1, 0, 2, 3).reshape(2, groups, GROUP, width)
    return v.transpose(1, 0, 2, 3).reshape(rows, width)


def flip(value, axis, bits):
    count = lax.axis_size(axis)
    return lax.ppermute(value, axis, [(source, source ^ bits) for source in range(count)])


def from_behind(value, axis, steps):
    count = lax.axis_size(axis)
    pairs = [(source, (source + steps) % count) for source in range(count)]
    return lax.ppermute(value, axis, pairs)


STAGES = 2
NEAR = 4


def body(
    bands, send_table, recv_table, regrid_weight, embed_weight, norm1_gain, qkv_weight, rel_bias,
    proj_weight, norm2_gain, up_weight, down_weight, unembed_weight,
):
    pd, width = bands.shape
    slots = send_table.shape[1]
    kk = recv_table.shape[0]
    d = embed_weight.shape[1]
    pixsq = regrid_weight.shape[1] // kk
    pix = int(round(pixsq**0.5))
    wide = pix * LANES
    count = lax.axis_size("tile")
    cap = slots // count
    chips = count // 2
    direct = chips == 2 * NEAR and cap % GROUP == 0
    vm = pltpu.VMEM
    per = slots // STAGES
    groups = per // GROUP
    my = lax.axis_index("tile").astype(jnp.int32).reshape(1)
    if not direct:
        my = my * 0

    if direct:
        turns = [*range(NEAR, chips), *range(NEAR - 1, 0, -1)]

        outgoing = call(pick_direct_kernel, [In(send_table), In(bands)],
                        [sds((2, cap, width), BF16)] * chips, [vm((count, cap, width), BF16)], my)
        came = [outgoing[0]] + [None] * (chips - 1)
        for s in turns:
            came[s] = flip(outgoing[s], "tile", 2 * s)
    else:
        outgoing = call(pick_kernel, [In(send_table), In(bands)], [sds((slots, width), BF16)])
        incoming = swap(outgoing, "tile")

    heads = rel_bias.shape[1]
    span = WIN * WIN
    wsend = call(weights_kernel, [In(recv_table), In(regrid_weight)], [sds((2 * slots, pixsq), BF16)],
                 flops=2e8, after=[outgoing[0] if direct else outgoing])
    wback = swap_pairs(wsend, "tile")
    mix, scatter_a, scatter_b, embed_pad, bias, select = call(
        functools.partial(prep_kernel, cap, direct),
        [In(recv_table), In(regrid_weight), In(embed_weight), In(rel_bias.transpose(1, 0, 2))],
        [sds((slots // GROUP, 2 * pix * GROUP, pix * GROUP), BF16), sds((pd, slots // 2), BF16), sds((pd, 3 * slots // 2), BF16),
         sds((wide, d), BF16), sds((rel_bias.shape[0], span, heads * span), F32),
         sds((2 * slots, pd), BF16)],
        [vm((heads, 2 * LANES), F32)], my, flops=4e9, after=[wsend])

    def relay(arrays, after=()):
        shape = (len(arrays), *arrays[0].shape[1:])
        return call(relay_kernel, [at(x, 1) for x in arrays], [sds(shape, BF16)], after=after)

    def regrid_scratch(rows):
        return [vm((rows, wide), F32), vm((2 * rows, wide), BF16)]

    if direct:
        near = [at(x, 0) for x in came[:NEAR]]
    else:
        near, far = [at(incoming, slice(0, slots // 4))], [at(incoming, slice(slots // 4, slots))]
    total = call(functools.partial(early_kernel, pix, direct),
                 [*near, In(mix), In(scatter_a), In(embed_pad)], [sds((pd, d), F32)],
                 regrid_scratch(slots // 4), flops=2e9)
    if direct:
        for_partner = relay(came, [total])
        passed = flip(for_partner, "tile", 1)
        far = [at(passed, i) for i in range(NEAR)]
        far += [y for i in range(NEAR, chips) for y in (at(came[i], 0), at(passed, i))]

    def layer(n):
        return [In(norm1_gain), In(norm2_gain), at(qkv_weight, n), at(bias, n)], [
            at(proj_weight, n), at(up_weight, n), at(down_weight, n)]

    half = pd // 2
    ins_a, ins_b = layer(0)
    low, high = call(
        functools.partial(first_kernel, pix, direct, 0),
        [*far, In(mix), In(scatter_b), In(embed_pad), In(total), *ins_a, *ins_b],
        [sds((half, d), BF16)] * 2, regrid_scratch(3 * slots // 4), flops=4e9)
    right = from_behind(low, "tile", -1)
    left = from_behind(high, "tile", 1)
    ins_a, ins_b = layer(1)
    rows = 2 * cap
    sent = call(
        functools.partial(second_kernel, 1),
        [In(low), In(high), *ins_a, In(left), In(right), *ins_b, In(select)],
        [sds((2, rows, d), BF16)] * chips if direct else [sds((2 * slots, d), BF16)], flops=2e9)
    one_sent = sent[0] if direct else sent
    size = cap // GROUP if direct else None
    mix_back, unembed_pad, owner = call(
        functools.partial(prep_back_kernel, size), [In(wback), In(unembed_weight.T), In(send_table)],
        [sds((slots // GROUP, pix * GROUP, 2 * pix * GROUP), BF16), sds((wide, d), BF16),
         sds((GROUP, slots), jnp.int32)], (), my, flops=2e9, after=[one_sent])

    back_scratch = [vm((2 * per, wide), F32), vm((per, wide), F32)]
    if direct:
        got = [sent[0]] + [None] * (chips - 1)
        for s in turns:
            got[s] = flip(sent[s], "tile", 2 * s)
        near_pass = flip(relay(got[:NEAR], [mix_back]), "tile", 1)
        near = [y for i, x in enumerate(got[:NEAR]) for y in (at(x, 0), at(near_pass, i))]
    else:
        got = swap_pairs(sent, "tile").reshape(STAGES, 2 * per, d)
        near, far = [at(got, 0)], [at(got, 1)]
    prior = call(functools.partial(back_kernel, size, 0), [*near, In(unembed_pad), In(mix_back)],
                 [sds((per, wide), BF16)], back_scratch, my, flops=2e9)
    if direct:
        far_pass = flip(relay(got[NEAR:], [prior]), "tile", 1)
        far = [y for i, x in enumerate(got[NEAR:]) for y in (at(x, 0), at(far_pass, i))]
    return call(functools.partial(last_kernel, size, groups), [*far, In(unembed_pad), In(mix_back), In(prior), In(owner)],
                [sds((pd, width), F32)], back_scratch, my, flops=3e9)


def solution(mesh):
    in_specs = (
        P(("groups", "tile"), None), P("tile", None), P(None, "tile"), P("tile", None),
        P(), P(), P(), P(), P(), P(), P(), P(), P(),
    )
    out_specs = P(("groups", "tile"), None)
    return jax.shard_map(body, mesh=mesh, in_specs=in_specs, out_specs=out_specs, check_vma=False)
```

```python
import functools

import jax
import jax.numpy as jnp
import numpy as np
from jax import lax
from jax.experimental import pallas as pl
from jax.experimental.pallas import tpu as pltpu
from jax.sharding import PartitionSpec as P


WIN = 8
ROWS = 24
LANES = 128
GROUP = 8

norm_eps = 1e-05
F32 = jnp.float32
BF16 = jnp.bfloat16


def iota(shape, axis):
    return lax.broadcasted_iota(jnp.int32, shape, axis)


def mm(a, b):
    return jnp.dot(a, b, preferred_element_type=F32)


def mm_tn(a, b):
    return lax.dot_general(a, b, (((0,), (0,)), ((), ())), preferred_element_type=F32)


def mm_nt(a, b):
    return lax.dot_general(a, b, (((1,), (1,)), ((), ())), preferred_element_type=F32)


VMEM_LIMIT = 16 << 20


class In:
    def __init__(self, array, index=None):
        self.array = array
        self.index = index


def at(array, index):
    return In(array, index)


class Loaded:
    def __init__(self, ref):
        self.ref = ref

    def __call__(self):
        return self.ref


def call(kernel, ins, outs, scratch=(), table=None, flops=0, after=()):
    def run(*refs):
        refs = list(refs)
        lead = [refs.pop(0)] if table is not None else []
        loads = []
        for one in ins:
            ref = refs.pop(0)
            loads.append(Loaded(ref if one.index is None else ref.at[one.index]))
        del refs[: len(after)]
        held = [refs.pop(0) for _ in outs]
        kernel(*lead, loads, held, refs)

    vmem = pl.BlockSpec(memory_space=pltpu.VMEM)
    in_specs = [] if table is None else [pl.BlockSpec(memory_space=pltpu.SMEM)]
    moved = sum(int(np.prod(s.array.shape)) * s.array.dtype.itemsize for s in ins)
    got = pl.pallas_call(
        run,
        out_shape=list(outs),
        in_specs=in_specs + [vmem] * len(ins) + [pl.BlockSpec(memory_space=pl.ANY)] * len(after),
        out_specs=[vmem] * len(outs),
        scratch_shapes=list(scratch),
        compiler_params=pltpu.CompilerParams(vmem_limit_bytes=VMEM_LIMIT),
        cost_estimate=pl.CostEstimate(flops=int(flops), bytes_accessed=moved, transcendentals=0),
    )(*([] if table is None else [table]), *[one.array for one in ins], *after)
    return got if len(outs) > 1 else got[0]


def sds(shape, dtype):
    return jax.ShapeDtypeStruct(shape, dtype)


def chosen_rows(bands_ref, send_ref):
    rows, slots = bands_ref.shape[0], send_ref.shape[1]
    onehot = (iota((rows, slots), 0) == send_ref[...]).astype(F32).astype(BF16)
    return mm_tn(onehot, bands_ref[...])


def pick_kernel(loads, outs, scratch):
    send, bands = loads
    outs[0][...] = chosen_rows(bands(), send()).astype(BF16)


def pick_direct_kernel(my_ref, loads, outs, scratch):
    send, bands = loads
    held = scratch[0]
    held[...] = chosen_rows(bands(), send()).reshape(held.shape).astype(BF16)
    for s, out in enumerate(outs):
        for e in range(2):
            out[e] = held[my_ref[0] ^ (2 * s + e)]


def relay_kernel(loads, outs, scratch):
    for i, one in enumerate(loads):
        outs[0][i] = one()[...]


def spread(weights, fixed_first, pix):
    width = pix * GROUP
    shape = (pix * pix, pix * width)
    r, c = iota(shape, 0), iota(shape, 1)
    outer, inner = c // width, (c % width) // GROUP
    if fixed_first:
        sel = (r // pix == outer) & (r % pix == inner)
    else:
        sel = (r % pix == outer) & (r // pix == inner)
    out = mm(weights, sel.astype(F32).astype(BF16))
    own = iota(out.shape, 0) % GROUP == iota(out.shape, 1) % GROUP
    return jnp.where(own, out, 0.0)


def store_spread(out_ref, value, row0, col0, pix):
    groups = value.shape[0] // GROUP
    width = pix * GROUP
    for o in range(0, pix, 2):
        lo = value[:, o * width : (o + 1) * width].reshape(groups, GROUP, width)
        hi = value[:, (o + 1) * width : (o + 2) * width].reshape(groups, GROUP, width)
        both = jnp.concatenate([lo, hi], axis=1).astype(BF16)
        out_ref[:, row0 + o * GROUP : row0 + (o + 2) * GROUP, col0 : col0 + width] = both


def tile_move(ch, j, total):
    lo = (ch * j // LANES) * LANES
    hi = min(lo + 2 * LANES, total)
    shape = (hi - lo, LANES)
    move = (iota(shape, 0) - (ch * j - lo) == iota(shape, 1)) & (iota(shape, 1) < ch)
    return lo, hi, move.astype(F32).astype(BF16)


def weights_by_slot(recv, weight, slots, level):
    pixsq = weight.shape[1] // recv.shape[0]
    r = iota((slots, recv.shape[1]), 0)
    total = None
    for k in (2 * level, 2 * level + 1):
        hit = (recv[k : k + 1, :] == r).astype(F32).astype(BF16)
        term = mm(hit, weight[:, k * pixsq : (k + 1) * pixsq])
        total = term if total is None else total + term
    return total


def over(values, size):
    return jnp.floor((values.astype(F32) + 0.5) * (1.0 / size)).astype(jnp.int32)


def bias_rows(rel_ref, tab_ref, out_ref):
    heads, blocks, entries = rel_ref.shape
    span = WIN * WIN
    half = WIN // 2

    def row_col(pos):
        side = pos // (span // 2)
        return (pos % (span // 2)) // half, side * half + pos % half

    shape = (span, LANES)
    ra, ca = row_col(iota(shape, 0))
    rb, cb = row_col(iota(shape, 1) % span)
    index = (ra - rb + WIN - 1) * (2 * WIN - 1) + ca - cb + WIN - 1
    low = jnp.minimum(index, LANES - 1)
    high = jnp.maximum(index - LANES, 0)
    first = iota(shape, 1) < span
    for b in range(blocks):
        for h in range(heads):
            tab_ref[h : h + 1, :entries] = rel_ref[h, b : b + 1, :]
        for m in range(heads // 2):
            both = []
            for h in (2 * m, 2 * m + 1):
                lo = jnp.broadcast_to(tab_ref[h : h + 1, :LANES], shape)
                hi = jnp.broadcast_to(tab_ref[h : h + 1, LANES:], shape)
                got_lo = jnp.take_along_axis(lo, low, axis=1, mode="promise_in_bounds")
                got_hi = jnp.take_along_axis(hi, high, axis=1, mode="promise_in_bounds")
                both.append(jnp.where(index < LANES, got_lo, got_hi))
            out_ref[b, :, m * LANES : (m + 1) * LANES] = jnp.where(first, both[0], both[1])


def weights_kernel(loads, outs, scratch):
    recv, weight = (one() for one in loads)
    slots = 2 * recv.shape[1]
    pixsq = weight.shape[1] // recv.shape[0]
    totals = [weights_by_slot(recv, weight, slots, v).reshape(slots // GROUP, GROUP, pixsq) for v in range(2)]
    outs[0][...] = jnp.concatenate(totals, axis=1).reshape(2 * slots, pixsq).astype(BF16)


def split_slots(recv, cap, me):
    slot = recv[...]
    sender = over(slot, cap)
    inner = slot - sender * cap
    return sender ^ me, inner


def patch_turn(pd):
    half = WIN // 2
    r, c = iota((pd, pd), 0), iota((pd, pd), 1)
    side, rest = r // (ROWS * half), r % (ROWS * half)
    return ((rest // half) * WIN + side * half + rest % half == c).astype(F32).astype(BF16)


def chosen(shape, axis, vals, chunk_of=None, size=1):
    r = iota(shape, axis)
    if chunk_of is not None:
        chunk = over(r, size)
        r = chunk_of(chunk) * size + r - chunk * size
    slot = (r // (2 * GROUP)) * GROUP + r % GROUP
    level = (r // GROUP) % 2
    first = (vals(0) == slot) | (vals(1) == slot)
    second = (vals(2) == slot) | (vals(3) == slot)
    hit = (first & (level == 0)) | (second & (level == 1))
    return hit.astype(F32).astype(BF16)


def tables_kernel(cap, direct, me_ref, loads, outs, scratch):
    recv, embed, rel = (one() for one in loads)
    *scatter_refs, embed_out, bias_ref, select_ref = outs
    pd = recv.shape[1]
    slots = 2 * pd
    pix = embed_out.shape[0] // LANES
    ch = embed.shape[0] // pix
    turn = patch_turn(pd)
    parts = [v.astype(F32).astype(BF16) for v in split_slots(recv, cap, me_ref[0])]
    cols = (mm_nt(turn, parts[0]) * cap + mm_nt(turn, parts[1])).astype(jnp.int32)
    rows = (mm_nt(parts[0], turn) * cap + mm_nt(parts[1], turn)).astype(jnp.int32)
    select_ref[...] = chosen((2 * slots, pd), 0, lambda k: rows[k : k + 1, :])
    for stage, ref in enumerate(scatter_refs):
        ref[...] = chosen(ref.shape, 1, lambda k: cols[:, k : k + 1],
                          functools.partial(stage_chunk, stage, direct), 2 * slots // (4 * NEAR))
    for i in range(pix):
        lo, hi, move = tile_move(ch, i, embed.shape[0])
        embed_out[i * LANES : (i + 1) * LANES, :] = mm_tn(move, embed[lo:hi, :]).astype(BF16)
    bias_rows(rel, scratch[0], bias_ref)


def mix_kernel(cap, me_ref, loads, outs, scratch):
    recv, weight = (one() for one in loads)
    slots = 2 * recv.shape[1]
    pix = int(round((weight.shape[1] // recv.shape[0]) ** 0.5))
    sender, inner = split_slots(recv, cap, me_ref[0])
    for level in range(2):
        total = weights_by_slot(sender * cap + inner, weight, slots, level)
        store_spread(outs[0], spread(total.astype(BF16), True, pix), level * pix * GROUP, 0, pix)


def prep_back_kernel(size, me_ref, loads, outs, scratch):
    weight, unembed, send = loads
    weight_ref, unembed = weight(), unembed()
    mix_ref, unembed_out, owner_ref = outs
    owner = jnp.broadcast_to(send()[...], (GROUP, send.ref.shape[1]))
    if size is not None:
        cap = size * GROUP
        count = owner.shape[1] // cap
        chunk = over(iota(owner.shape, 1), cap)
        for bit in range(count.bit_length() - 1):
            gap = cap << bit
            up = pltpu.roll(owner, owner.shape[1] - gap, 1)
            down = pltpu.roll(owner, gap, 1)
            swapped = jnp.where((chunk >> bit) & 1 == 0, up, down)
            owner = jnp.where((me_ref[0] >> bit) & 1 == 1, swapped, owner)
    owner_ref[...] = owner
    rows, pixsq = weight_ref.shape
    pix = int(round(pixsq**0.5))
    ch = unembed.shape[0] // pix
    groups = rows // (2 * GROUP)
    w3 = weight_ref[...].astype(F32).reshape(groups, 2, GROUP, pixsq)
    for level in range(2):
        w_l = w3[:, level].reshape(groups * GROUP, pixsq).astype(BF16)
        store_spread(mix_ref, spread(w_l, False, pix), 0, level * pix * GROUP, pix)
    for i in range(pix):
        lo, hi, move = tile_move(ch, i, unembed.shape[0])
        unembed_out[i * LANES : (i + 1) * LANES, :] = mm_tn(move, unembed[lo:hi, :]).astype(BF16)


def layer_norm(values, gain):
    average = jnp.mean(values, axis=-1, keepdims=True)
    centred = values - average
    spread_ = jnp.mean(centred * centred, axis=-1, keepdims=True)
    return centred * lax.rsqrt(spread_ + norm_eps) * gain


def head_mask(heads, span, d):
    head_of = iota((heads * span, d), 0) // span == iota((heads * span, d), 1) // (d // heads)
    return head_of.astype(F32).astype(BF16)


def softmax_parts(scores, side):
    out = []
    for m in range(scores.shape[1] // LANES):
        part = scores[:, m * LANES : (m + 1) * LANES]
        low = iota(part.shape, 1) % LANES < side
        top_lo = jnp.max(jnp.where(low, part, -3e38), axis=-1, keepdims=True)
        top_hi = jnp.max(jnp.where(low, -3e38, part), axis=-1, keepdims=True)
        out.append(jnp.exp(part - jnp.where(low, top_lo, top_hi)))
    return jnp.concatenate(out, axis=1)


def attend_rows(query, key, value, bias, heads, mask, blocked):
    d = query.shape[1]
    key_all = jnp.concatenate([key] * heads, axis=0) * mask
    value_all = jnp.concatenate([value] * heads, axis=0) * mask
    scores = mm_nt(query, key_all) * (d // heads) ** (-0.5) + bias
    if blocked is not None:
        scores = jnp.where(blocked, -1e30, scores)
    weights = softmax_parts(scores, key.shape[0]).astype(BF16)
    return mm(weights, value_all), weights


def feed_forward(residual, gain2, up, down):
    normed = layer_norm(residual, gain2).astype(BF16)
    hidden = jax.nn.gelu(mm(normed, up)).astype(BF16)
    return (residual + mm(hidden, down)).astype(BF16)


def lay_tiles(rows, count):
    return jnp.concatenate([rows[:, t * LANES : (t + 1) * LANES] for t in range(count)], axis=0)


def joined(chunks):
    pieces = [one()[...].astype(F32).reshape(-1, one.ref.shape[-1]) for one in chunks]
    return jnp.concatenate(pieces, axis=0).astype(BF16)


def stage_chunk(stage, direct, i):
    if not direct:
        return i + (0 if stage == 0 else NEAR)
    if stage == 0:
        return 2 * i
    return jnp.where(i < NEAR, 2 * i + 1, i + NEAR)


def regrid_part(stage, direct, data, x_ref, c_ref, mix, scatter, embed, pix):
    slots, width = data.shape
    ch = width // pix
    for j in range(pix):
        lo, hi, move = tile_move(ch, j, width)
        x_ref[:, j * LANES : (j + 1) * LANES] = mm(data[:, lo:hi], move)
    mix_ref = mix()
    size = mix_ref.shape[0] // (4 * NEAR)

    def group(g, carry):
        chunk = lax.div(g, size)
        where = stage_chunk(stage, direct, chunk) * size + g - chunk * size
        tiles = lay_tiles(x_ref[pl.ds(pl.multiple_of(g * GROUP, GROUP), GROUP), :], pix).astype(BF16)
        out = mm(mix_ref[where], tiles)
        to = pl.ds(pl.multiple_of(g * 2 * GROUP, 2 * GROUP), 2 * GROUP)
        for i in range(pix):
            low = out[i * GROUP : (i + 1) * GROUP]
            high = out[(pix + i) * GROUP : (pix + i + 1) * GROUP]
            both = jnp.concatenate([low, high], axis=0).astype(BF16)
            c_ref[to, i * LANES : (i + 1) * LANES] = both
        return carry

    lax.fori_loop(0, slots // GROUP, group, 0, unroll=4)
    scatter_ref, embed_ref = scatter(), embed()
    total = None
    for j in range(0, pix, 2):
        cols = slice(j * LANES, (j + 2) * LANES)
        pixels = mm(scatter_ref[...], c_ref[:, cols])
        term = mm(pixels.astype(BF16), embed_ref[cols, :])
        total = term if total is None else total + term
    return total


def early_kernel(pix, direct, loads, outs, scratch):
    *chunks, mix, scatter, embed = loads
    outs[0][...] = regrid_part(0, direct, joined(chunks), *scratch, mix, scatter, embed, pix)


def first_kernel(pix, direct, layer, loads, outs, scratch):
    *chunks, mix, scatter, embed, prior, gain1, gain2, qkv, bias, proj, up, down = loads
    total = regrid_part(1, direct, joined(chunks), *scratch, mix, scatter, embed, pix)
    state = (prior()[...] + total).astype(BF16).astype(F32)
    pd, d = state.shape
    heads = bias.ref.shape[1] // (WIN * WIN)
    normed = layer_norm(state, gain1()[layer : layer + 1, :]).astype(BF16)
    packed = mm(normed, qkv()[...]).astype(BF16)
    query, key, value = packed[:, :d], packed[:, d : 2 * d], packed[:, 2 * d :]
    half = pd // 2
    win_rows = ROWS // WIN
    part_rows = half // win_rows
    bias_all = bias()[...]
    mask = head_mask(heads, WIN * WIN, d)
    mixed = [None] * (2 * win_rows)
    weights = [None] * (2 * win_rows)
    for w in range(win_rows):
        def rows(v):
            lo, hi = w * part_rows, (w + 1) * part_rows
            return jnp.concatenate([v[lo:hi], v[half + lo : half + hi]], axis=0)

        out, wts = attend_rows(rows(query), rows(key), rows(value), bias_all, heads, mask, None)
        mixed[w], mixed[win_rows + w] = out[:part_rows], out[part_rows:]
        weights[w], weights[win_rows + w] = wts[:part_rows], wts[part_rows:]
    total = mm(jnp.concatenate(weights, axis=0), mask)
    mixed = (jnp.concatenate(mixed, axis=0) / total).astype(BF16)
    attended = mm(mixed, proj()[...]).astype(BF16)
    residual = state + attended.astype(F32)
    new = feed_forward(residual, gain2()[layer : layer + 1, :], up()[...], down()[...])
    outs[0][...] = new[:half]
    outs[1][...] = new[half:]


def turned(low, high):
    shift = low.shape[0] * (WIN // 2) // ROWS
    turn = lambda v: jnp.concatenate([v[shift:], v[:shift]], axis=0)
    return jnp.concatenate([turn(low[...]), turn(high[...])], axis=0).astype(F32)


def own_kernel(layer, loads, outs, scratch):
    low, high, gain1, qkv = loads
    normed = layer_norm(turned(low(), high()), gain1()[layer : layer + 1, :]).astype(BF16)
    outs[0][...] = mm(normed, qkv()[...]).astype(BF16)


def second_kernel(layer, loads, outs, scratch):
    packed, low, high, gain1, gain2, qkv, bias, left, right, proj, up, down, select = loads
    half, d = low.ref.shape
    heads = bias.ref.shape[1] // (WIN * WIN)
    shift = half * (WIN // 2) // ROWS
    back = lambda v: jnp.concatenate([v[half - shift :], v[: half - shift]], axis=0)
    own = turned(low(), high())
    gain = gain1()[layer : layer + 1, :]
    normed_s = layer_norm(turned(left(), right()), gain).astype(BF16)
    packed = packed()[...]
    packed_s = mm(normed_s, qkv()[:, d:]).astype(BF16)
    query, key, value = packed[:, :d], packed[:, d : 2 * d], packed[:, 2 * d :]
    key_s, value_s = packed_s[:, :d], packed_s[:, d:]
    win_rows = ROWS // WIN
    part = half // win_rows
    span = WIN * WIN
    bias_all = bias()[...]
    mask = head_mask(heads, span, d)
    outs_m, outs_w = [[], []], [[], []]
    for w in range(win_rows):
        near = slice(w * part, (w + 1) * part)
        far = slice(half + w * part, half + (w + 1) * part)
        for side in range(2):
            if side == 0:
                q = query[near]
                k = jnp.concatenate([key_s[near], key[near]], axis=0)
                v = jnp.concatenate([value_s[near], value[near]], axis=0)
                b = bias_all[part:]
            else:
                q = query[far]
                k = jnp.concatenate([key[far], key_s[far]], axis=0)
                v = jnp.concatenate([value[far], value_s[far]], axis=0)
                b = bias_all[:part]
            blocked = None
            if w == win_rows - 1:
                shape = (part, heads * span)
                q_up = iota(shape, 0) % part >= part // 2
                k_up = iota(shape, 1) % part >= part // 2
                blocked = q_up != k_up
            out, wts = attend_rows(q, k, v, b, heads, mask, blocked)
            outs_m[side].append(out)
            outs_w[side].append(wts)
    total = mm(jnp.concatenate(outs_w[0] + outs_w[1], axis=0), mask)
    mixed = (jnp.concatenate(outs_m[0] + outs_m[1], axis=0) / total).astype(BF16)
    attended = mm(mixed, proj()[...]).astype(BF16)
    residual = own + attended.astype(F32)
    new = feed_forward(residual, gain2()[layer : layer + 1, :], up()[...], down()[...])
    state = jnp.concatenate([back(new[:half]), back(new[half:])], axis=0)
    sent = mm(select()[...], state).astype(BF16)
    if len(outs) == 1:
        outs[0][...] = sent
        return
    rows = sent.shape[0] // (2 * len(outs))
    for x in range(2 * len(outs)):
        outs[x // 2][x % 2] = sent[x * rows : (x + 1) * rows]


def back_part(size, first, me_ref, chunks, mix, unembed, p_ref, slot_ref):
    rows = jnp.concatenate([one()[...].reshape(-1, one.ref.shape[-1]) for one in chunks], axis=0)
    unembed_ref = unembed()
    pix = unembed_ref.shape[0] // LANES
    for j in range(0, pix, 2):
        cols = slice(j * LANES, (j + 2) * LANES)
        p_ref[:, cols] = mm_nt(rows, unembed_ref[cols, :])
    mix_ref = mix()

    def group(g, carry):
        got = p_ref[pl.ds(pl.multiple_of(g * 2 * GROUP, 2 * GROUP), 2 * GROUP), :]
        data = jnp.concatenate([lay_tiles(got[:GROUP], pix), lay_tiles(got[GROUP:], pix)], axis=0)
        where = first + g
        if size is not None:
            chunk = lax.div(where, size)
            where = (chunk ^ me_ref[0]) * size + where - chunk * size
        out = mm(mix_ref[where], data.astype(BF16))
        to = pl.ds(pl.multiple_of(g * GROUP, GROUP), GROUP)
        for i in range(pix):
            slot_ref[to, i * LANES : (i + 1) * LANES] = out[i * GROUP : (i + 1) * GROUP]
        return carry

    lax.fori_loop(0, rows.shape[0] // (2 * GROUP), group, 0, unroll=4)


def back_kernel(size, first, me_ref, loads, outs, scratch):
    *chunks, unembed, mix = loads
    back_part(size, first, me_ref, chunks, mix, unembed, *scratch)
    outs[0][...] = scratch[1][...].astype(BF16)


def last_kernel(size, first, me_ref, loads, outs, scratch):
    *chunks, unembed, mix, prior, send = loads
    back_part(size, first, me_ref, chunks, mix, unembed, *scratch)
    slot_ref, out_ref = scratch[1], outs[0]
    pix = unembed.ref.shape[0] // LANES
    pd, total = out_ref.shape
    ch = total // pix
    prior_ref = prior()
    owner = send()
    onehot = (iota((pd, owner.shape[1]), 0) == owner[:1, :]).astype(F32).astype(BF16)
    tiles = [None] * (-(-total // LANES))
    for j in range(0, pix, 2):
        cols = slice(j * LANES, (j + 2) * LANES)
        slots = jnp.concatenate([prior_ref[:, cols], slot_ref[:, cols].astype(BF16)], axis=0)
        both = mm(onehot, slots)
        for jj in (j, j + 1):
            val = both[:, (jj - j) * LANES : (jj - j + 1) * LANES]
            t, off = divmod(ch * jj, LANES)
            if off:
                val = pltpu.roll(val, off, 1)
            lane = iota(val.shape, 1)
            low, high = jnp.where(lane >= off, val, 0.0), jnp.where(lane < off, val, 0.0)
            for tt, piece in ((t, low), (t + 1, high)):
                if tt == t + 1 and off + ch <= LANES:
                    continue
                tiles[tt] = piece if tiles[tt] is None else tiles[tt] + piece
    for t, tile in enumerate(tiles):
        hi = min((t + 1) * LANES, total)
        out_ref[:, t * LANES : hi] = tile[:, : hi - t * LANES]


def swap(value, axis):
    return lax.all_to_all(value, axis, split_axis=0, concat_axis=0, tiled=True)


def swap_pairs(value, axis):
    count = lax.axis_size(axis)
    rows, width = value.shape
    cap = rows // (2 * count)
    if cap % GROUP == 0:
        return swap(value, axis)
    groups = rows // (2 * GROUP)
    v = value.reshape(groups, 2, GROUP, width).transpose(1, 0, 2, 3).reshape(2, count, cap, width)
    v = swap(v.transpose(1, 0, 2, 3).reshape(rows, width), axis)
    v = v.reshape(count, 2, cap, width).transpose(1, 0, 2, 3).reshape(2, groups, GROUP, width)
    return v.transpose(1, 0, 2, 3).reshape(rows, width)


def flip(value, axis, bits):
    count = lax.axis_size(axis)
    return lax.ppermute(value, axis, [(source, source ^ bits) for source in range(count)])


def from_behind(value, axis, steps):
    count = lax.axis_size(axis)
    pairs = [(source, (source + steps) % count) for source in range(count)]
    return lax.ppermute(value, axis, pairs)


STAGES = 2
NEAR = 4


def body(
    bands, send_table, recv_table, regrid_weight, embed_weight, norm1_gain, qkv_weight, rel_bias,
    proj_weight, norm2_gain, up_weight, down_weight, unembed_weight,
):
    pd, width = bands.shape
    slots = send_table.shape[1]
    kk = recv_table.shape[0]
    d = embed_weight.shape[1]
    pixsq = regrid_weight.shape[1] // kk
    pix = int(round(pixsq**0.5))
    wide = pix * LANES
    count = lax.axis_size("tile")
    cap = slots // count
    chips = count // 2
    direct = chips == 2 * NEAR and cap % GROUP == 0
    vm = pltpu.VMEM
    per = slots // STAGES
    groups = per // GROUP
    my = lax.axis_index("tile").astype(jnp.int32).reshape(1)
    if not direct:
        my = my * 0

    if direct:
        turns = [*range(NEAR, chips), *range(NEAR - 1, 0, -1)]

        outgoing = call(pick_direct_kernel, [In(send_table), In(bands)],
                        [sds((2, cap, width), BF16)] * chips, [vm((count, cap, width), BF16)], my, flops=1e10)
        came = [outgoing[0]] + [None] * (chips - 1)
        for s in turns:
            came[s] = flip(outgoing[s], "tile", 2 * s)
    else:
        outgoing = call(pick_kernel, [In(send_table), In(bands)], [sds((slots, width), BF16)])
        incoming = swap(outgoing, "tile")

    heads = rel_bias.shape[1]
    span = WIN * WIN
    wsend = call(weights_kernel, [In(recv_table), In(regrid_weight)], [sds((2 * slots, pixsq), BF16)],
                 flops=1e10, after=[outgoing[0] if direct else outgoing])
    wback = swap_pairs(wsend, "tile")
    scatter_a, scatter_b, embed_pad, bias, select = call(
        functools.partial(tables_kernel, cap, direct),
        [In(recv_table), In(embed_weight), In(rel_bias.transpose(1, 0, 2))],
        [sds((pd, slots // 2), BF16), sds((pd, 3 * slots // 2), BF16), sds((wide, d), BF16),
         sds((rel_bias.shape[0], span, heads * span), F32), sds((2 * slots, pd), BF16)],
        [vm((heads, 2 * LANES), F32)], my, flops=2e9, after=[wsend])
    mix = call(functools.partial(mix_kernel, cap), [In(recv_table), In(regrid_weight)],
               [sds((slots // GROUP, 2 * pix * GROUP, pix * GROUP), BF16)], (), my, flops=2e9, after=[embed_pad])

    def relay(arrays, after=()):
        shape = (len(arrays), *arrays[0].shape[1:])
        return call(relay_kernel, [at(x, 1) for x in arrays], [sds(shape, BF16)], after=after)

    def regrid_scratch(rows):
        return [vm((rows, wide), F32), vm((2 * rows, wide), BF16)]

    if direct:
        near = [at(x, 0) for x in came[:NEAR]]
    else:
        near, far = [at(incoming, slice(0, slots // 4))], [at(incoming, slice(slots // 4, slots))]
    total = call(functools.partial(early_kernel, pix, direct),
                 [*near, In(mix), In(scatter_a), In(embed_pad)], [sds((pd, d), F32)],
                 regrid_scratch(slots // 4), flops=2e9)
    if direct:
        for_partner = relay(came, [total])
        passed = flip(for_partner, "tile", 1)
        far = [at(passed, i) for i in range(NEAR)]
        far += [y for i in range(NEAR, chips) for y in (at(came[i], 0), at(passed, i))]

    def layer(n):
        return [In(norm1_gain), In(norm2_gain), at(qkv_weight, n), at(bias, n)], [
            at(proj_weight, n), at(up_weight, n), at(down_weight, n)]

    half = pd // 2
    ins_a, ins_b = layer(0)
    low, high = call(
        functools.partial(first_kernel, pix, direct, 0),
        [*far, In(mix), In(scatter_b), In(embed_pad), In(total), *ins_a, *ins_b],
        [sds((half, d), BF16)] * 2, regrid_scratch(3 * slots // 4), flops=4e9)
    right = from_behind(low, "tile", -1)
    left = from_behind(high, "tile", 1)
    ins_a, ins_b = layer(1)
    packed = call(functools.partial(own_kernel, 1), [In(low), In(high), In(norm1_gain), at(qkv_weight, 1)],
                  [sds((pd, 3 * d), BF16)], flops=2e8)
    rows = 2 * cap
    sent = call(
        functools.partial(second_kernel, 1),
        [In(packed), In(low), In(high), *ins_a, In(left), In(right), *ins_b, In(select)],
        [sds((2, rows, d), BF16)] * chips if direct else [sds((2 * slots, d), BF16)], flops=2e9)
    one_sent = sent[0] if direct else sent
    size = cap // GROUP if direct else None
    mix_back, unembed_pad, owner = call(
        functools.partial(prep_back_kernel, size), [In(wback), In(unembed_weight.T), In(send_table)],
        [sds((slots // GROUP, pix * GROUP, 2 * pix * GROUP), BF16), sds((wide, d), BF16),
         sds((GROUP, slots), jnp.int32)], (), my, flops=2e9, after=[one_sent])

    back_scratch = [vm((2 * per, wide), F32), vm((per, wide), F32)]
    if direct:
        got = [sent[0]] + [None] * (chips - 1)
        for s in turns:
            got[s] = flip(sent[s], "tile", 2 * s)
        near_all = relay(got[:NEAR], [mix_back])
        near_pass = flip(near_all, "tile", 1)
        near = [y for i, x in enumerate(got[:NEAR]) for y in (at(x, 0), at(near_pass, i))]
    else:
        got = swap_pairs(sent, "tile").reshape(STAGES, 2 * per, d)
        near, far = [at(got, 0)], [at(got, 1)]
    prior = call(functools.partial(back_kernel, size, 0), [*near, In(unembed_pad), In(mix_back)],
                 [sds((per, wide), BF16)], back_scratch, my, flops=2e9)
    if direct:
        far_pass = flip(relay(got[NEAR:], [prior]), "tile", 1)
        far = [y for i, x in enumerate(got[NEAR:]) for y in (at(x, 0), at(far_pass, i))]
    return call(functools.partial(last_kernel, size, groups), [*far, In(unembed_pad), In(mix_back), In(prior), In(owner)],
                [sds((pd, width), F32)], back_scratch, my, flops=3e9)


def solution(mesh):
    in_specs = (
        P(("groups", "tile"), None), P("tile", None), P(None, "tile"), P("tile", None),
        P(), P(), P(), P(), P(), P(), P(), P(), P(),
    )
    out_specs = P(("groups", "tile"), None)
    return jax.shard_map(body, mesh=mesh, in_specs=in_specs, out_specs=out_specs, check_vma=False)
```

```python
import functools

import jax
import jax.numpy as jnp
import numpy as np
from jax import lax
from jax.experimental import pallas as pl
from jax.experimental.pallas import tpu as pltpu
from jax.sharding import PartitionSpec as P


WIN = 8
ROWS = 24
K = 4
LANES = 128
GROUP = 8

norm_eps = 1e-05
F32 = jnp.float32
BF16 = jnp.bfloat16


def iota(shape, axis):
    return lax.broadcasted_iota(jnp.int32, shape, axis)


def mm(a, b):
    return jnp.dot(a, b, preferred_element_type=F32)


def mm_tn(a, b):
    return lax.dot_general(a, b, (((0,), (0,)), ((), ())), preferred_element_type=F32)


def mm_nt(a, b):
    return lax.dot_general(a, b, (((1,), (1,)), ((), ())), preferred_element_type=F32)


VMEM_LIMIT = 16 << 20


class In:
    def __init__(self, array, index=None):
        self.array = array
        self.index = index


def at(array, index):
    return In(array, index)


class Loaded:
    def __init__(self, ref):
        self.ref = ref

    def __call__(self):
        return self.ref


def call(kernel, ins, outs, scratch=(), table=(), flops=0, after=()):
    def run(*refs):
        refs = list(refs)
        lead = [refs.pop(0) for _ in table]
        loads = []
        for one in ins:
            ref = refs.pop(0)
            loads.append(Loaded(ref if one.index is None else ref.at[one.index]))
        del refs[: len(after)]
        held = [refs.pop(0) for _ in outs]
        kernel(*lead, loads, held, refs)

    vmem = pl.BlockSpec(memory_space=pltpu.VMEM)
    in_specs = [pl.BlockSpec(memory_space=pltpu.SMEM)] * len(table)
    moved = sum(int(np.prod(s.array.shape)) * s.array.dtype.itemsize for s in ins)
    got = pl.pallas_call(
        run,
        out_shape=list(outs),
        in_specs=in_specs + [vmem] * len(ins) + [pl.BlockSpec(memory_space=pl.ANY)] * len(after),
        out_specs=[vmem] * len(outs),
        scratch_shapes=list(scratch),
        compiler_params=pltpu.CompilerParams(vmem_limit_bytes=VMEM_LIMIT),
        cost_estimate=pl.CostEstimate(flops=int(flops), bytes_accessed=moved, transcendentals=0),
    )(*table, *[one.array for one in ins], *after)
    return got if len(outs) > 1 else got[0]


def sds(shape, dtype):
    return jax.ShapeDtypeStruct(shape, dtype)


def chosen_rows(bands_ref, send_ref):
    rows, slots = bands_ref.shape[0], send_ref.shape[1]
    onehot = (iota((rows, slots), 0) == send_ref[...]).astype(F32).astype(BF16)
    return mm_tn(onehot, bands_ref[...])


def pick_kernel(loads, outs, scratch):
    send, bands = loads
    outs[0][...] = chosen_rows(bands(), send()).astype(BF16)


def pick_direct_kernel(my_ref, loads, outs, scratch):
    send, bands = loads
    held = scratch[0]
    held[...] = chosen_rows(bands(), send()).reshape(held.shape).astype(BF16)
    for s, out in enumerate(outs):
        for e in range(2):
            out[e] = held[my_ref[0] ^ (2 * s + e)]


def relay_kernel(loads, outs, scratch):
    for i, one in enumerate(loads):
        outs[0][i] = one()[...]


def spread(weights, fixed_first, pix):
    width = pix * GROUP
    shape = (pix * pix, pix * width)
    r, c = iota(shape, 0), iota(shape, 1)
    outer, inner = c // width, (c % width) // GROUP
    if fixed_first:
        sel = (r // pix == outer) & (r % pix == inner)
    else:
        sel = (r % pix == outer) & (r // pix == inner)
    out = mm(weights, sel.astype(F32).astype(BF16))
    own = iota(out.shape, 0) % GROUP == iota(out.shape, 1) % GROUP
    return jnp.where(own, out, 0.0)


def store_spread(out_ref, value, row0, col0, pix):
    groups = value.shape[0] // GROUP
    width = pix * GROUP
    for o in range(0, pix, 2):
        lo = value[:, o * width : (o + 1) * width].reshape(groups, GROUP, width)
        hi = value[:, (o + 1) * width : (o + 2) * width].reshape(groups, GROUP, width)
        both = jnp.concatenate([lo, hi], axis=1).astype(BF16)
        out_ref[:, row0 + o * GROUP : row0 + (o + 2) * GROUP, col0 : col0 + width] = both


def tile_move(ch, j, total):
    lo = (ch * j // LANES) * LANES
    hi = min(lo + 2 * LANES, total)
    shape = (hi - lo, LANES)
    move = (iota(shape, 0) - (ch * j - lo) == iota(shape, 1)) & (iota(shape, 1) < ch)
    return lo, hi, move.astype(F32).astype(BF16)


def weights_by_slot(recv, weight, slots, level, share=0, width=None):
    pixsq = weight.shape[1] // recv.shape[0]
    width = width or pixsq
    r = iota((slots, recv.shape[1]), 0)
    total = None
    for k in (2 * level, 2 * level + 1):
        hit = (recv[k : k + 1, :] == r).astype(F32).astype(BF16)
        first = k * pixsq if width == pixsq else pl.multiple_of(k * pixsq + share * width, LANES)
        term = mm(hit, weight[:, pl.ds(first, width)])
        total = term if total is None else total + term
    return total


def over(values, size):
    return jnp.floor((values.astype(F32) + 0.5) * (1.0 / size)).astype(jnp.int32)


def bias_rows(rel_ref, tab_ref, out_ref):
    heads, blocks, entries = rel_ref.shape
    span = WIN * WIN
    half = WIN // 2

    def row_col(pos):
        side = pos // (span // 2)
        return (pos % (span // 2)) // half, side * half + pos % half

    shape = (span, LANES)
    ra, ca = row_col(iota(shape, 0))
    rb, cb = row_col(iota(shape, 1) % span)
    index = (ra - rb + WIN - 1) * (2 * WIN - 1) + ca - cb + WIN - 1
    low = jnp.minimum(index, LANES - 1)
    high = jnp.maximum(index - LANES, 0)
    first = iota(shape, 1) < span
    for b in range(blocks):
        for h in range(heads):
            tab_ref[h : h + 1, :entries] = rel_ref[h, b : b + 1, :]
        for m in range(heads // 2):
            both = []
            for h in (2 * m, 2 * m + 1):
                lo = jnp.broadcast_to(tab_ref[h : h + 1, :LANES], shape)
                hi = jnp.broadcast_to(tab_ref[h : h + 1, LANES:], shape)
                got_lo = jnp.take_along_axis(lo, low, axis=1, mode="promise_in_bounds")
                got_hi = jnp.take_along_axis(hi, high, axis=1, mode="promise_in_bounds")
                both.append(jnp.where(index < LANES, got_lo, got_hi))
            out_ref[b, :, m * LANES : (m + 1) * LANES] = jnp.where(first, both[0], both[1])


def weights_kernel(group_ref, loads, outs, scratch):
    recv, weight = (one() for one in loads)
    slots = 2 * recv.shape[1]
    width = outs[0].shape[1]
    totals = [weights_by_slot(recv, weight, slots, v, group_ref[0], width) for v in range(2)]
    totals = [t.reshape(slots // GROUP, GROUP, width) for t in totals]
    outs[0][...] = jnp.concatenate(totals, axis=1).reshape(2 * slots, width).astype(BF16)


def split_slots(recv, cap, me):
    slot = recv[...]
    sender = over(slot, cap)
    inner = slot - sender * cap
    return sender ^ me, inner


def patch_turn(pd):
    half = WIN // 2
    r, c = iota((pd, pd), 0), iota((pd, pd), 1)
    side, rest = r // (ROWS * half), r % (ROWS * half)
    return ((rest // half) * WIN + side * half + rest % half == c).astype(F32).astype(BF16)


def chosen(shape, axis, vals, chunk_of=None, size=1):
    r = iota(shape, axis)
    if chunk_of is not None:
        chunk = over(r, size)
        r = chunk_of(chunk) * size + r - chunk * size
    slot = (r // (2 * GROUP)) * GROUP + r % GROUP
    level = (r // GROUP) % 2
    first = (vals(0) == slot) | (vals(1) == slot)
    second = (vals(2) == slot) | (vals(3) == slot)
    hit = (first & (level == 0)) | (second & (level == 1))
    return hit.astype(F32).astype(BF16)


def tables_kernel(cap, direct, me_ref, loads, outs, scratch):
    recv, embed, rel = (one() for one in loads)
    *scatter_refs, embed_out, bias_ref, select_ref, digits_ref = outs
    pd = recv.shape[1]
    slots = 2 * pd
    pix = embed_out.shape[0] // LANES
    ch = embed.shape[0] // pix
    turn = patch_turn(pd)
    parts = [v.astype(F32).astype(BF16) for v in split_slots(recv, cap, me_ref[0])]
    cols = (mm_nt(turn, parts[0]) * cap + mm_nt(turn, parts[1])).astype(jnp.int32)
    digits = [mm_nt(v, turn) for v in parts]
    rows = (digits[0] * cap + digits[1]).astype(jnp.int32)
    select_ref[...] = chosen(select_ref.shape, 0, lambda k: rows[k : k + 1, :])
    digits_ref[...] = jnp.zeros_like(digits_ref)
    digits_ref[:, :pd] = jnp.concatenate(digits, axis=0).astype(BF16)
    for stage, ref in enumerate(scatter_refs):
        ref[...] = chosen(ref.shape, 1, lambda k: cols[:, k : k + 1],
                          functools.partial(stage_chunk, stage, direct), 2 * slots // (4 * NEAR))
    for i in range(pix):
        lo, hi, move = tile_move(ch, i, embed.shape[0])
        embed_out[i * LANES : (i + 1) * LANES, :] = mm_tn(move, embed[lo:hi, :]).astype(BF16)
    bias_rows(rel, scratch[0], bias_ref)


def mix_kernel(cap, me_ref, loads, outs, scratch):
    recv, weight = (one() for one in loads)
    slots = 2 * recv.shape[1]
    pix = int(round((weight.shape[1] // recv.shape[0]) ** 0.5))
    sender, inner = split_slots(recv, cap, me_ref[0])
    for level in range(2):
        total = weights_by_slot(sender * cap + inner, weight, slots, level)
        store_spread(outs[0], spread(total.astype(BF16), True, pix), level * pix * GROUP, 0, pix)


def prep_back_kernel(size, me_ref, group_ref, loads, outs, scratch):
    *weight, unembed, send = loads
    unembed = unembed()
    mix_ref, unembed_out, owner_ref = outs
    owner = jnp.broadcast_to(send()[...], (GROUP, send.ref.shape[1]))
    if size is not None:
        cap = size * GROUP
        count = owner.shape[1] // cap
        chunk = over(iota(owner.shape, 1), cap)
        for bit in range(count.bit_length() - 1):
            gap = cap << bit
            up = pltpu.roll(owner, owner.shape[1] - gap, 1)
            down = pltpu.roll(owner, gap, 1)
            swapped = jnp.where((chunk >> bit) & 1 == 0, up, down)
            owner = jnp.where((me_ref[0] >> bit) & 1 == 1, swapped, owner)
    owner_ref[...] = owner
    if len(weight) == 2:
        mine, other = (one()[...].astype(F32) for one in weight)
        first = group_ref[0] == 0
        both = [jnp.where(first, mine, other), jnp.where(first, other, mine)]
        weights = jnp.concatenate(both, axis=1)
    else:
        weights = weight[0]()[...].astype(F32)
    rows, pixsq = weights.shape
    pix = int(round(pixsq**0.5))
    ch = unembed.shape[0] // pix
    groups = rows // (2 * GROUP)
    w3 = weights.reshape(groups, 2, GROUP, pixsq)
    for level in range(2):
        w_l = w3[:, level].reshape(groups * GROUP, pixsq).astype(BF16)
        store_spread(mix_ref, spread(w_l, False, pix), 0, level * pix * GROUP, pix)
    for i in range(pix):
        lo, hi, move = tile_move(ch, i, unembed.shape[0])
        unembed_out[i * LANES : (i + 1) * LANES, :] = mm_tn(move, unembed[lo:hi, :]).astype(BF16)


def layer_norm(values, gain):
    average = jnp.mean(values, axis=-1, keepdims=True)
    centred = values - average
    spread_ = jnp.mean(centred * centred, axis=-1, keepdims=True)
    return centred * lax.rsqrt(spread_ + norm_eps) * gain


def head_mask(heads, span, d):
    head_of = iota((heads * span, d), 0) // span == iota((heads * span, d), 1) // (d // heads)
    return head_of.astype(F32).astype(BF16)


def softmax_parts(scores, side):
    out = []
    for m in range(scores.shape[1] // LANES):
        part = scores[:, m * LANES : (m + 1) * LANES]
        low = iota(part.shape, 1) % LANES < side
        top_lo = jnp.max(jnp.where(low, part, -3e38), axis=-1, keepdims=True)
        top_hi = jnp.max(jnp.where(low, -3e38, part), axis=-1, keepdims=True)
        out.append(jnp.exp(part - jnp.where(low, top_lo, top_hi)))
    return jnp.concatenate(out, axis=1)


def attend_rows(query, key, value, bias, heads, mask, blocked):
    d = query.shape[1]
    key_all = jnp.concatenate([key] * heads, axis=0) * mask
    value_all = jnp.concatenate([value] * heads, axis=0) * mask
    scores = mm_nt(query, key_all) * (d // heads) ** (-0.5) + bias
    if blocked is not None:
        scores = jnp.where(blocked, -1e30, scores)
    weights = softmax_parts(scores, key.shape[0]).astype(BF16)
    return mm(weights, value_all), weights


def feed_forward(residual, gain2, up, down):
    normed = layer_norm(residual, gain2).astype(BF16)
    hidden = jax.nn.gelu(mm(normed, up)).astype(BF16)
    return (residual + mm(hidden, down)).astype(BF16)


def lay_tiles(rows, count):
    return jnp.concatenate([rows[:, t * LANES : (t + 1) * LANES] for t in range(count)], axis=0)


def joined(chunks):
    pieces = [one()[...].astype(F32).reshape(-1, one.ref.shape[-1]) for one in chunks]
    return jnp.concatenate(pieces, axis=0).astype(BF16)


def stage_chunk(stage, direct, i):
    if not direct:
        return i + (0 if stage == 0 else NEAR)
    if stage == 0:
        return 2 * i
    return jnp.where(i < NEAR, 2 * i + 1, i + NEAR)


def regrid_part(stage, direct, data, x_ref, c_ref, mix, scatter, embed, pix):
    slots, width = data.shape
    ch = width // pix
    for j in range(pix):
        lo, hi, move = tile_move(ch, j, width)
        x_ref[:, j * LANES : (j + 1) * LANES] = mm(data[:, lo:hi], move)
    mix_ref = mix()
    size = mix_ref.shape[0] // (4 * NEAR)

    def group(g, carry):
        chunk = lax.div(g, size)
        where = stage_chunk(stage, direct, chunk) * size + g - chunk * size
        tiles = lay_tiles(x_ref[pl.ds(pl.multiple_of(g * GROUP, GROUP), GROUP), :], pix).astype(BF16)
        out = mm(mix_ref[where], tiles)
        to = pl.ds(pl.multiple_of(g * 2 * GROUP, 2 * GROUP), 2 * GROUP)
        for i in range(pix):
            low = out[i * GROUP : (i + 1) * GROUP]
            high = out[(pix + i) * GROUP : (pix + i + 1) * GROUP]
            both = jnp.concatenate([low, high], axis=0).astype(BF16)
            c_ref[to, i * LANES : (i + 1) * LANES] = both
        return carry

    lax.fori_loop(0, slots // GROUP, group, 0, unroll=4)
    scatter_ref, embed_ref = scatter(), embed()
    total = None
    for j in range(0, pix, 2):
        cols = slice(j * LANES, (j + 2) * LANES)
        pixels = mm(scatter_ref[...], c_ref[:, cols])
        term = mm(pixels.astype(BF16), embed_ref[cols, :])
        total = term if total is None else total + term
    return total


def early_kernel(pix, direct, loads, outs, scratch):
    *chunks, mix, scatter, embed = loads
    if direct:
        for i, one in enumerate(chunks):
            outs[1][i] = one()[1]
        chunks = [Loaded(one.ref.at[0]) for one in chunks]
    outs[0][...] = regrid_part(0, direct, joined(chunks), *scratch, mix, scatter, embed, pix)


def first_kernel(pix, direct, layer, loads, outs, scratch):
    *chunks, mix, scatter, embed, prior, gain1, gain2, qkv, bias, proj, up, down = loads
    total = regrid_part(1, direct, joined(chunks), *scratch, mix, scatter, embed, pix)
    state = (prior()[...] + total).astype(BF16).astype(F32)
    pd, d = state.shape
    heads = bias.ref.shape[1] // (WIN * WIN)
    normed = layer_norm(state, gain1()[layer : layer + 1, :]).astype(BF16)
    packed = mm(normed, qkv()[...]).astype(BF16)
    query, key, value = packed[:, :d], packed[:, d : 2 * d], packed[:, 2 * d :]
    half = pd // 2
    win_rows = ROWS // WIN
    part_rows = half // win_rows
    bias_all = bias()[...]
    mask = head_mask(heads, WIN * WIN, d)
    mixed = [None] * (2 * win_rows)
    weights = [None] * (2 * win_rows)
    for w in range(win_rows):
        def rows(v):
            lo, hi = w * part_rows, (w + 1) * part_rows
            return jnp.concatenate([v[lo:hi], v[half + lo : half + hi]], axis=0)

        out, wts = attend_rows(rows(query), rows(key), rows(value), bias_all, heads, mask, None)
        mixed[w], mixed[win_rows + w] = out[:part_rows], out[part_rows:]
        weights[w], weights[win_rows + w] = wts[:part_rows], wts[part_rows:]
    total = mm(jnp.concatenate(weights, axis=0), mask)
    mixed = (jnp.concatenate(mixed, axis=0) / total).astype(BF16)
    attended = mm(mixed, proj()[...]).astype(BF16)
    residual = state + attended.astype(F32)
    new = feed_forward(residual, gain2()[layer : layer + 1, :], up()[...], down()[...])
    outs[0][...] = new[:half]
    outs[1][...] = new[half:]


def turned(low, high):
    shift = low.shape[0] * (WIN // 2) // ROWS
    turn = lambda v: jnp.concatenate([v[shift:], v[:shift]], axis=0)
    return jnp.concatenate([turn(low[...]), turn(high[...])], axis=0).astype(F32)


def own_kernel(layer, loads, outs, scratch):
    low, high, gain1, qkv = loads
    normed = layer_norm(turned(low(), high()), gain1()[layer : layer + 1, :]).astype(BF16)
    outs[0][...] = mm(normed, qkv()[...]).astype(BF16)


def put_chunks(sent, chips):
    rows = sent.shape[0] // (2 * len(chips))
    for x in range(2 * len(chips)):
        chips[x // 2][x % 2] = sent[x * rows : (x + 1) * rows]


def pass_on_kernel(cap, loads, outs, scratch):
    state = loads[0]()
    kk = K
    pd = state.shape[0] - 2 * kk
    digits = state[pd:, :pd].astype(F32)
    slot = (digits[:kk] * cap + digits[kk:]).astype(jnp.int32)
    rows = 2 * cap
    select = chosen((2 * NEAR * rows, pd), 0, lambda k: slot[k : k + 1, :], lambda c: c + 2 * NEAR, rows)
    put_chunks(mm(select, state[:pd, :]).astype(BF16), outs)


def second_kernel(layer, loads, outs, scratch):
    packed, low, high, gain1, gain2, qkv, bias, left, right, proj, up, down, select, digits = loads
    half, d = low.ref.shape
    heads = bias.ref.shape[1] // (WIN * WIN)
    shift = half * (WIN // 2) // ROWS
    back = lambda v: jnp.concatenate([v[half - shift :], v[: half - shift]], axis=0)
    own = turned(low(), high())
    gain = gain1()[layer : layer + 1, :]
    normed_s = layer_norm(turned(left(), right()), gain).astype(BF16)
    packed = packed()[...]
    packed_s = mm(normed_s, qkv()[:, d:]).astype(BF16)
    query, key, value = packed[:, :d], packed[:, d : 2 * d], packed[:, 2 * d :]
    key_s, value_s = packed_s[:, :d], packed_s[:, d:]
    win_rows = ROWS // WIN
    part = half // win_rows
    span = WIN * WIN
    bias_all = bias()[...]
    mask = head_mask(heads, span, d)
    outs_m, outs_w = [[], []], [[], []]
    for w in range(win_rows):
        near = slice(w * part, (w + 1) * part)
        far = slice(half + w * part, half + (w + 1) * part)
        for side in range(2):
            if side == 0:
                q = query[near]
                k = jnp.concatenate([key_s[near], key[near]], axis=0)
                v = jnp.concatenate([value_s[near], value[near]], axis=0)
                b = bias_all[part:]
            else:
                q = query[far]
                k = jnp.concatenate([key[far], key_s[far]], axis=0)
                v = jnp.concatenate([value[far], value_s[far]], axis=0)
                b = bias_all[:part]
            blocked = None
            if w == win_rows - 1:
                shape = (part, heads * span)
                q_up = iota(shape, 0) % part >= part // 2
                k_up = iota(shape, 1) % part >= part // 2
                blocked = q_up != k_up
            out, wts = attend_rows(q, k, v, b, heads, mask, blocked)
            outs_m[side].append(out)
            outs_w[side].append(wts)
    total = mm(jnp.concatenate(outs_w[0] + outs_w[1], axis=0), mask)
    mixed = (jnp.concatenate(outs_m[0] + outs_m[1], axis=0) / total).astype(BF16)
    attended = mm(mixed, proj()[...]).astype(BF16)
    residual = own + attended.astype(F32)
    new = feed_forward(residual, gain2()[layer : layer + 1, :], up()[...], down()[...])
    state = jnp.concatenate([back(new[:half]), back(new[half:])], axis=0)
    sent = mm(select()[...], state).astype(BF16)
    if len(outs) == 1:
        outs[0][...] = sent
        return
    *chips, mirror = outs
    put_chunks(sent, chips)
    mirror[: 2 * half, :] = state
    mirror[2 * half :, :] = digits()[...]


def back_part(size, first, me_ref, chunks, mix, unembed, p_ref, slot_ref):
    rows = jnp.concatenate([one()[...].reshape(-1, one.ref.shape[-1]) for one in chunks], axis=0)
    unembed_ref = unembed()
    pix = unembed_ref.shape[0] // LANES
    for j in range(0, pix, 2):
        cols = slice(j * LANES, (j + 2) * LANES)
        p_ref[:, cols] = mm_nt(rows, unembed_ref[cols, :])
    mix_ref = mix()

    def group(g, carry):
        got = p_ref[pl.ds(pl.multiple_of(g * 2 * GROUP, 2 * GROUP), 2 * GROUP), :]
        data = jnp.concatenate([lay_tiles(got[:GROUP], pix), lay_tiles(got[GROUP:], pix)], axis=0)
        where = first + g
        if size is not None:
            chunk = lax.div(where, size)
            where = (chunk ^ me_ref[0]) * size + where - chunk * size
        out = mm(mix_ref[where], data.astype(BF16))
        to = pl.ds(pl.multiple_of(g * GROUP, GROUP), GROUP)
        for i in range(pix):
            slot_ref[to, i * LANES : (i + 1) * LANES] = out[i * GROUP : (i + 1) * GROUP]
        return carry

    lax.fori_loop(0, rows.shape[0] // (2 * GROUP), group, 0, unroll=4)


def back_kernel(size, first, me_ref, loads, outs, scratch):
    *chunks, unembed, mix = loads
    back_part(size, first, me_ref, chunks, mix, unembed, *scratch)
    outs[0][...] = scratch[1][...].astype(BF16)


def last_kernel(size, first, me_ref, loads, outs, scratch):
    *chunks, unembed, mix, prior, send = loads
    back_part(size, first, me_ref, chunks, mix, unembed, *scratch)
    slot_ref, out_ref = scratch[1], outs[0]
    pix = unembed.ref.shape[0] // LANES
    pd, total = out_ref.shape
    ch = total // pix
    prior_ref = prior()
    owner = send()
    onehot = (iota((pd, owner.shape[1]), 0) == owner[:1, :]).astype(F32).astype(BF16)
    tiles = [None] * (-(-total // LANES))
    for j in range(0, pix, 2):
        cols = slice(j * LANES, (j + 2) * LANES)
        slots = jnp.concatenate([prior_ref[:, cols], slot_ref[:, cols].astype(BF16)], axis=0)
        both = mm(onehot, slots)
        for jj in (j, j + 1):
            val = both[:, (jj - j) * LANES : (jj - j + 1) * LANES]
            t, off = divmod(ch * jj, LANES)
            if off:
                val = pltpu.roll(val, off, 1)
            lane = iota(val.shape, 1)
            low, high = jnp.where(lane >= off, val, 0.0), jnp.where(lane < off, val, 0.0)
            for tt, piece in ((t, low), (t + 1, high)):
                if tt == t + 1 and off + ch <= LANES:
                    continue
                tiles[tt] = piece if tiles[tt] is None else tiles[tt] + piece
    for t, tile in enumerate(tiles):
        hi = min((t + 1) * LANES, total)
        out_ref[:, t * LANES : hi] = tile[:, : hi - t * LANES]


def swap(value, axis):
    return lax.all_to_all(value, axis, split_axis=0, concat_axis=0, tiled=True)


def swap_pairs(value, axis):
    count = lax.axis_size(axis)
    rows, width = value.shape
    cap = rows // (2 * count)
    if cap % GROUP == 0:
        return swap(value, axis)
    groups = rows // (2 * GROUP)
    v = value.reshape(groups, 2, GROUP, width).transpose(1, 0, 2, 3).reshape(2, count, cap, width)
    v = swap(v.transpose(1, 0, 2, 3).reshape(rows, width), axis)
    v = v.reshape(count, 2, cap, width).transpose(1, 0, 2, 3).reshape(2, groups, GROUP, width)
    return v.transpose(1, 0, 2, 3).reshape(rows, width)


def flip(value, axis, bits):
    count = lax.axis_size(axis)
    return lax.ppermute(value, axis, [(source, source ^ bits) for source in range(count)])


def from_behind(value, axis, steps):
    count = lax.axis_size(axis)
    pairs = [(source, (source + steps) % count) for source in range(count)]
    return lax.ppermute(value, axis, pairs)


STAGES = 2
NEAR = 4


def body(
    bands, send_table, recv_table, regrid_weight, embed_weight, norm1_gain, qkv_weight, rel_bias,
    proj_weight, norm2_gain, up_weight, down_weight, unembed_weight,
):
    pd, width = bands.shape
    slots = send_table.shape[1]
    kk = recv_table.shape[0]
    d = embed_weight.shape[1]
    pixsq = regrid_weight.shape[1] // kk
    pix = int(round(pixsq**0.5))
    wide = pix * LANES
    count = lax.axis_size("tile")
    cap = slots // count
    chips = count // 2
    direct = chips == 2 * NEAR and cap % GROUP == 0
    vm = pltpu.VMEM
    per = slots // STAGES
    groups = per // GROUP
    my = lax.axis_index("tile").astype(jnp.int32).reshape(1)
    if not direct:
        my = my * 0

    if direct:
        turns = [*range(NEAR, chips), *range(NEAR - 1, 0, -1)]

        outgoing = call(pick_direct_kernel, [In(send_table), In(bands)],
                        [sds((2, cap, width), BF16)] * chips, [vm((count, cap, width), BF16)], [my], flops=1e+09)
        came = [outgoing[0]] + [None] * (chips - 1)
        for s in turns:
            came[s] = flip(outgoing[s], "tile", 2 * s)
    else:
        outgoing = call(pick_kernel, [In(send_table), In(bands)], [sds((slots, width), BF16)])
        incoming = swap(outgoing, "tile")

    heads = rel_bias.shape[1]
    span = WIN * WIN
    shared = lax.axis_size("groups") == 2 and pixsq % (2 * LANES) == 0
    group = lax.axis_index("groups").astype(jnp.int32).reshape(1)
    wsend = call(weights_kernel, [In(recv_table), In(regrid_weight)],
                 [sds((2 * slots, pixsq // 2 if shared else pixsq), BF16)], (), [group],
                 flops=1e+09, after=[outgoing[0] if direct else outgoing])
    wback = swap_pairs(wsend, "tile")
    scatter_a, scatter_b, embed_pad, bias, select, digits = call(
        functools.partial(tables_kernel, cap, direct),
        [In(recv_table), In(embed_weight), In(rel_bias.transpose(1, 0, 2))],
        [sds((pd, slots // 2), BF16), sds((pd, 3 * slots // 2), BF16), sds((wide, d), BF16),
         sds((rel_bias.shape[0], span, heads * span), F32), sds((slots if direct else 2 * slots, pd), BF16),
         sds((2 * kk, d), BF16)],
        [vm((heads, 2 * LANES), F32)], [my], flops=2e+08, after=[wsend])
    mix = call(functools.partial(mix_kernel, cap), [In(recv_table), In(regrid_weight)],
               [sds((slots // GROUP, 2 * pix * GROUP, pix * GROUP), BF16)], (), [my], flops=2e+08, after=[embed_pad])

    def relay(arrays, after=()):
        shape = (len(arrays), *arrays[0].shape[1:])
        return call(relay_kernel, [at(x, 1) for x in arrays], [sds(shape, BF16)], after=after)

    def regrid_scratch(rows):
        return [vm((rows, wide), F32), vm((2 * rows, wide), BF16)]

    if direct:
        near = [In(x) for x in came[:NEAR]]
    else:
        near, far = [at(incoming, slice(0, slots // 4))], [at(incoming, slice(slots // 4, slots))]
    total = call(functools.partial(early_kernel, pix, direct),
                 [*near, In(mix), In(scatter_a), In(embed_pad)],
                 [sds((pd, d), F32)] + [sds((NEAR, cap, width), BF16)] * direct,
                 regrid_scratch(slots // 4), flops=2e+08)
    if direct:
        total, near_pass = total
        for_partner = call(relay_kernel, [*[at(near_pass, i) for i in range(NEAR)], *[at(x, 1) for x in came[NEAR:]]],
                           [sds((chips, cap, width), BF16)])
        passed = flip(for_partner, "tile", 1)
        far = [at(passed, i) for i in range(NEAR)]
        far += [y for i in range(NEAR, chips) for y in (at(came[i], 0), at(passed, i))]

    def layer(n):
        return [In(norm1_gain), In(norm2_gain), at(qkv_weight, n), at(bias, n)], [
            at(proj_weight, n), at(up_weight, n), at(down_weight, n)]

    half = pd // 2
    ins_a, ins_b = layer(0)
    low, high = call(
        functools.partial(first_kernel, pix, direct, 0),
        [*far, In(mix), In(scatter_b), In(embed_pad), In(total), *ins_a, *ins_b],
        [sds((half, d), BF16)] * 2, regrid_scratch(3 * slots // 4), flops=4e+08)
    right = from_behind(low, "tile", -1)
    left = from_behind(high, "tile", 1)
    wbacks = [wback]
    if shared:
        wbacks.append(flip(wback, "groups", 1))
    ins_a, ins_b = layer(1)
    packed = call(functools.partial(own_kernel, 1), [In(low), In(high), In(norm1_gain), at(qkv_weight, 1)],
                  [sds((pd, 3 * d), BF16)], flops=2e+07)
    rows = 2 * cap
    sent = call(
        functools.partial(second_kernel, 1),
        [In(packed), In(low), In(high), *ins_a, In(left), In(right), *ins_b, In(select), In(digits)],
        [sds((2, rows, d), BF16)] * NEAR + [sds((pd + 2 * kk, d), BF16)] if direct else [sds((2 * slots, d), BF16)], flops=2e+08)
    one_sent = sent[0] if direct else sent
    size = cap // GROUP if direct else None
    mix_back, unembed_pad, owner = call(
        functools.partial(prep_back_kernel, size), [*[In(w) for w in wbacks], In(unembed_weight.T), In(send_table)],
        [sds((slots // GROUP, pix * GROUP, 2 * pix * GROUP), BF16), sds((wide, d), BF16),
         sds((GROUP, slots), jnp.int32)], (), [my, group], flops=2e+08, after=[one_sent])

    back_scratch = [vm((2 * per, wide), F32), vm((per, wide), F32)]
    if direct:
        *sent, mirror = sent
        mirror = flip(mirror, "tile", 2 * NEAR)
        got = [sent[0]] + [flip(sent[s], "tile", 2 * s) for s in range(1, NEAR)]
        passed = call(functools.partial(pass_on_kernel, cap), [In(mirror)],
                      [sds((2, rows, d), BF16)] * NEAR, flops=3e+07)
        got += [passed[0]] + [flip(passed[s], "tile", 2 * s) for s in range(1, NEAR)]
        near_all = relay(got[:NEAR], [mix_back])
        near_pass = flip(near_all, "tile", 1)
        near = [y for i, x in enumerate(got[:NEAR]) for y in (at(x, 0), at(near_pass, i))]
    else:
        got = swap_pairs(sent, "tile").reshape(STAGES, 2 * per, d)
        near, far = [at(got, 0)], [at(got, 1)]
    prior = call(functools.partial(back_kernel, size, 0), [*near, In(unembed_pad), In(mix_back)],
                 [sds((per, wide), BF16)], back_scratch, [my], flops=2e+08)
    if direct:
        far_pass = flip(relay(got[NEAR:], [prior]), "tile", 1)
        far = [y for i, x in enumerate(got[NEAR:]) for y in (at(x, 0), at(far_pass, i))]
    return call(functools.partial(last_kernel, size, groups), [*far, In(unembed_pad), In(mix_back), In(prior), In(owner)],
                [sds((pd, width), F32)], back_scratch, [my], flops=3e+08)


def solution(mesh):
    in_specs = (
        P(("groups", "tile"), None), P("tile", None), P(None, "tile"), P("tile", None),
        P(), P(), P(), P(), P(), P(), P(), P(), P(),
    )
    out_specs = P(("groups", "tile"), None)
    return jax.shard_map(body, mesh=mesh, in_specs=in_specs, out_specs=out_specs, check_vma=False)
```

```python
import functools

import jax
import jax.numpy as jnp
import numpy as np
from jax import lax
from jax.experimental import pallas as pl
from jax.experimental.pallas import tpu as pltpu
from jax.sharding import PartitionSpec as P


WIN = 8
ROWS = 24
LANES = 128
GROUP = 8

norm_eps = 1e-05
F32 = jnp.float32
BF16 = jnp.bfloat16


def iota(shape, axis):
    return lax.broadcasted_iota(jnp.int32, shape, axis)


def mm(a, b):
    return jnp.dot(a, b, preferred_element_type=F32)


def mm_tn(a, b):
    return lax.dot_general(a, b, (((0,), (0,)), ((), ())), preferred_element_type=F32)


def mm_nt(a, b):
    return lax.dot_general(a, b, (((1,), (1,)), ((), ())), preferred_element_type=F32)


VMEM_LIMIT = 16 << 20


class In:
    def __init__(self, array, index=None):
        self.array = array
        self.index = index


def at(array, index):
    return In(array, index)


class Loaded:
    def __init__(self, ref):
        self.ref = ref

    def __call__(self):
        return self.ref


def call(kernel, ins, outs, scratch=(), table=None, flops=0, after=()):
    def run(*refs):
        refs = list(refs)
        lead = [refs.pop(0)] if table is not None else []
        loads = []
        for one in ins:
            ref = refs.pop(0)
            loads.append(Loaded(ref if one.index is None else ref.at[one.index]))
        del refs[: len(after)]
        held = [refs.pop(0) for _ in outs]
        kernel(*lead, loads, held, refs)

    vmem = pl.BlockSpec(memory_space=pltpu.VMEM)
    in_specs = [] if table is None else [pl.BlockSpec(memory_space=pltpu.SMEM)]
    moved = sum(int(np.prod(s.array.shape)) * s.array.dtype.itemsize for s in ins)
    got = pl.pallas_call(
        run,
        out_shape=list(outs),
        in_specs=in_specs + [vmem] * len(ins) + [pl.BlockSpec(memory_space=pl.ANY)] * len(after),
        out_specs=[vmem] * len(outs),
        scratch_shapes=list(scratch),
        compiler_params=pltpu.CompilerParams(vmem_limit_bytes=VMEM_LIMIT),
        cost_estimate=pl.CostEstimate(flops=int(flops), bytes_accessed=moved, transcendentals=0),
    )(*([] if table is None else [table]), *[one.array for one in ins], *after)
    return got if len(outs) > 1 else got[0]


def sds(shape, dtype):
    return jax.ShapeDtypeStruct(shape, dtype)


def chosen_rows(bands_ref, send_ref):
    rows, slots = bands_ref.shape[0], send_ref.shape[1]
    onehot = (iota((rows, slots), 0) == send_ref[...]).astype(F32).astype(BF16)
    return mm_tn(onehot, bands_ref[...])


def pick_kernel(loads, outs, scratch):
    send, bands = loads
    outs[0][...] = chosen_rows(bands(), send()).astype(BF16)


def pick_direct_kernel(my_ref, loads, outs, scratch):
    send, bands = loads
    held = scratch[0]
    held[...] = chosen_rows(bands(), send()).reshape(held.shape).astype(BF16)
    for s, out in enumerate(outs):
        for e in range(2):
            out[e] = held[my_ref[0] ^ (2 * s + e)]


def relay_kernel(loads, outs, scratch):
    for i, one in enumerate(loads):
        outs[0][i] = one()[...]


def spread(weights, fixed_first, pix):
    width = pix * GROUP
    shape = (pix * pix, pix * width)
    r, c = iota(shape, 0), iota(shape, 1)
    outer, inner = c // width, (c % width) // GROUP
    if fixed_first:
        sel = (r // pix == outer) & (r % pix == inner)
    else:
        sel = (r % pix == outer) & (r // pix == inner)
    out = mm(weights, sel.astype(F32).astype(BF16))
    own = iota(out.shape, 0) % GROUP == iota(out.shape, 1) % GROUP
    return jnp.where(own, out, 0.0)


def store_spread(out_ref, value, row0, col0, pix):
    groups = value.shape[0] // GROUP
    width = pix * GROUP
    for o in range(0, pix, 2):
        lo = value[:, o * width : (o + 1) * width].reshape(groups, GROUP, width)
        hi = value[:, (o + 1) * width : (o + 2) * width].reshape(groups, GROUP, width)
        both = jnp.concatenate([lo, hi], axis=1).astype(BF16)
        out_ref[:, row0 + o * GROUP : row0 + (o + 2) * GROUP, col0 : col0 + width] = both


def tile_move(ch, j, total):
    lo = (ch * j // LANES) * LANES
    hi = min(lo + 2 * LANES, total)
    shape = (hi - lo, LANES)
    move = (iota(shape, 0) - (ch * j - lo) == iota(shape, 1)) & (iota(shape, 1) < ch)
    return lo, hi, move.astype(F32).astype(BF16)


def weights_by_slot(recv, weight, slots, level):
    pixsq = weight.shape[1] // recv.shape[0]
    r = iota((slots, recv.shape[1]), 0)
    total = None
    for k in (2 * level, 2 * level + 1):
        hit = (recv[k : k + 1, :] == r).astype(F32).astype(BF16)
        term = mm(hit, weight[:, k * pixsq : (k + 1) * pixsq])
        total = term if total is None else total + term
    return total


def over(values, size):
    return jnp.floor((values.astype(F32) + 0.5) * (1.0 / size)).astype(jnp.int32)


def bias_rows(rel_ref, tab_ref, out_ref):
    heads, blocks, entries = rel_ref.shape
    span = WIN * WIN
    half = WIN // 2

    def row_col(pos):
        side = pos // (span // 2)
        return (pos % (span // 2)) // half, side * half + pos % half

    shape = (span, LANES)
    ra, ca = row_col(iota(shape, 0))
    rb, cb = row_col(iota(shape, 1) % span)
    index = (ra - rb + WIN - 1) * (2 * WIN - 1) + ca - cb + WIN - 1
    low = jnp.minimum(index, LANES - 1)
    high = jnp.maximum(index - LANES, 0)
    first = iota(shape, 1) < span
    for b in range(blocks):
        for h in range(heads):
            tab_ref[h : h + 1, :entries] = rel_ref[h, b : b + 1, :]
        for m in range(heads // 2):
            both = []
            for h in (2 * m, 2 * m + 1):
                lo = jnp.broadcast_to(tab_ref[h : h + 1, :LANES], shape)
                hi = jnp.broadcast_to(tab_ref[h : h + 1, LANES:], shape)
                got_lo = jnp.take_along_axis(lo, low, axis=1, mode="promise_in_bounds")
                got_hi = jnp.take_along_axis(hi, high, axis=1, mode="promise_in_bounds")
                both.append(jnp.where(index < LANES, got_lo, got_hi))
            out_ref[b, :, m * LANES : (m + 1) * LANES] = jnp.where(first, both[0], both[1])


def weights_kernel(loads, outs, scratch):
    recv, weight = (one() for one in loads)
    slots = 2 * recv.shape[1]
    pixsq = weight.shape[1] // recv.shape[0]
    totals = [weights_by_slot(recv, weight, slots, v).reshape(slots // GROUP, GROUP, pixsq) for v in range(2)]
    outs[0][...] = jnp.concatenate(totals, axis=1).reshape(2 * slots, pixsq).astype(BF16)


def split_slots(recv, cap, me):
    slot = recv[...]
    sender = over(slot, cap)
    inner = slot - sender * cap
    return sender ^ me, inner


def patch_turn(pd):
    half = WIN // 2
    r, c = iota((pd, pd), 0), iota((pd, pd), 1)
    side, rest = r // (ROWS * half), r % (ROWS * half)
    return ((rest // half) * WIN + side * half + rest % half == c).astype(F32).astype(BF16)


def chosen(shape, axis, vals, chunk_of=None, size=1):
    r = iota(shape, axis)
    if chunk_of is not None:
        chunk = over(r, size)
        r = chunk_of(chunk) * size + r - chunk * size
    slot = (r // (2 * GROUP)) * GROUP + r % GROUP
    level = (r // GROUP) % 2
    first = (vals(0) == slot) | (vals(1) == slot)
    second = (vals(2) == slot) | (vals(3) == slot)
    hit = (first & (level == 0)) | (second & (level == 1))
    return hit.astype(F32).astype(BF16)


def tables_kernel(cap, direct, me_ref, loads, outs, scratch):
    recv, embed, rel = (one() for one in loads)
    *scatter_refs, embed_out, bias_ref, select_ref = outs
    pd = recv.shape[1]
    slots = 2 * pd
    pix = embed_out.shape[0] // LANES
    ch = embed.shape[0] // pix
    turn = patch_turn(pd)
    parts = [v.astype(F32).astype(BF16) for v in split_slots(recv, cap, me_ref[0])]
    cols = (mm_nt(turn, parts[0]) * cap + mm_nt(turn, parts[1])).astype(jnp.int32)
    rows = (mm_nt(parts[0], turn) * cap + mm_nt(parts[1], turn)).astype(jnp.int32)
    select_ref[...] = chosen((2 * slots, pd), 0, lambda k: rows[k : k + 1, :])
    for stage, ref in enumerate(scatter_refs):
        ref[...] = chosen(ref.shape, 1, lambda k: cols[:, k : k + 1],
                          functools.partial(stage_chunk, stage, direct), 2 * slots // (4 * NEAR))
    for i in range(pix):
        lo, hi, move = tile_move(ch, i, embed.shape[0])
        embed_out[i * LANES : (i + 1) * LANES, :] = mm_tn(move, embed[lo:hi, :]).astype(BF16)
    bias_rows(rel, scratch[0], bias_ref)


def mix_kernel(cap, me_ref, loads, outs, scratch):
    recv, weight = (one() for one in loads)
    slots = 2 * recv.shape[1]
    pix = int(round((weight.shape[1] // recv.shape[0]) ** 0.5))
    sender, inner = split_slots(recv, cap, me_ref[0])
    for level in range(2):
        total = weights_by_slot(sender * cap + inner, weight, slots, level)
        store_spread(outs[0], spread(total.astype(BF16), True, pix), level * pix * GROUP, 0, pix)


def prep_back_kernel(size, me_ref, loads, outs, scratch):
    weight, unembed, send = loads
    weight_ref, unembed = weight(), unembed()
    mix_ref, unembed_out, owner_ref = outs
    owner = jnp.broadcast_to(send()[...], (GROUP, send.ref.shape[1]))
    if size is not None:
        cap = size * GROUP
        count = owner.shape[1] // cap
        chunk = over(iota(owner.shape, 1), cap)
        for bit in range(count.bit_length() - 1):
            gap = cap << bit
            up = pltpu.roll(owner, owner.shape[1] - gap, 1)
            down = pltpu.roll(owner, gap, 1)
            swapped = jnp.where((chunk >> bit) & 1 == 0, up, down)
            owner = jnp.where((me_ref[0] >> bit) & 1 == 1, swapped, owner)
    owner_ref[...] = owner
    rows, pixsq = weight_ref.shape
    pix = int(round(pixsq**0.5))
    ch = unembed.shape[0] // pix
    groups = rows // (2 * GROUP)
    w3 = weight_ref[...].astype(F32).reshape(groups, 2, GROUP, pixsq)
    for level in range(2):
        w_l = w3[:, level].reshape(groups * GROUP, pixsq).astype(BF16)
        store_spread(mix_ref, spread(w_l, False, pix), 0, level * pix * GROUP, pix)
    for i in range(pix):
        lo, hi, move = tile_move(ch, i, unembed.shape[0])
        unembed_out[i * LANES : (i + 1) * LANES, :] = mm_tn(move, unembed[lo:hi, :]).astype(BF16)


def layer_norm(values, gain):
    average = jnp.mean(values, axis=-1, keepdims=True)
    centred = values - average
    spread_ = jnp.mean(centred * centred, axis=-1, keepdims=True)
    return centred * lax.rsqrt(spread_ + norm_eps) * gain


def head_mask(heads, span, d):
    size = d // heads
    shape = (LANES // size * span, LANES)
    return (iota(shape, 0) // span == iota(shape, 1) // size).astype(F32).astype(BF16)


def by_group(weights, values):
    rows = values[0].shape[0]
    parts = [mm(weights[:, g * rows : (g + 1) * rows], v) for g, v in enumerate(values)]
    return jnp.concatenate(parts, axis=1)


def softmax_parts(scores, side):
    out = []
    for m in range(scores.shape[1] // LANES):
        part = scores[:, m * LANES : (m + 1) * LANES]
        low = iota(part.shape, 1) % LANES < side
        top_lo = jnp.max(jnp.where(low, part, -3e38), axis=-1, keepdims=True)
        top_hi = jnp.max(jnp.where(low, -3e38, part), axis=-1, keepdims=True)
        out.append(jnp.exp(part - jnp.where(low, top_lo, top_hi)))
    return jnp.concatenate(out, axis=1)


def attend_rows(query, key, value, bias, heads, mask, blocked):
    d = query.shape[1]
    times = mask.shape[0] // key.shape[0]
    scores, values = [], []
    for g in range(d // LANES):
        lanes = slice(g * LANES, (g + 1) * LANES)
        expand = lambda v: jnp.concatenate([v[:, lanes]] * times, axis=0) * mask
        scores.append(mm_nt(query[:, lanes], expand(key)))
        values.append(expand(value))
    scores = jnp.concatenate(scores, axis=1) * (d // heads) ** (-0.5) + bias
    if blocked is not None:
        scores = jnp.where(blocked, -1e30, scores)
    weights = softmax_parts(scores, key.shape[0]).astype(BF16)
    return by_group(weights, values), weights


def feed_forward(residual, gain2, up, down):
    normed = layer_norm(residual, gain2).astype(BF16)
    hidden = jax.nn.gelu(mm(normed, up)).astype(BF16)
    return (residual + mm(hidden, down)).astype(BF16)


def lay_tiles(rows, count):
    return jnp.concatenate([rows[:, t * LANES : (t + 1) * LANES] for t in range(count)], axis=0)


def joined(chunks):
    pieces = [one()[...].astype(F32).reshape(-1, one.ref.shape[-1]) for one in chunks]
    return jnp.concatenate(pieces, axis=0).astype(BF16)


def stage_chunk(stage, direct, i):
    if not direct:
        return i + (0 if stage == 0 else NEAR)
    if stage == 0:
        return 2 * i
    return jnp.where(i < NEAR, 2 * i + 1, i + NEAR)


def regrid_part(stage, direct, data, x_ref, c_ref, mix, scatter, embed, pix):
    slots, width = data.shape
    ch = width // pix
    for j in range(pix):
        lo, hi, move = tile_move(ch, j, width)
        x_ref[:, j * LANES : (j + 1) * LANES] = mm(data[:, lo:hi], move)
    mix_ref = mix()
    size = mix_ref.shape[0] // (4 * NEAR)

    def group(g, carry):
        chunk = lax.div(g, size)
        where = stage_chunk(stage, direct, chunk) * size + g - chunk * size
        tiles = lay_tiles(x_ref[pl.ds(pl.multiple_of(g * GROUP, GROUP), GROUP), :], pix).astype(BF16)
        out = mm(mix_ref[where], tiles)
        to = pl.ds(pl.multiple_of(g * 2 * GROUP, 2 * GROUP), 2 * GROUP)
        for i in range(pix):
            low = out[i * GROUP : (i + 1) * GROUP]
            high = out[(pix + i) * GROUP : (pix + i + 1) * GROUP]
            both = jnp.concatenate([low, high], axis=0).astype(BF16)
            c_ref[to, i * LANES : (i + 1) * LANES] = both
        return carry

    lax.fori_loop(0, slots // GROUP, group, 0, unroll=4)
    scatter_ref, embed_ref = scatter(), embed()
    total = None
    for j in range(0, pix, 2):
        cols = slice(j * LANES, (j + 2) * LANES)
        pixels = mm(scatter_ref[...], c_ref[:, cols])
        term = mm(pixels.astype(BF16), embed_ref[cols, :])
        total = term if total is None else total + term
    return total


def early_kernel(pix, direct, loads, outs, scratch):
    *chunks, mix, scatter, embed = loads
    outs[0][...] = regrid_part(0, direct, joined(chunks), *scratch, mix, scatter, embed, pix)


def first_kernel(pix, direct, layer, loads, outs, scratch):
    *chunks, mix, scatter, embed, prior, gain1, gain2, qkv, bias, proj, up, down = loads
    total = regrid_part(1, direct, joined(chunks), *scratch, mix, scatter, embed, pix)
    state = (prior()[...] + total).astype(BF16).astype(F32)
    pd, d = state.shape
    heads = bias.ref.shape[1] // (WIN * WIN)
    normed = layer_norm(state, gain1()[layer : layer + 1, :]).astype(BF16)
    packed = mm(normed, qkv()[...]).astype(BF16)
    query, key, value = packed[:, :d], packed[:, d : 2 * d], packed[:, 2 * d :]
    half = pd // 2
    win_rows = ROWS // WIN
    part_rows = half // win_rows
    bias_all = bias()[...]
    mask = head_mask(heads, WIN * WIN, d)
    mixed = [None] * (2 * win_rows)
    weights = [None] * (2 * win_rows)
    for w in range(win_rows):
        def rows(v):
            lo, hi = w * part_rows, (w + 1) * part_rows
            return jnp.concatenate([v[lo:hi], v[half + lo : half + hi]], axis=0)

        out, wts = attend_rows(rows(query), rows(key), rows(value), bias_all, heads, mask, None)
        mixed[w], mixed[win_rows + w] = out[:part_rows], out[part_rows:]
        weights[w], weights[win_rows + w] = wts[:part_rows], wts[part_rows:]
    total = by_group(jnp.concatenate(weights, axis=0), [mask] * (d // LANES))
    mixed = (jnp.concatenate(mixed, axis=0) / total).astype(BF16)
    attended = mm(mixed, proj()[...]).astype(BF16)
    residual = state + attended.astype(F32)
    new = feed_forward(residual, gain2()[layer : layer + 1, :], up()[...], down()[...])
    outs[0][...] = new[:half]
    outs[1][...] = new[half:]


def turned(low, high):
    shift = low.shape[0] * (WIN // 2) // ROWS
    turn = lambda v: jnp.concatenate([v[shift:], v[:shift]], axis=0)
    return jnp.concatenate([turn(low[...]), turn(high[...])], axis=0).astype(F32)


def own_kernel(layer, loads, outs, scratch):
    low, high, gain1, qkv = loads
    normed = layer_norm(turned(low(), high()), gain1()[layer : layer + 1, :]).astype(BF16)
    outs[0][...] = mm(normed, qkv()[...]).astype(BF16)


def second_kernel(layer, loads, outs, scratch):
    packed, low, high, gain1, gain2, qkv, bias, left, right, proj, up, down, select = loads
    half, d = low.ref.shape
    heads = bias.ref.shape[1] // (WIN * WIN)
    shift = half * (WIN // 2) // ROWS
    back = lambda v: jnp.concatenate([v[half - shift :], v[: half - shift]], axis=0)
    own = turned(low(), high())
    gain = gain1()[layer : layer + 1, :]
    normed_s = layer_norm(turned(left(), right()), gain).astype(BF16)
    packed = packed()[...]
    packed_s = mm(normed_s, qkv()[:, d:]).astype(BF16)
    query, key, value = packed[:, :d], packed[:, d : 2 * d], packed[:, 2 * d :]
    key_s, value_s = packed_s[:, :d], packed_s[:, d:]
    win_rows = ROWS // WIN
    part = half // win_rows
    span = WIN * WIN
    bias_all = bias()[...]
    mask = head_mask(heads, span, d)
    outs_m, outs_w = [[], []], [[], []]
    for w in range(win_rows):
        near = slice(w * part, (w + 1) * part)
        far = slice(half + w * part, half + (w + 1) * part)
        for side in range(2):
            if side == 0:
                q = query[near]
                k = jnp.concatenate([key_s[near], key[near]], axis=0)
                v = jnp.concatenate([value_s[near], value[near]], axis=0)
                b = bias_all[part:]
            else:
                q = query[far]
                k = jnp.concatenate([key[far], key_s[far]], axis=0)
                v = jnp.concatenate([value[far], value_s[far]], axis=0)
                b = bias_all[:part]
            blocked = None
            if w == win_rows - 1:
                shape = (part, heads * span)
                q_up = iota(shape, 0) % part >= part // 2
                k_up = iota(shape, 1) % part >= part // 2
                blocked = q_up != k_up
            out, wts = attend_rows(q, k, v, b, heads, mask, blocked)
            outs_m[side].append(out)
            outs_w[side].append(wts)
    total = by_group(jnp.concatenate(outs_w[0] + outs_w[1], axis=0), [mask] * (d // LANES))
    mixed = (jnp.concatenate(outs_m[0] + outs_m[1], axis=0) / total).astype(BF16)
    attended = mm(mixed, proj()[...]).astype(BF16)
    residual = own + attended.astype(F32)
    new = feed_forward(residual, gain2()[layer : layer + 1, :], up()[...], down()[...])
    state = jnp.concatenate([back(new[:half]), back(new[half:])], axis=0)
    sent = mm(select()[...], state).astype(BF16)
    if len(outs) == 1:
        outs[0][...] = sent
        return
    rows = sent.shape[0] // (2 * len(outs))
    for x in range(2 * len(outs)):
        outs[x // 2][x % 2] = sent[x * rows : (x + 1) * rows]


def back_part(size, first, me_ref, chunks, mix, unembed, p_ref, slot_ref):
    rows = jnp.concatenate([one()[...].reshape(-1, one.ref.shape[-1]) for one in chunks], axis=0)
    unembed_ref = unembed()
    pix = unembed_ref.shape[0] // LANES
    for j in range(0, pix, 2):
        cols = slice(j * LANES, (j + 2) * LANES)
        p_ref[:, cols] = mm_nt(rows, unembed_ref[cols, :])
    mix_ref = mix()

    def group(g, carry):
        got = p_ref[pl.ds(pl.multiple_of(g * 2 * GROUP, 2 * GROUP), 2 * GROUP), :]
        data = jnp.concatenate([lay_tiles(got[:GROUP], pix), lay_tiles(got[GROUP:], pix)], axis=0)
        where = first + g
        if size is not None:
            chunk = lax.div(where, size)
            where = (chunk ^ me_ref[0]) * size + where - chunk * size
        out = mm(mix_ref[where], data.astype(BF16))
        to = pl.ds(pl.multiple_of(g * GROUP, GROUP), GROUP)
        for i in range(pix):
            slot_ref[to, i * LANES : (i + 1) * LANES] = out[i * GROUP : (i + 1) * GROUP]
        return carry

    lax.fori_loop(0, rows.shape[0] // (2 * GROUP), group, 0, unroll=4)


def back_kernel(size, first, me_ref, loads, outs, scratch):
    *chunks, unembed, mix = loads
    back_part(size, first, me_ref, chunks, mix, unembed, *scratch)
    outs[0][...] = scratch[1][...].astype(BF16)


def last_kernel(size, first, me_ref, loads, outs, scratch):
    *chunks, unembed, mix, prior, send = loads
    back_part(size, first, me_ref, chunks, mix, unembed, *scratch)
    slot_ref, out_ref = scratch[1], outs[0]
    pix = unembed.ref.shape[0] // LANES
    pd, total = out_ref.shape
    ch = total // pix
    prior_ref = prior()
    owner = send()
    onehot = (iota((pd, owner.shape[1]), 0) == owner[:1, :]).astype(F32).astype(BF16)
    tiles = [None] * (-(-total // LANES))
    for j in range(0, pix, 2):
        cols = slice(j * LANES, (j + 2) * LANES)
        slots = jnp.concatenate([prior_ref[:, cols], slot_ref[:, cols].astype(BF16)], axis=0)
        both = mm(onehot, slots)
        for jj in (j, j + 1):
            val = both[:, (jj - j) * LANES : (jj - j + 1) * LANES]
            t, off = divmod(ch * jj, LANES)
            if off:
                val = pltpu.roll(val, off, 1)
            lane = iota(val.shape, 1)
            low, high = jnp.where(lane >= off, val, 0.0), jnp.where(lane < off, val, 0.0)
            for tt, piece in ((t, low), (t + 1, high)):
                if tt == t + 1 and off + ch <= LANES:
                    continue
                tiles[tt] = piece if tiles[tt] is None else tiles[tt] + piece
    for t, tile in enumerate(tiles):
        hi = min((t + 1) * LANES, total)
        out_ref[:, t * LANES : hi] = tile[:, : hi - t * LANES]


def swap(value, axis):
    return lax.all_to_all(value, axis, split_axis=0, concat_axis=0, tiled=True)


def swap_pairs(value, axis):
    count = lax.axis_size(axis)
    rows, width = value.shape
    cap = rows // (2 * count)
    if cap % GROUP == 0:
        return swap(value, axis)
    groups = rows // (2 * GROUP)
    v = value.reshape(groups, 2, GROUP, width).transpose(1, 0, 2, 3).reshape(2, count, cap, width)
    v = swap(v.transpose(1, 0, 2, 3).reshape(rows, width), axis)
    v = v.reshape(count, 2, cap, width).transpose(1, 0, 2, 3).reshape(2, groups, GROUP, width)
    return v.transpose(1, 0, 2, 3).reshape(rows, width)


def flip(value, axis, bits):
    count = lax.axis_size(axis)
    return lax.ppermute(value, axis, [(source, source ^ bits) for source in range(count)])


def from_behind(value, axis, steps):
    count = lax.axis_size(axis)
    pairs = [(source, (source + steps) % count) for source in range(count)]
    return lax.ppermute(value, axis, pairs)


STAGES = 2
NEAR = 4


def body(
    bands, send_table, recv_table, regrid_weight, embed_weight, norm1_gain, qkv_weight, rel_bias,
    proj_weight, norm2_gain, up_weight, down_weight, unembed_weight,
):
    pd, width = bands.shape
    slots = send_table.shape[1]
    kk = recv_table.shape[0]
    d = embed_weight.shape[1]
    pixsq = regrid_weight.shape[1] // kk
    pix = int(round(pixsq**0.5))
    wide = pix * LANES
    count = lax.axis_size("tile")
    cap = slots // count
    chips = count // 2
    direct = chips == 2 * NEAR and cap % GROUP == 0
    vm = pltpu.VMEM
    per = slots // STAGES
    groups = per // GROUP
    my = lax.axis_index("tile").astype(jnp.int32).reshape(1)
    if not direct:
        my = my * 0

    if direct:
        turns = [*range(NEAR, chips), *range(NEAR - 1, 0, -1)]

        outgoing = call(pick_direct_kernel, [In(send_table), In(bands)],
                        [sds((2, cap, width), BF16)] * chips, [vm((count, cap, width), BF16)], my, flops=1e10)
        came = [outgoing[0]] + [None] * (chips - 1)
        for s in turns:
            came[s] = flip(outgoing[s], "tile", 2 * s)
    else:
        outgoing = call(pick_kernel, [In(send_table), In(bands)], [sds((slots, width), BF16)])
        incoming = swap(outgoing, "tile")

    heads = rel_bias.shape[1]
    span = WIN * WIN
    wsend = call(weights_kernel, [In(recv_table), In(regrid_weight)], [sds((2 * slots, pixsq), BF16)],
                 flops=1e10, after=[outgoing[0] if direct else outgoing])
    wback = swap_pairs(wsend, "tile")
    scatter_a, scatter_b, embed_pad, bias, select = call(
        functools.partial(tables_kernel, cap, direct),
        [In(recv_table), In(embed_weight), In(rel_bias.transpose(1, 0, 2))],
        [sds((pd, slots // 2), BF16), sds((pd, 3 * slots // 2), BF16), sds((wide, d), BF16),
         sds((rel_bias.shape[0], span, heads * span), F32), sds((2 * slots, pd), BF16)],
        [vm((heads, 2 * LANES), F32)], my, flops=2e9, after=[wsend])
    mix = call(functools.partial(mix_kernel, cap), [In(recv_table), In(regrid_weight)],
               [sds((slots // GROUP, 2 * pix * GROUP, pix * GROUP), BF16)], (), my, flops=2e9, after=[embed_pad])

    def relay(arrays, after=()):
        shape = (len(arrays), *arrays[0].shape[1:])
        return call(relay_kernel, [at(x, 1) for x in arrays], [sds(shape, BF16)], after=after)

    def regrid_scratch(rows):
        return [vm((rows, wide), F32), vm((2 * rows, wide), BF16)]

    if direct:
        near = [at(x, 0) for x in came[:NEAR]]
    else:
        near, far = [at(incoming, slice(0, slots // 4))], [at(incoming, slice(slots // 4, slots))]
    total = call(functools.partial(early_kernel, pix, direct),
                 [*near, In(mix), In(scatter_a), In(embed_pad)], [sds((pd, d), F32)],
                 regrid_scratch(slots // 4), flops=2e9)
    if direct:
        for_partner = relay(came, [total])
        passed = flip(for_partner, "tile", 1)
        far = [at(passed, i) for i in range(NEAR)]
        far += [y for i in range(NEAR, chips) for y in (at(came[i], 0), at(passed, i))]

    def layer(n):
        return [In(norm1_gain), In(norm2_gain), at(qkv_weight, n), at(bias, n)], [
            at(proj_weight, n), at(up_weight, n), at(down_weight, n)]

    half = pd // 2
    ins_a, ins_b = layer(0)
    low, high = call(
        functools.partial(first_kernel, pix, direct, 0),
        [*far, In(mix), In(scatter_b), In(embed_pad), In(total), *ins_a, *ins_b],
        [sds((half, d), BF16)] * 2, regrid_scratch(3 * slots // 4), flops=4e9)
    right = from_behind(low, "tile", -1)
    left = from_behind(high, "tile", 1)
    ins_a, ins_b = layer(1)
    packed = call(functools.partial(own_kernel, 1), [In(low), In(high), In(norm1_gain), at(qkv_weight, 1)],
                  [sds((pd, 3 * d), BF16)], flops=2e8)
    rows = 2 * cap
    sent = call(
        functools.partial(second_kernel, 1),
        [In(packed), In(low), In(high), *ins_a, In(left), In(right), *ins_b, In(select)],
        [sds((2, rows, d), BF16)] * chips if direct else [sds((2 * slots, d), BF16)], flops=2e9)
    one_sent = sent[0] if direct else sent
    size = cap // GROUP if direct else None
    mix_back, unembed_pad, owner = call(
        functools.partial(prep_back_kernel, size), [In(wback), In(unembed_weight.T), In(send_table)],
        [sds((slots // GROUP, pix * GROUP, 2 * pix * GROUP), BF16), sds((wide, d), BF16),
         sds((GROUP, slots), jnp.int32)], (), my, flops=2e9, after=[one_sent])

    back_scratch = [vm((2 * per, wide), F32), vm((per, wide), F32)]
    if direct:
        got = [sent[0]] + [None] * (chips - 1)
        for s in turns:
            got[s] = flip(sent[s], "tile", 2 * s)
        near_all = relay(got[:NEAR], [mix_back])
        near_pass = flip(near_all, "tile", 1)
        near = [y for i, x in enumerate(got[:NEAR]) for y in (at(x, 0), at(near_pass, i))]
    else:
        got = swap_pairs(sent, "tile").reshape(STAGES, 2 * per, d)
        near, far = [at(got, 0)], [at(got, 1)]
    prior = call(functools.partial(back_kernel, size, 0), [*near, In(unembed_pad), In(mix_back)],
                 [sds((per, wide), BF16)], back_scratch, my, flops=2e9)
    if direct:
        far_pass = flip(relay(got[NEAR:], [prior]), "tile", 1)
        far = [y for i, x in enumerate(got[NEAR:]) for y in (at(x, 0), at(far_pass, i))]
    return call(functools.partial(last_kernel, size, groups), [*far, In(unembed_pad), In(mix_back), In(prior), In(owner)],
                [sds((pd, width), F32)], back_scratch, my, flops=3e9)


def solution(mesh):
    in_specs = (
        P(("groups", "tile"), None), P("tile", None), P(None, "tile"), P("tile", None),
        P(), P(), P(), P(), P(), P(), P(), P(), P(),
    )
    out_specs = P(("groups", "tile"), None)
    return jax.shard_map(body, mesh=mesh, in_specs=in_specs, out_specs=out_specs, check_vma=False)
```

```python
import functools

import jax
import jax.numpy as jnp
import numpy as np
from jax import lax
from jax.experimental import pallas as pl
from jax.experimental.pallas import tpu as pltpu
from jax.sharding import PartitionSpec as P


WIN = 8
ROWS = 24
LANES = 128
GROUP = 8

norm_eps = 1e-05
F32 = jnp.float32
BF16 = jnp.bfloat16


def iota(shape, axis):
    return lax.broadcasted_iota(jnp.int32, shape, axis)


def mm(a, b):
    return jnp.dot(a, b, preferred_element_type=F32)


def mm_tn(a, b):
    return lax.dot_general(a, b, (((0,), (0,)), ((), ())), preferred_element_type=F32)


def mm_nt(a, b):
    return lax.dot_general(a, b, (((1,), (1,)), ((), ())), preferred_element_type=F32)


VMEM_LIMIT = 16 << 20


class In:
    def __init__(self, array, index=None):
        self.array = array
        self.index = index


def at(array, index):
    return In(array, index)


class Loaded:
    def __init__(self, ref):
        self.ref = ref

    def __call__(self):
        return self.ref


def call(kernel, ins, outs, scratch=(), table=None, flops=0, after=()):
    def run(*refs):
        refs = list(refs)
        lead = [refs.pop(0)] if table is not None else []
        loads = []
        for one in ins:
            ref = refs.pop(0)
            loads.append(Loaded(ref if one.index is None else ref.at[one.index]))
        del refs[: len(after)]
        held = [refs.pop(0) for _ in outs]
        kernel(*lead, loads, held, refs)

    vmem = pl.BlockSpec(memory_space=pltpu.VMEM)
    in_specs = [] if table is None else [pl.BlockSpec(memory_space=pltpu.SMEM)]
    moved = sum(int(np.prod(s.array.shape)) * s.array.dtype.itemsize for s in ins)
    got = pl.pallas_call(
        run,
        out_shape=list(outs),
        in_specs=in_specs + [vmem] * len(ins) + [pl.BlockSpec(memory_space=pl.ANY)] * len(after),
        out_specs=[vmem] * len(outs),
        scratch_shapes=list(scratch),
        compiler_params=pltpu.CompilerParams(vmem_limit_bytes=VMEM_LIMIT),
        cost_estimate=pl.CostEstimate(flops=int(flops), bytes_accessed=moved, transcendentals=0),
    )(*([] if table is None else [table]), *[one.array for one in ins], *after)
    return got if len(outs) > 1 else got[0]


def sds(shape, dtype):
    return jax.ShapeDtypeStruct(shape, dtype)


def chosen_rows(bands_ref, send_ref):
    rows, slots = bands_ref.shape[0], send_ref.shape[1]
    onehot = (iota((rows, slots), 0) == send_ref[...]).astype(F32).astype(BF16)
    return mm_tn(onehot, bands_ref[...])


def pick_kernel(loads, outs, scratch):
    send, bands = loads
    outs[0][...] = chosen_rows(bands(), send()).astype(BF16)


def pick_direct_kernel(my_ref, loads, outs, scratch):
    send, bands = loads
    held = scratch[0]
    held[...] = chosen_rows(bands(), send()).reshape(held.shape).astype(BF16)
    for s, out in enumerate(outs):
        for e in range(2):
            out[e] = held[my_ref[0] ^ (2 * s + e)]


def relay_kernel(loads, outs, scratch):
    for i, one in enumerate(loads):
        outs[0][i] = one()[...]


def spread(weights, fixed_first, pix):
    width = pix * GROUP
    shape = (pix * pix, pix * width)
    r, c = iota(shape, 0), iota(shape, 1)
    outer, inner = c // width, (c % width) // GROUP
    if fixed_first:
        sel = (r // pix == outer) & (r % pix == inner)
    else:
        sel = (r % pix == outer) & (r // pix == inner)
    out = mm(weights, sel.astype(F32).astype(BF16))
    own = iota(out.shape, 0) % GROUP == iota(out.shape, 1) % GROUP
    return jnp.where(own, out, 0.0)


def store_spread(out_ref, value, row0, col0, pix):
    groups = value.shape[0] // GROUP
    width = pix * GROUP
    for o in range(0, pix, 2):
        lo = value[:, o * width : (o + 1) * width].reshape(groups, GROUP, width)
        hi = value[:, (o + 1) * width : (o + 2) * width].reshape(groups, GROUP, width)
        both = jnp.concatenate([lo, hi], axis=1).astype(BF16)
        out_ref[:, row0 + o * GROUP : row0 + (o + 2) * GROUP, col0 : col0 + width] = both


def tile_move(ch, j, total):
    lo = (ch * j // LANES) * LANES
    hi = min(lo + 2 * LANES, total)
    shape = (hi - lo, LANES)
    move = (iota(shape, 0) - (ch * j - lo) == iota(shape, 1)) & (iota(shape, 1) < ch)
    return lo, hi, move.astype(F32).astype(BF16)


def weights_by_slot(recv, weight, slots, level):
    pixsq = weight.shape[1] // recv.shape[0]
    r = iota((slots, recv.shape[1]), 0)
    total = None
    for k in (2 * level, 2 * level + 1):
        hit = (recv[k : k + 1, :] == r).astype(F32).astype(BF16)
        term = mm(hit, weight[:, k * pixsq : (k + 1) * pixsq])
        total = term if total is None else total + term
    return total


def over(values, size):
    return jnp.floor((values.astype(F32) + 0.5) * (1.0 / size)).astype(jnp.int32)


def bias_rows(rel_ref, tab_ref, out_ref):
    heads, blocks, entries = rel_ref.shape
    span = WIN * WIN
    half = WIN // 2

    def row_col(pos):
        side = pos // (span // 2)
        return (pos % (span // 2)) // half, side * half + pos % half

    shape = (span, LANES)
    ra, ca = row_col(iota(shape, 0))
    rb, cb = row_col(iota(shape, 1) % span)
    index = (ra - rb + WIN - 1) * (2 * WIN - 1) + ca - cb + WIN - 1
    low = jnp.minimum(index, LANES - 1)
    high = jnp.maximum(index - LANES, 0)
    first = iota(shape, 1) < span
    for b in range(blocks):
        for h in range(heads):
            tab_ref[h : h + 1, :entries] = rel_ref[h, b : b + 1, :]
        for m in range(heads // 2):
            both = []
            for h in (2 * m, 2 * m + 1):
                lo = jnp.broadcast_to(tab_ref[h : h + 1, :LANES], shape)
                hi = jnp.broadcast_to(tab_ref[h : h + 1, LANES:], shape)
                got_lo = jnp.take_along_axis(lo, low, axis=1, mode="promise_in_bounds")
                got_hi = jnp.take_along_axis(hi, high, axis=1, mode="promise_in_bounds")
                both.append(jnp.where(index < LANES, got_lo, got_hi))
            out_ref[b, :, m * LANES : (m + 1) * LANES] = jnp.where(first, both[0], both[1])


def weights_kernel(loads, outs, scratch):
    recv, weight = (one() for one in loads)
    slots = 2 * recv.shape[1]
    pixsq = weight.shape[1] // recv.shape[0]
    totals = [weights_by_slot(recv, weight, slots, v).reshape(slots // GROUP, GROUP, pixsq) for v in range(2)]
    outs[0][...] = jnp.concatenate(totals, axis=1).reshape(2 * slots, pixsq).astype(BF16)


def split_slots(recv, cap, me):
    slot = recv[...]
    sender = over(slot, cap)
    inner = slot - sender * cap
    return sender ^ me, inner


def patch_turn(pd):
    half = WIN // 2
    r, c = iota((pd, pd), 0), iota((pd, pd), 1)
    side, rest = r // (ROWS * half), r % (ROWS * half)
    return ((rest // half) * WIN + side * half + rest % half == c).astype(F32).astype(BF16)


def chosen(shape, axis, vals, chunk_of=None, size=1):
    r = iota(shape, axis)
    if chunk_of is not None:
        chunk = over(r, size)
        r = chunk_of(chunk) * size + r - chunk * size
    slot = (r // (2 * GROUP)) * GROUP + r % GROUP
    level = (r // GROUP) % 2
    first = (vals(0) == slot) | (vals(1) == slot)
    second = (vals(2) == slot) | (vals(3) == slot)
    hit = (first & (level == 0)) | (second & (level == 1))
    return hit.astype(F32).astype(BF16)


def tables_kernel(cap, direct, me_ref, loads, outs, scratch):
    recv, embed, rel = (one() for one in loads)
    *scatter_refs, embed_out, bias_ref, select_ref = outs
    pd = recv.shape[1]
    slots = 2 * pd
    pix = embed_out.shape[0] // LANES
    ch = embed.shape[0] // pix
    turn = patch_turn(pd)
    parts = [v.astype(F32).astype(BF16) for v in split_slots(recv, cap, me_ref[0])]
    cols = (mm_nt(turn, parts[0]) * cap + mm_nt(turn, parts[1])).astype(jnp.int32)
    rows = (mm_nt(parts[0], turn) * cap + mm_nt(parts[1], turn)).astype(jnp.int32)
    select_ref[...] = chosen((2 * slots, pd), 0, lambda k: rows[k : k + 1, :])
    for stage, ref in enumerate(scatter_refs):
        ref[...] = chosen(ref.shape, 1, lambda k: cols[:, k : k + 1],
                          functools.partial(stage_chunk, stage, direct), 2 * slots // (4 * NEAR))
    for i in range(pix):
        lo, hi, move = tile_move(ch, i, embed.shape[0])
        embed_out[i * LANES : (i + 1) * LANES, :] = mm_tn(move, embed[lo:hi, :]).astype(BF16)
    bias_rows(rel, scratch[0], bias_ref)


def mix_kernel(cap, me_ref, loads, outs, scratch):
    recv, weight = (one() for one in loads)
    slots = 2 * recv.shape[1]
    pix = int(round((weight.shape[1] // recv.shape[0]) ** 0.5))
    sender, inner = split_slots(recv, cap, me_ref[0])
    for level in range(2):
        total = weights_by_slot(sender * cap + inner, weight, slots, level)
        store_spread(outs[0], spread(total.astype(BF16), True, pix), level * pix * GROUP, 0, pix)


def prep_back_kernel(size, me_ref, loads, outs, scratch):
    weight, unembed, send = loads
    weight_ref, unembed = weight(), unembed()
    mix_ref, unembed_out, owner_ref = outs
    owner = jnp.broadcast_to(send()[...], (GROUP, send.ref.shape[1]))
    if size is not None:
        cap = size * GROUP
        count = owner.shape[1] // cap
        chunk = over(iota(owner.shape, 1), cap)
        for bit in range(count.bit_length() - 1):
            gap = cap << bit
            up = pltpu.roll(owner, owner.shape[1] - gap, 1)
            down = pltpu.roll(owner, gap, 1)
            swapped = jnp.where((chunk >> bit) & 1 == 0, up, down)
            owner = jnp.where((me_ref[0] >> bit) & 1 == 1, swapped, owner)
    owner_ref[...] = owner
    rows, pixsq = weight_ref.shape
    pix = int(round(pixsq**0.5))
    ch = unembed.shape[0] // pix
    groups = rows // (2 * GROUP)
    w3 = weight_ref[...].astype(F32).reshape(groups, 2, GROUP, pixsq)
    for level in range(2):
        w_l = w3[:, level].reshape(groups * GROUP, pixsq).astype(BF16)
        store_spread(mix_ref, spread(w_l, False, pix), 0, level * pix * GROUP, pix)
    for i in range(pix):
        lo, hi, move = tile_move(ch, i, unembed.shape[0])
        unembed_out[i * LANES : (i + 1) * LANES, :] = mm_tn(move, unembed[lo:hi, :]).astype(BF16)


def layer_norm(values, gain):
    average = jnp.mean(values, axis=-1, keepdims=True)
    centred = values - average
    spread_ = jnp.mean(centred * centred, axis=-1, keepdims=True)
    return centred * lax.rsqrt(spread_ + norm_eps) * gain


def head_mask(heads, span, d):
    size = d // heads
    shape = (LANES // size * span, LANES)
    return (iota(shape, 0) // span == iota(shape, 1) // size).astype(F32).astype(BF16)


def by_group(weights, values):
    rows = values[0].shape[0]
    parts = [mm(weights[:, g * rows : (g + 1) * rows], v) for g, v in enumerate(values)]
    return jnp.concatenate(parts, axis=1)


def softmax_parts(scores, side):
    out = []
    for m in range(scores.shape[1] // LANES):
        part = scores[:, m * LANES : (m + 1) * LANES]
        low = iota(part.shape, 1) % LANES < side
        top_lo = jnp.max(jnp.where(low, part, -3e38), axis=-1, keepdims=True)
        top_hi = jnp.max(jnp.where(low, -3e38, part), axis=-1, keepdims=True)
        out.append(jnp.exp(part - jnp.where(low, top_lo, top_hi)))
    return jnp.concatenate(out, axis=1)


def attend_rows(query, key, value, bias, heads, mask, blocked):
    d = query.shape[1]
    times = mask.shape[0] // key.shape[0]
    scores, values = [], []
    for g in range(d // LANES):
        lanes = slice(g * LANES, (g + 1) * LANES)
        expand = lambda v: jnp.concatenate([v[:, lanes]] * times, axis=0) * mask
        scores.append(mm_nt(query[:, lanes], expand(key)))
        values.append(expand(value))
    scores = jnp.concatenate(scores, axis=1) * (d // heads) ** (-0.5) + bias
    if blocked is not None:
        scores = jnp.where(blocked, -1e30, scores)
    weights = softmax_parts(scores, key.shape[0]).astype(BF16)
    return by_group(weights, values), weights


def feed_forward(residual, gain2, up, down):
    normed = layer_norm(residual, gain2).astype(BF16)
    hidden = jax.nn.gelu(mm(normed, up)).astype(BF16)
    return (residual + mm(hidden, down)).astype(BF16)


def lay_tiles(rows, count):
    return jnp.concatenate([rows[:, t * LANES : (t + 1) * LANES] for t in range(count)], axis=0)


def joined(chunks):
    pieces = [one()[...].astype(F32).reshape(-1, one.ref.shape[-1]) for one in chunks]
    return jnp.concatenate(pieces, axis=0).astype(BF16)


def stage_chunk(stage, direct, i):
    if not direct:
        return i + (0 if stage == 0 else NEAR)
    if stage == 0:
        return 2 * i
    return jnp.where(i < NEAR, 2 * i + 1, i + NEAR)


def regrid_part(stage, direct, data, x_ref, c_ref, mix, scatter, embed, pix):
    slots, width = data.shape
    ch = width // pix
    for j in range(pix):
        lo, hi, move = tile_move(ch, j, width)
        x_ref[:, j * LANES : (j + 1) * LANES] = mm(data[:, lo:hi], move)
    mix_ref = mix()
    size = mix_ref.shape[0] // (4 * NEAR)

    def group(g, carry):
        chunk = lax.div(g, size)
        where = stage_chunk(stage, direct, chunk) * size + g - chunk * size
        tiles = lay_tiles(x_ref[pl.ds(pl.multiple_of(g * GROUP, GROUP), GROUP), :], pix).astype(BF16)
        out = mm(mix_ref[where], tiles)
        to = pl.ds(pl.multiple_of(g * 2 * GROUP, 2 * GROUP), 2 * GROUP)
        for i in range(pix):
            low = out[i * GROUP : (i + 1) * GROUP]
            high = out[(pix + i) * GROUP : (pix + i + 1) * GROUP]
            both = jnp.concatenate([low, high], axis=0).astype(BF16)
            c_ref[to, i * LANES : (i + 1) * LANES] = both
        return carry

    lax.fori_loop(0, slots // GROUP, group, 0, unroll=4)
    scatter_ref, embed_ref = scatter(), embed()
    pixels = []
    for j in range(0, pix, 2):
        cols = slice(j * LANES, (j + 2) * LANES)
        pixels.append(mm(scatter_ref[...], c_ref[:, cols]).astype(BF16))
    return mm(jnp.concatenate(pixels, axis=1), embed_ref[...])


def early_kernel(pix, direct, loads, outs, scratch):
    *chunks, mix, scatter, embed = loads
    outs[0][...] = regrid_part(0, direct, joined(chunks), *scratch, mix, scatter, embed, pix)


def first_kernel(pix, direct, layer, loads, outs, scratch):
    *chunks, mix, scatter, embed, prior, gain1, gain2, qkv, bias, proj, up, down = loads
    total = regrid_part(1, direct, joined(chunks), *scratch, mix, scatter, embed, pix)
    state = (prior()[...] + total).astype(BF16).astype(F32)
    pd, d = state.shape
    heads = bias.ref.shape[1] // (WIN * WIN)
    normed = layer_norm(state, gain1()[layer : layer + 1, :]).astype(BF16)
    packed = mm(normed, qkv()[...]).astype(BF16)
    query, key, value = packed[:, :d], packed[:, d : 2 * d], packed[:, 2 * d :]
    half = pd // 2
    win_rows = ROWS // WIN
    part_rows = half // win_rows
    bias_all = bias()[...]
    mask = head_mask(heads, WIN * WIN, d)
    mixed = [None] * (2 * win_rows)
    weights = [None] * (2 * win_rows)
    for w in range(win_rows):
        def rows(v):
            lo, hi = w * part_rows, (w + 1) * part_rows
            return jnp.concatenate([v[lo:hi], v[half + lo : half + hi]], axis=0)

        out, wts = attend_rows(rows(query), rows(key), rows(value), bias_all, heads, mask, None)
        mixed[w], mixed[win_rows + w] = out[:part_rows], out[part_rows:]
        weights[w], weights[win_rows + w] = wts[:part_rows], wts[part_rows:]
    total = by_group(jnp.concatenate(weights, axis=0), [mask] * (d // LANES))
    mixed = (jnp.concatenate(mixed, axis=0) / total).astype(BF16)
    attended = mm(mixed, proj()[...]).astype(BF16)
    residual = state + attended.astype(F32)
    new = feed_forward(residual, gain2()[layer : layer + 1, :], up()[...], down()[...])
    outs[0][...] = new[:half]
    outs[1][...] = new[half:]


def turned(low, high):
    shift = low.shape[0] * (WIN // 2) // ROWS
    turn = lambda v: jnp.concatenate([v[shift:], v[:shift]], axis=0)
    return jnp.concatenate([turn(low[...]), turn(high[...])], axis=0).astype(F32)


def own_kernel(layer, loads, outs, scratch):
    low, high, gain1, qkv = loads
    normed = layer_norm(turned(low(), high()), gain1()[layer : layer + 1, :]).astype(BF16)
    outs[0][...] = mm(normed, qkv()[...]).astype(BF16)


def second_kernel(layer, loads, outs, scratch):
    packed, low, high, gain1, gain2, qkv, bias, left, right, proj, up, down, select = loads
    half, d = low.ref.shape
    heads = bias.ref.shape[1] // (WIN * WIN)
    shift = half * (WIN // 2) // ROWS
    back = lambda v: jnp.concatenate([v[half - shift :], v[: half - shift]], axis=0)
    own = turned(low(), high())
    gain = gain1()[layer : layer + 1, :]
    normed_s = layer_norm(turned(left(), right()), gain).astype(BF16)
    packed = packed()[...]
    packed_s = mm(normed_s, qkv()[:, d:]).astype(BF16)
    query, key, value = packed[:, :d], packed[:, d : 2 * d], packed[:, 2 * d :]
    key_s, value_s = packed_s[:, :d], packed_s[:, d:]
    win_rows = ROWS // WIN
    part = half // win_rows
    span = WIN * WIN
    bias_all = bias()[...]
    mask = head_mask(heads, span, d)
    outs_m, outs_w = [[], []], [[], []]
    for w in range(win_rows):
        near = slice(w * part, (w + 1) * part)
        far = slice(half + w * part, half + (w + 1) * part)
        for side in range(2):
            if side == 0:
                q = query[near]
                k = jnp.concatenate([key_s[near], key[near]], axis=0)
                v = jnp.concatenate([value_s[near], value[near]], axis=0)
                b = bias_all[part:]
            else:
                q = query[far]
                k = jnp.concatenate([key[far], key_s[far]], axis=0)
                v = jnp.concatenate([value[far], value_s[far]], axis=0)
                b = bias_all[:part]
            blocked = None
            if w == win_rows - 1:
                shape = (part, heads * span)
                q_up = iota(shape, 0) % part >= part // 2
                k_up = iota(shape, 1) % part >= part // 2
                blocked = q_up != k_up
            out, wts = attend_rows(q, k, v, b, heads, mask, blocked)
            outs_m[side].append(out)
            outs_w[side].append(wts)
    total = by_group(jnp.concatenate(outs_w[0] + outs_w[1], axis=0), [mask] * (d // LANES))
    mixed = (jnp.concatenate(outs_m[0] + outs_m[1], axis=0) / total).astype(BF16)
    attended = mm(mixed, proj()[...]).astype(BF16)
    residual = own + attended.astype(F32)
    new = feed_forward(residual, gain2()[layer : layer + 1, :], up()[...], down()[...])
    state = jnp.concatenate([back(new[:half]), back(new[half:])], axis=0)
    sent = mm(select()[...], state).astype(BF16)
    if len(outs) == 1:
        outs[0][...] = sent
        return
    rows = sent.shape[0] // (2 * len(outs))
    for x in range(2 * len(outs)):
        outs[x // 2][x % 2] = sent[x * rows : (x + 1) * rows]


def back_part(size, first, me_ref, chunks, mix, unembed, p_ref, slot_ref):
    rows = jnp.concatenate([one()[...].reshape(-1, one.ref.shape[-1]) for one in chunks], axis=0)
    unembed_ref = unembed()
    pix = unembed_ref.shape[0] // LANES
    for j in range(0, pix, 2):
        cols = slice(j * LANES, (j + 2) * LANES)
        p_ref[:, cols] = mm_nt(rows, unembed_ref[cols, :])
    mix_ref = mix()

    def group(g, carry):
        got = p_ref[pl.ds(pl.multiple_of(g * 2 * GROUP, 2 * GROUP), 2 * GROUP), :]
        data = jnp.concatenate([lay_tiles(got[:GROUP], pix), lay_tiles(got[GROUP:], pix)], axis=0)
        where = first + g
        if size is not None:
            chunk = lax.div(where, size)
            where = (chunk ^ me_ref[0]) * size + where - chunk * size
        out = mm(mix_ref[where], data.astype(BF16))
        to = pl.ds(pl.multiple_of(g * GROUP, GROUP), GROUP)
        for i in range(pix):
            slot_ref[to, i * LANES : (i + 1) * LANES] = out[i * GROUP : (i + 1) * GROUP]
        return carry

    lax.fori_loop(0, rows.shape[0] // (2 * GROUP), group, 0, unroll=4)


def back_kernel(size, first, me_ref, loads, outs, scratch):
    *chunks, unembed, mix = loads
    back_part(size, first, me_ref, chunks, mix, unembed, *scratch)
    outs[0][...] = scratch[1][...].astype(BF16)


def last_kernel(size, first, me_ref, loads, outs, scratch):
    *chunks, unembed, mix, prior, send = loads
    back_part(size, first, me_ref, chunks, mix, unembed, *scratch)
    slot_ref, out_ref = scratch[1], outs[0]
    pix = unembed.ref.shape[0] // LANES
    pd, total = out_ref.shape
    ch = total // pix
    prior_ref = prior()
    owner = send()
    onehot = (iota((pd, owner.shape[1]), 0) == owner[:1, :]).astype(F32).astype(BF16)
    tiles = [None] * (-(-total // LANES))
    for j in range(0, pix, 2):
        cols = slice(j * LANES, (j + 2) * LANES)
        slots = jnp.concatenate([prior_ref[:, cols], slot_ref[:, cols].astype(BF16)], axis=0)
        both = mm(onehot, slots)
        for jj in (j, j + 1):
            val = both[:, (jj - j) * LANES : (jj - j + 1) * LANES]
            t, off = divmod(ch * jj, LANES)
            if off:
                val = pltpu.roll(val, off, 1)
            lane = iota(val.shape, 1)
            low, high = jnp.where(lane >= off, val, 0.0), jnp.where(lane < off, val, 0.0)
            for tt, piece in ((t, low), (t + 1, high)):
                if tt == t + 1 and off + ch <= LANES:
                    continue
                tiles[tt] = piece if tiles[tt] is None else tiles[tt] + piece
    for t, tile in enumerate(tiles):
        hi = min((t + 1) * LANES, total)
        out_ref[:, t * LANES : hi] = tile[:, : hi - t * LANES]


def swap(value, axis):
    return lax.all_to_all(value, axis, split_axis=0, concat_axis=0, tiled=True)


def swap_pairs(value, axis):
    count = lax.axis_size(axis)
    rows, width = value.shape
    cap = rows // (2 * count)
    if cap % GROUP == 0:
        return swap(value, axis)
    groups = rows // (2 * GROUP)
    v = value.reshape(groups, 2, GROUP, width).transpose(1, 0, 2, 3).reshape(2, count, cap, width)
    v = swap(v.transpose(1, 0, 2, 3).reshape(rows, width), axis)
    v = v.reshape(count, 2, cap, width).transpose(1, 0, 2, 3).reshape(2, groups, GROUP, width)
    return v.transpose(1, 0, 2, 3).reshape(rows, width)


def flip(value, axis, bits):
    count = lax.axis_size(axis)
    return lax.ppermute(value, axis, [(source, source ^ bits) for source in range(count)])


def from_behind(value, axis, steps):
    count = lax.axis_size(axis)
    pairs = [(source, (source + steps) % count) for source in range(count)]
    return lax.ppermute(value, axis, pairs)


STAGES = 2
NEAR = 4


def body(
    bands, send_table, recv_table, regrid_weight, embed_weight, norm1_gain, qkv_weight, rel_bias,
    proj_weight, norm2_gain, up_weight, down_weight, unembed_weight,
):
    pd, width = bands.shape
    slots = send_table.shape[1]
    kk = recv_table.shape[0]
    d = embed_weight.shape[1]
    pixsq = regrid_weight.shape[1] // kk
    pix = int(round(pixsq**0.5))
    wide = pix * LANES
    count = lax.axis_size("tile")
    cap = slots // count
    chips = count // 2
    direct = chips == 2 * NEAR and cap % GROUP == 0
    vm = pltpu.VMEM
    per = slots // STAGES
    groups = per // GROUP
    my = lax.axis_index("tile").astype(jnp.int32).reshape(1)
    if not direct:
        my = my * 0

    if direct:
        turns = [*range(NEAR, chips), *range(NEAR - 1, 0, -1)]

        outgoing = call(pick_direct_kernel, [In(send_table), In(bands)],
                        [sds((2, cap, width), BF16)] * chips, [vm((count, cap, width), BF16)], my, flops=1e10)
        came = [outgoing[0]] + [None] * (chips - 1)
        for s in turns:
            came[s] = flip(outgoing[s], "tile", 2 * s)
    else:
        outgoing = call(pick_kernel, [In(send_table), In(bands)], [sds((slots, width), BF16)])
        incoming = swap(outgoing, "tile")

    heads = rel_bias.shape[1]
    span = WIN * WIN
    wsend = call(weights_kernel, [In(recv_table), In(regrid_weight)], [sds((2 * slots, pixsq), BF16)],
                 flops=1e10, after=[outgoing[0] if direct else outgoing])
    wback = swap_pairs(wsend, "tile")
    scatter_a, scatter_b, embed_pad, bias, select = call(
        functools.partial(tables_kernel, cap, direct),
        [In(recv_table), In(embed_weight), In(rel_bias.transpose(1, 0, 2))],
        [sds((pd, slots // 2), BF16), sds((pd, 3 * slots // 2), BF16), sds((wide, d), BF16),
         sds((rel_bias.shape[0], span, heads * span), F32), sds((2 * slots, pd), BF16)],
        [vm((heads, 2 * LANES), F32)], my, flops=2e9, after=[wsend])
    mix = call(functools.partial(mix_kernel, cap), [In(recv_table), In(regrid_weight)],
               [sds((slots // GROUP, 2 * pix * GROUP, pix * GROUP), BF16)], (), my, flops=2e9, after=[embed_pad])

    def relay(arrays, after=()):
        shape = (len(arrays), *arrays[0].shape[1:])
        return call(relay_kernel, [at(x, 1) for x in arrays], [sds(shape, BF16)], after=after)

    def regrid_scratch(rows):
        return [vm((rows, wide), F32), vm((2 * rows, wide), BF16)]

    if direct:
        near = [at(x, 0) for x in came[:NEAR]]
    else:
        near, far = [at(incoming, slice(0, slots // 4))], [at(incoming, slice(slots // 4, slots))]
    total = call(functools.partial(early_kernel, pix, direct),
                 [*near, In(mix), In(scatter_a), In(embed_pad)], [sds((pd, d), F32)],
                 regrid_scratch(slots // 4), flops=2e9)
    if direct:
        for_partner = relay(came, [total])
        passed = flip(for_partner, "tile", 1)
        far = [at(passed, i) for i in range(NEAR)]
        far += [y for i in range(NEAR, chips) for y in (at(came[i], 0), at(passed, i))]

    def layer(n):
        return [In(norm1_gain), In(norm2_gain), at(qkv_weight, n), at(bias, n)], [
            at(proj_weight, n), at(up_weight, n), at(down_weight, n)]

    half = pd // 2
    ins_a, ins_b = layer(0)
    low, high = call(
        functools.partial(first_kernel, pix, direct, 0),
        [*far, In(mix), In(scatter_b), In(embed_pad), In(total), *ins_a, *ins_b],
        [sds((half, d), BF16)] * 2, regrid_scratch(3 * slots // 4), flops=4e9)
    right = from_behind(low, "tile", -1)
    left = from_behind(high, "tile", 1)
    ins_a, ins_b = layer(1)
    packed = call(functools.partial(own_kernel, 1), [In(low), In(high), In(norm1_gain), at(qkv_weight, 1)],
                  [sds((pd, 3 * d), BF16)], flops=2e8)
    rows = 2 * cap
    sent = call(
        functools.partial(second_kernel, 1),
        [In(packed), In(low), In(high), *ins_a, In(left), In(right), *ins_b, In(select)],
        [sds((2, rows, d), BF16)] * chips if direct else [sds((2 * slots, d), BF16)], flops=2e9)
    one_sent = sent[0] if direct else sent
    size = cap // GROUP if direct else None
    mix_back, unembed_pad, owner = call(
        functools.partial(prep_back_kernel, size), [In(wback), In(unembed_weight.T), In(send_table)],
        [sds((slots // GROUP, pix * GROUP, 2 * pix * GROUP), BF16), sds((wide, d), BF16),
         sds((GROUP, slots), jnp.int32)], (), my, flops=2e9, after=[one_sent])

    back_scratch = [vm((2 * per, wide), F32), vm((per, wide), F32)]
    if direct:
        got = [sent[0]] + [None] * (chips - 1)
        for s in turns:
            got[s] = flip(sent[s], "tile", 2 * s)
        near_all = relay(got[:NEAR], [mix_back])
        near_pass = flip(near_all, "tile", 1)
        near = [y for i, x in enumerate(got[:NEAR]) for y in (at(x, 0), at(near_pass, i))]
    else:
        got = swap_pairs(sent, "tile").reshape(STAGES, 2 * per, d)
        near, far = [at(got, 0)], [at(got, 1)]
    prior = call(functools.partial(back_kernel, size, 0), [*near, In(unembed_pad), In(mix_back)],
                 [sds((per, wide), BF16)], back_scratch, my, flops=2e9)
    if direct:
        far_pass = flip(relay(got[NEAR:], [prior]), "tile", 1)
        far = [y for i, x in enumerate(got[NEAR:]) for y in (at(x, 0), at(far_pass, i))]
    return call(functools.partial(last_kernel, size, groups), [*far, In(unembed_pad), In(mix_back), In(prior), In(owner)],
                [sds((pd, width), F32)], back_scratch, my, flops=3e9)


def solution(mesh):
    in_specs = (
        P(("groups", "tile"), None), P("tile", None), P(None, "tile"), P("tile", None),
        P(), P(), P(), P(), P(), P(), P(), P(), P(),
    )
    out_specs = P(("groups", "tile"), None)
    return jax.shard_map(body, mesh=mesh, in_specs=in_specs, out_specs=out_specs, check_vma=False)
```

```python
import functools

import jax
import jax.numpy as jnp
import numpy as np
from jax import lax
from jax.experimental import pallas as pl
from jax.experimental.pallas import tpu as pltpu
from jax.sharding import PartitionSpec as P


WIN = 8
ROWS = 24
LANES = 128
GROUP = 8

norm_eps = 1e-05
F32 = jnp.float32
BF16 = jnp.bfloat16


def iota(shape, axis):
    return lax.broadcasted_iota(jnp.int32, shape, axis)


def mm(a, b):
    return jnp.dot(a, b, preferred_element_type=F32)


def mm_tn(a, b):
    return lax.dot_general(a, b, (((0,), (0,)), ((), ())), preferred_element_type=F32)


def mm_nt(a, b):
    return lax.dot_general(a, b, (((1,), (1,)), ((), ())), preferred_element_type=F32)


VMEM_LIMIT = 16 << 20


class In:
    def __init__(self, array, index=None):
        self.array = array
        self.index = index


def at(array, index):
    return In(array, index)


class Loaded:
    def __init__(self, ref):
        self.ref = ref

    def __call__(self):
        return self.ref


def call(kernel, ins, outs, scratch=(), table=None, flops=0, after=()):
    def run(*refs):
        refs = list(refs)
        lead = [refs.pop(0)] if table is not None else []
        loads = []
        for one in ins:
            ref = refs.pop(0)
            loads.append(Loaded(ref if one.index is None else ref.at[one.index]))
        del refs[: len(after)]
        held = [refs.pop(0) for _ in outs]
        kernel(*lead, loads, held, refs)

    vmem = pl.BlockSpec(memory_space=pltpu.VMEM)
    in_specs = [] if table is None else [pl.BlockSpec(memory_space=pltpu.SMEM)]
    moved = sum(int(np.prod(s.array.shape)) * s.array.dtype.itemsize for s in ins)
    got = pl.pallas_call(
        run,
        out_shape=list(outs),
        in_specs=in_specs + [vmem] * len(ins) + [pl.BlockSpec(memory_space=pl.ANY)] * len(after),
        out_specs=[vmem] * len(outs),
        scratch_shapes=list(scratch),
        compiler_params=pltpu.CompilerParams(vmem_limit_bytes=VMEM_LIMIT),
        cost_estimate=pl.CostEstimate(flops=int(flops), bytes_accessed=moved, transcendentals=0),
    )(*([] if table is None else [table]), *[one.array for one in ins], *after)
    return got if len(outs) > 1 else got[0]


def sds(shape, dtype):
    return jax.ShapeDtypeStruct(shape, dtype)


def chosen_rows(bands_ref, send_ref):
    rows, slots = bands_ref.shape[0], send_ref.shape[1]
    onehot = (iota((rows, slots), 0) == send_ref[...]).astype(F32).astype(BF16)
    return mm_tn(onehot, bands_ref[...])


def pick_kernel(loads, outs, scratch):
    send, bands = loads
    outs[0][...] = chosen_rows(bands(), send()).astype(BF16)


def pick_direct_kernel(my_ref, loads, outs, scratch):
    send, bands = loads
    held = scratch[0]
    held[...] = chosen_rows(bands(), send()).reshape(held.shape).astype(BF16)
    for s, out in enumerate(outs):
        for e in range(2):
            out[e] = held[my_ref[0] ^ (2 * s + e)]


def relay_kernel(loads, outs, scratch):
    for i, one in enumerate(loads):
        outs[0][i] = one()[...]


def spread(weights, fixed_first, pix):
    width = pix * GROUP
    shape = (pix * pix, pix * width)
    r, c = iota(shape, 0), iota(shape, 1)
    outer, inner = c // width, (c % width) // GROUP
    if fixed_first:
        sel = (r // pix == outer) & (r % pix == inner)
    else:
        sel = (r % pix == outer) & (r // pix == inner)
    out = mm(weights, sel.astype(F32).astype(BF16))
    own = iota(out.shape, 0) % GROUP == iota(out.shape, 1) % GROUP
    return jnp.where(own, out, 0.0)


def store_spread(out_ref, value, row0, col0, pix):
    groups = value.shape[0] // GROUP
    width = pix * GROUP
    for o in range(0, pix, 2):
        lo = value[:, o * width : (o + 1) * width].reshape(groups, GROUP, width)
        hi = value[:, (o + 1) * width : (o + 2) * width].reshape(groups, GROUP, width)
        both = jnp.concatenate([lo, hi], axis=1).astype(BF16)
        out_ref[:, row0 + o * GROUP : row0 + (o + 2) * GROUP, col0 : col0 + width] = both


def tile_move(ch, j, total):
    lo = (ch * j // LANES) * LANES
    hi = min(lo + 2 * LANES, total)
    shape = (hi - lo, LANES)
    move = (iota(shape, 0) - (ch * j - lo) == iota(shape, 1)) & (iota(shape, 1) < ch)
    return lo, hi, move.astype(F32).astype(BF16)


def weights_by_slot(recv, weight, slots, level):
    pixsq = weight.shape[1] // recv.shape[0]
    r = iota((slots, recv.shape[1]), 0)
    total = None
    for k in (2 * level, 2 * level + 1):
        hit = (recv[k : k + 1, :] == r).astype(F32).astype(BF16)
        term = mm(hit, weight[:, k * pixsq : (k + 1) * pixsq])
        total = term if total is None else total + term
    return total


def over(values, size):
    return jnp.floor((values.astype(F32) + 0.5) * (1.0 / size)).astype(jnp.int32)


def bias_rows(rel_ref, tab_ref, out_ref):
    heads, blocks, entries = rel_ref.shape
    span = WIN * WIN
    half = WIN // 2

    def row_col(pos):
        side = pos // (span // 2)
        return (pos % (span // 2)) // half, side * half + pos % half

    shape = (span, LANES)
    ra, ca = row_col(iota(shape, 0))
    rb, cb = row_col(iota(shape, 1) % span)
    index = (ra - rb + WIN - 1) * (2 * WIN - 1) + ca - cb + WIN - 1
    low = jnp.minimum(index, LANES - 1)
    high = jnp.maximum(index - LANES, 0)
    first = iota(shape, 1) < span
    for b in range(blocks):
        for h in range(heads):
            tab_ref[h : h + 1, :entries] = rel_ref[h, b : b + 1, :]
        for m in range(heads // 2):
            both = []
            for h in (2 * m, 2 * m + 1):
                lo = jnp.broadcast_to(tab_ref[h : h + 1, :LANES], shape)
                hi = jnp.broadcast_to(tab_ref[h : h + 1, LANES:], shape)
                got_lo = jnp.take_along_axis(lo, low, axis=1, mode="promise_in_bounds")
                got_hi = jnp.take_along_axis(hi, high, axis=1, mode="promise_in_bounds")
                both.append(jnp.where(index < LANES, got_lo, got_hi))
            out_ref[b, :, m * LANES : (m + 1) * LANES] = jnp.where(first, both[0], both[1])


def weights_kernel(loads, outs, scratch):
    recv, weight = (one() for one in loads)
    slots = 2 * recv.shape[1]
    pixsq = weight.shape[1] // recv.shape[0]
    totals = [weights_by_slot(recv, weight, slots, v).reshape(slots // GROUP, GROUP, pixsq) for v in range(2)]
    outs[0][...] = jnp.concatenate(totals, axis=1).reshape(2 * slots, pixsq).astype(BF16)


def split_slots(recv, cap, me):
    slot = recv[...]
    sender = over(slot, cap)
    inner = slot - sender * cap
    return sender ^ me, inner


def patch_turn(pd):
    half = WIN // 2
    r, c = iota((pd, pd), 0), iota((pd, pd), 1)
    side, rest = r // (ROWS * half), r % (ROWS * half)
    return ((rest // half) * WIN + side * half + rest % half == c).astype(F32).astype(BF16)


def chosen(shape, axis, vals, chunk_of=None, size=1):
    r = iota(shape, axis)
    if chunk_of is not None:
        chunk = over(r, size)
        r = chunk_of(chunk) * size + r - chunk * size
    slot = (r // (2 * GROUP)) * GROUP + r % GROUP
    level = (r // GROUP) % 2
    first = (vals(0) == slot) | (vals(1) == slot)
    second = (vals(2) == slot) | (vals(3) == slot)
    hit = (first & (level == 0)) | (second & (level == 1))
    return hit.astype(F32).astype(BF16)


def tables_kernel(cap, direct, me_ref, loads, outs, scratch):
    recv, embed, rel = (one() for one in loads)
    *scatter_refs, embed_out, bias_ref, select_ref = outs
    pd = recv.shape[1]
    slots = 2 * pd
    pix = embed_out.shape[0] // LANES
    ch = embed.shape[0] // pix
    turn = patch_turn(pd)
    parts = [v.astype(F32).astype(BF16) for v in split_slots(recv, cap, me_ref[0])]
    cols = (mm_nt(turn, parts[0]) * cap + mm_nt(turn, parts[1])).astype(jnp.int32)
    rows = (mm_nt(parts[0], turn) * cap + mm_nt(parts[1], turn)).astype(jnp.int32)
    select_ref[...] = chosen((2 * slots, pd), 0, lambda k: rows[k : k + 1, :])
    for stage, ref in enumerate(scatter_refs):
        ref[...] = chosen(ref.shape, 1, lambda k: cols[:, k : k + 1],
                          functools.partial(stage_chunk, stage, direct), 2 * slots // (4 * NEAR))
    for i in range(pix):
        lo, hi, move = tile_move(ch, i, embed.shape[0])
        embed_out[i * LANES : (i + 1) * LANES, :] = mm_tn(move, embed[lo:hi, :]).astype(BF16)
    bias_rows(rel, scratch[0], bias_ref)


def mix_kernel(cap, me_ref, loads, outs, scratch):
    recv, weight = (one() for one in loads)
    slots = 2 * recv.shape[1]
    pix = int(round((weight.shape[1] // recv.shape[0]) ** 0.5))
    sender, inner = split_slots(recv, cap, me_ref[0])
    for level in range(2):
        total = weights_by_slot(sender * cap + inner, weight, slots, level)
        store_spread(outs[0], spread(total.astype(BF16), True, pix), level * pix * GROUP, 0, pix)


def prep_back_kernel(size, me_ref, loads, outs, scratch):
    weight, unembed, send = loads
    weight_ref, unembed = weight(), unembed()
    mix_ref, unembed_out, owner_ref = outs
    owner = jnp.broadcast_to(send()[...], (GROUP, send.ref.shape[1]))
    if size is not None:
        cap = size * GROUP
        count = owner.shape[1] // cap
        chunk = over(iota(owner.shape, 1), cap)
        for bit in range(count.bit_length() - 1):
            gap = cap << bit
            up = pltpu.roll(owner, owner.shape[1] - gap, 1)
            down = pltpu.roll(owner, gap, 1)
            swapped = jnp.where((chunk >> bit) & 1 == 0, up, down)
            owner = jnp.where((me_ref[0] >> bit) & 1 == 1, swapped, owner)
        r, c = iota((owner.shape[1], owner.shape[1]), 0), iota((owner.shape[1], owner.shape[1]), 1)
        chunk = over(c, cap)
        late = chunk - 2 * NEAR
        late = 2 * NEAR + jnp.where(late < NEAR, 2 * late, 2 * late - 2 * NEAR + 1)
        source = jnp.where(chunk < 2 * NEAR, chunk, late) * cap + c - chunk * cap
        move = (r == source).astype(F32).astype(BF16)
        low = owner % (2 * LANES // 4)
        owner = [mm(v.astype(F32).astype(BF16), move) for v in (owner - low, low)]
        owner = (owner[0] + owner[1]).astype(jnp.int32)
    owner_ref[...] = owner
    rows, pixsq = weight_ref.shape
    pix = int(round(pixsq**0.5))
    ch = unembed.shape[0] // pix
    groups = rows // (2 * GROUP)
    w3 = weight_ref[...].astype(F32).reshape(groups, 2, GROUP, pixsq)
    for level in range(2):
        w_l = w3[:, level].reshape(groups * GROUP, pixsq).astype(BF16)
        store_spread(mix_ref, spread(w_l, False, pix), 0, level * pix * GROUP, pix)
    for i in range(pix):
        lo, hi, move = tile_move(ch, i, unembed.shape[0])
        unembed_out[i * LANES : (i + 1) * LANES, :] = mm_tn(move, unembed[lo:hi, :]).astype(BF16)


def layer_norm(values, gain):
    average = jnp.mean(values, axis=-1, keepdims=True)
    centred = values - average
    spread_ = jnp.mean(centred * centred, axis=-1, keepdims=True)
    return centred * lax.rsqrt(spread_ + norm_eps) * gain


def head_mask(heads, span, d):
    size = d // heads
    shape = (LANES // size * span, LANES)
    return (iota(shape, 0) // span == iota(shape, 1) // size).astype(F32).astype(BF16)


def by_group(weights, values):
    rows = values[0].shape[0]
    parts = [mm(weights[:, g * rows : (g + 1) * rows], v) for g, v in enumerate(values)]
    return jnp.concatenate(parts, axis=1)


def softmax_parts(scores, side):
    out = []
    for m in range(scores.shape[1] // LANES):
        part = scores[:, m * LANES : (m + 1) * LANES]
        low = iota(part.shape, 1) % LANES < side
        top_lo = jnp.max(jnp.where(low, part, -3e38), axis=-1, keepdims=True)
        top_hi = jnp.max(jnp.where(low, -3e38, part), axis=-1, keepdims=True)
        out.append(jnp.exp(part - jnp.where(low, top_lo, top_hi)))
    return jnp.concatenate(out, axis=1)


def attend_rows(query, key, value, bias, heads, mask, blocked):
    d = query.shape[1]
    times = mask.shape[0] // key.shape[0]
    scores, values = [], []
    for g in range(d // LANES):
        lanes = slice(g * LANES, (g + 1) * LANES)
        expand = lambda v: jnp.concatenate([v[:, lanes]] * times, axis=0) * mask
        scores.append(mm_nt(query[:, lanes], expand(key)))
        values.append(expand(value))
    scores = jnp.concatenate(scores, axis=1) * (d // heads) ** (-0.5) + bias
    if blocked is not None:
        scores = jnp.where(blocked, -1e30, scores)
    weights = softmax_parts(scores, key.shape[0]).astype(BF16)
    return by_group(weights, values), weights


def feed_forward(residual, gain2, up, down):
    normed = layer_norm(residual, gain2).astype(BF16)
    hidden = jax.nn.gelu(mm(normed, up)).astype(BF16)
    return (residual + mm(hidden, down)).astype(BF16)


def lay_tiles(rows, count):
    return jnp.concatenate([rows[:, t * LANES : (t + 1) * LANES] for t in range(count)], axis=0)


def joined(chunks):
    pieces = [one()[...].astype(F32).reshape(-1, one.ref.shape[-1]) for one in chunks]
    return jnp.concatenate(pieces, axis=0).astype(BF16)


def stage_chunk(stage, direct, i):
    if not direct:
        return i + (0 if stage == 0 else NEAR)
    if stage == 0:
        return 2 * i
    return jnp.where(i < NEAR, 2 * i + 1, i + NEAR)


def regrid_part(stage, direct, data, x_ref, c_ref, mix, scatter, embed, pix):
    slots, width = data.shape
    ch = width // pix
    for j in range(pix):
        lo, hi, move = tile_move(ch, j, width)
        x_ref[:, j * LANES : (j + 1) * LANES] = mm(data[:, lo:hi], move)
    mix_ref = mix()
    size = mix_ref.shape[0] // (4 * NEAR)

    def group(g, carry):
        chunk = lax.div(g, size)
        where = stage_chunk(stage, direct, chunk) * size + g - chunk * size
        tiles = lay_tiles(x_ref[pl.ds(pl.multiple_of(g * GROUP, GROUP), GROUP), :], pix).astype(BF16)
        out = mm(mix_ref[where], tiles)
        to = pl.ds(pl.multiple_of(g * 2 * GROUP, 2 * GROUP), 2 * GROUP)
        for i in range(pix):
            low = out[i * GROUP : (i + 1) * GROUP]
            high = out[(pix + i) * GROUP : (pix + i + 1) * GROUP]
            both = jnp.concatenate([low, high], axis=0).astype(BF16)
            c_ref[to, i * LANES : (i + 1) * LANES] = both
        return carry

    lax.fori_loop(0, slots // GROUP, group, 0, unroll=12)
    scatter_ref, embed_ref = scatter(), embed()
    pixels = []
    for j in range(0, pix, 2):
        cols = slice(j * LANES, (j + 2) * LANES)
        pixels.append(mm(scatter_ref[...], c_ref[:, cols]).astype(BF16))
    return mm(jnp.concatenate(pixels, axis=1), embed_ref[...])


def early_kernel(pix, direct, loads, outs, scratch):
    *chunks, mix, scatter, embed = loads
    outs[0][...] = regrid_part(0, direct, joined(chunks), *scratch, mix, scatter, embed, pix)


def first_kernel(pix, direct, layer, loads, outs, scratch):
    *chunks, mix, scatter, embed, prior, gain1, gain2, qkv, bias, proj, up, down = loads
    total = regrid_part(1, direct, joined(chunks), *scratch, mix, scatter, embed, pix)
    state = (prior()[...] + total).astype(BF16).astype(F32)
    pd, d = state.shape
    heads = bias.ref.shape[1] // (WIN * WIN)
    normed = layer_norm(state, gain1()[layer : layer + 1, :]).astype(BF16)
    packed = mm(normed, qkv()[...]).astype(BF16)
    query, key, value = packed[:, :d], packed[:, d : 2 * d], packed[:, 2 * d :]
    half = pd // 2
    win_rows = ROWS // WIN
    part_rows = half // win_rows
    bias_all = bias()[...]
    mask = head_mask(heads, WIN * WIN, d)
    mixed = [None] * (2 * win_rows)
    weights = [None] * (2 * win_rows)
    for w in range(win_rows):
        def rows(v):
            lo, hi = w * part_rows, (w + 1) * part_rows
            return jnp.concatenate([v[lo:hi], v[half + lo : half + hi]], axis=0)

        out, wts = attend_rows(rows(query), rows(key), rows(value), bias_all, heads, mask, None)
        mixed[w], mixed[win_rows + w] = out[:part_rows], out[part_rows:]
        weights[w], weights[win_rows + w] = wts[:part_rows], wts[part_rows:]
    total = by_group(jnp.concatenate(weights, axis=0), [mask] * (d // LANES))
    mixed = (jnp.concatenate(mixed, axis=0) / total).astype(BF16)
    attended = mm(mixed, proj()[...]).astype(BF16)
    residual = state + attended.astype(F32)
    new = feed_forward(residual, gain2()[layer : layer + 1, :], up()[...], down()[...])
    outs[0][...] = new[:half]
    outs[1][...] = new[half:]


def turned(low, high):
    shift = low.shape[0] * (WIN // 2) // ROWS
    turn = lambda v: jnp.concatenate([v[shift:], v[:shift]], axis=0)
    return jnp.concatenate([turn(low[...]), turn(high[...])], axis=0).astype(F32)


def own_kernel(layer, loads, outs, scratch):
    low, high, gain1, qkv = loads
    normed = layer_norm(turned(low(), high()), gain1()[layer : layer + 1, :]).astype(BF16)
    outs[0][...] = mm(normed, qkv()[...]).astype(BF16)


def second_kernel(layer, loads, outs, scratch):
    packed, low, high, gain1, gain2, qkv, bias, left, right, proj, up, down, select = loads
    half, d = low.ref.shape
    heads = bias.ref.shape[1] // (WIN * WIN)
    shift = half * (WIN // 2) // ROWS
    back = lambda v: jnp.concatenate([v[half - shift :], v[: half - shift]], axis=0)
    own = turned(low(), high())
    gain = gain1()[layer : layer + 1, :]
    normed_s = layer_norm(turned(left(), right()), gain).astype(BF16)
    packed = packed()[...]
    packed_s = mm(normed_s, qkv()[:, d:]).astype(BF16)
    query, key, value = packed[:, :d], packed[:, d : 2 * d], packed[:, 2 * d :]
    key_s, value_s = packed_s[:, :d], packed_s[:, d:]
    win_rows = ROWS // WIN
    part = half // win_rows
    span = WIN * WIN
    bias_all = bias()[...]
    mask = head_mask(heads, span, d)
    outs_m, outs_w = [[], []], [[], []]
    for w in range(win_rows):
        near = slice(w * part, (w + 1) * part)
        far = slice(half + w * part, half + (w + 1) * part)
        for side in range(2):
            if side == 0:
                q = query[near]
                k = jnp.concatenate([key_s[near], key[near]], axis=0)
                v = jnp.concatenate([value_s[near], value[near]], axis=0)
                b = bias_all[part:]
            else:
                q = query[far]
                k = jnp.concatenate([key[far], key_s[far]], axis=0)
                v = jnp.concatenate([value[far], value_s[far]], axis=0)
                b = bias_all[:part]
            blocked = None
            if w == win_rows - 1:
                shape = (part, heads * span)
                q_up = iota(shape, 0) % part >= part // 2
                k_up = iota(shape, 1) % part >= part // 2
                blocked = q_up != k_up
            out, wts = attend_rows(q, k, v, b, heads, mask, blocked)
            outs_m[side].append(out)
            outs_w[side].append(wts)
    total = by_group(jnp.concatenate(outs_w[0] + outs_w[1], axis=0), [mask] * (d // LANES))
    mixed = (jnp.concatenate(outs_m[0] + outs_m[1], axis=0) / total).astype(BF16)
    attended = mm(mixed, proj()[...]).astype(BF16)
    residual = own + attended.astype(F32)
    new = feed_forward(residual, gain2()[layer : layer + 1, :], up()[...], down()[...])
    state = jnp.concatenate([back(new[:half]), back(new[half:])], axis=0)
    sent = mm(select()[...], state).astype(BF16)
    if len(outs) == 1:
        outs[0][...] = sent
        return
    rows = sent.shape[0] // (2 * len(outs))
    for x in range(2 * len(outs)):
        outs[x // 2][x % 2] = sent[x * rows : (x + 1) * rows]


def return_chunk(stage, i):
    return i if stage == 0 else 2 * NEAR + 2 * i + stage - 1


def back_part(size, first, me_ref, chunks, mix, unembed, p_ref, slot_ref):
    rows = jnp.concatenate([one()[...].reshape(-1, one.ref.shape[-1]) for one in chunks], axis=0)
    unembed_ref = unembed()
    pix = unembed_ref.shape[0] // LANES
    for j in range(0, pix, 2):
        cols = slice(j * LANES, (j + 2) * LANES)
        p_ref[:, cols] = mm_nt(rows, unembed_ref[cols, :])
    mix_ref = mix()

    def group(g, carry):
        got = p_ref[pl.ds(pl.multiple_of(g * 2 * GROUP, 2 * GROUP), 2 * GROUP), :]
        data = jnp.concatenate([lay_tiles(got[:GROUP], pix), lay_tiles(got[GROUP:], pix)], axis=0)
        where = first + g
        if size is not None:
            chunk = lax.div(g, size)
            where = (return_chunk(first, chunk) ^ me_ref[0]) * size + g - chunk * size
        out = mm(mix_ref[where], data.astype(BF16))
        to = pl.ds(pl.multiple_of(g * GROUP, GROUP), GROUP)
        for i in range(pix):
            slot_ref[to, i * LANES : (i + 1) * LANES] = out[i * GROUP : (i + 1) * GROUP]
        return carry

    lax.fori_loop(0, rows.shape[0] // (2 * GROUP), group, 0, unroll=12)


def back_kernel(size, first, me_ref, loads, outs, scratch):
    *chunks, unembed, mix = loads
    back_part(size, first, me_ref, chunks, mix, unembed, *scratch)
    outs[0][...] = scratch[1][...].astype(BF16)


def last_kernel(size, first, me_ref, loads, outs, scratch):
    *chunks, unembed, mix, prior, send = loads
    if size is not None:
        *chunks, own_far = chunks
    back_part(size, first, me_ref, chunks, mix, unembed, *scratch)
    slot_ref, out_ref = scratch[1], outs[0]
    pix = unembed.ref.shape[0] // LANES
    pd, total = out_ref.shape
    ch = total // pix
    prior_ref = prior()
    owner = send()
    onehot = (iota((pd, owner.shape[1]), 0) == owner[:1, :]).astype(F32).astype(BF16)
    tiles = [None] * (-(-total // LANES))
    for j in range(0, pix, 2):
        cols = slice(j * LANES, (j + 2) * LANES)
        slots = [prior_ref[:, cols]] + ([own_far()[:, cols]] if size is not None else [])
        slots = jnp.concatenate([*slots, slot_ref[:, cols].astype(BF16)], axis=0)
        both = mm(onehot, slots)
        for jj in (j, j + 1):
            val = both[:, (jj - j) * LANES : (jj - j + 1) * LANES]
            t, off = divmod(ch * jj, LANES)
            if off:
                val = pltpu.roll(val, off, 1)
            lane = iota(val.shape, 1)
            low, high = jnp.where(lane >= off, val, 0.0), jnp.where(lane < off, val, 0.0)
            for tt, piece in ((t, low), (t + 1, high)):
                if tt == t + 1 and off + ch <= LANES:
                    continue
                tiles[tt] = piece if tiles[tt] is None else tiles[tt] + piece
    for t, tile in enumerate(tiles):
        hi = min((t + 1) * LANES, total)
        out_ref[:, t * LANES : hi] = tile[:, : hi - t * LANES]


def swap(value, axis):
    return lax.all_to_all(value, axis, split_axis=0, concat_axis=0, tiled=True)


def swap_pairs(value, axis):
    count = lax.axis_size(axis)
    rows, width = value.shape
    cap = rows // (2 * count)
    if cap % GROUP == 0:
        return swap(value, axis)
    groups = rows // (2 * GROUP)
    v = value.reshape(groups, 2, GROUP, width).transpose(1, 0, 2, 3).reshape(2, count, cap, width)
    v = swap(v.transpose(1, 0, 2, 3).reshape(rows, width), axis)
    v = v.reshape(count, 2, cap, width).transpose(1, 0, 2, 3).reshape(2, groups, GROUP, width)
    return v.transpose(1, 0, 2, 3).reshape(rows, width)


def flip(value, axis, bits):
    count = lax.axis_size(axis)
    return lax.ppermute(value, axis, [(source, source ^ bits) for source in range(count)])


def from_behind(value, axis, steps):
    count = lax.axis_size(axis)
    pairs = [(source, (source + steps) % count) for source in range(count)]
    return lax.ppermute(value, axis, pairs)


STAGES = 2
NEAR = 4


def body(
    bands, send_table, recv_table, regrid_weight, embed_weight, norm1_gain, qkv_weight, rel_bias,
    proj_weight, norm2_gain, up_weight, down_weight, unembed_weight,
):
    pd, width = bands.shape
    slots = send_table.shape[1]
    kk = recv_table.shape[0]
    d = embed_weight.shape[1]
    pixsq = regrid_weight.shape[1] // kk
    pix = int(round(pixsq**0.5))
    wide = pix * LANES
    count = lax.axis_size("tile")
    cap = slots // count
    chips = count // 2
    direct = chips == 2 * NEAR and cap % GROUP == 0
    vm = pltpu.VMEM
    per = slots // STAGES
    groups = per // GROUP
    my = lax.axis_index("tile").astype(jnp.int32).reshape(1)
    if not direct:
        my = my * 0

    if direct:
        turns = [*range(NEAR, chips), *range(NEAR - 1, 0, -1)]

        outgoing = call(pick_direct_kernel, [In(send_table), In(bands)],
                        [sds((2, cap, width), BF16)] * chips, [vm((count, cap, width), BF16)], my, flops=1e10)
        came = [outgoing[0]] + [None] * (chips - 1)
        for s in turns:
            came[s] = flip(outgoing[s], "tile", 2 * s)
    else:
        outgoing = call(pick_kernel, [In(send_table), In(bands)], [sds((slots, width), BF16)])
        incoming = swap(outgoing, "tile")

    heads = rel_bias.shape[1]
    span = WIN * WIN
    wsend = call(weights_kernel, [In(recv_table), In(regrid_weight)], [sds((2 * slots, pixsq), BF16)],
                 flops=1e10, after=[outgoing[0] if direct else outgoing])
    wback = swap_pairs(wsend, "tile")
    scatter_a, scatter_b, embed_pad, bias, select = call(
        functools.partial(tables_kernel, cap, direct),
        [In(recv_table), In(embed_weight), In(rel_bias.transpose(1, 0, 2))],
        [sds((pd, slots // 2), BF16), sds((pd, 3 * slots // 2), BF16), sds((wide, d), BF16),
         sds((rel_bias.shape[0], span, heads * span), F32), sds((2 * slots, pd), BF16)],
        [vm((heads, 2 * LANES), F32)], my, flops=2e9, after=[wsend])
    mix = call(functools.partial(mix_kernel, cap), [In(recv_table), In(regrid_weight)],
               [sds((slots // GROUP, 2 * pix * GROUP, pix * GROUP), BF16)], (), my, flops=2e9, after=[embed_pad])

    def relay(arrays, after=()):
        shape = (len(arrays), *arrays[0].shape[1:])
        return call(relay_kernel, [at(x, 1) for x in arrays], [sds(shape, BF16)], after=after)

    def regrid_scratch(rows):
        return [vm((rows, wide), F32), vm((2 * rows, wide), BF16)]

    if direct:
        near = [at(x, 0) for x in came[:NEAR]]
    else:
        near, far = [at(incoming, slice(0, slots // 4))], [at(incoming, slice(slots // 4, slots))]
    total = call(functools.partial(early_kernel, pix, direct),
                 [*near, In(mix), In(scatter_a), In(embed_pad)], [sds((pd, d), F32)],
                 regrid_scratch(slots // 4), flops=2e9)
    if direct:
        for_partner = relay(came, [total])
        passed = flip(for_partner, "tile", 1)
        far = [at(passed, i) for i in range(NEAR)]
        far += [y for i in range(NEAR, chips) for y in (at(came[i], 0), at(passed, i))]

    def layer(n):
        return [In(norm1_gain), In(norm2_gain), at(qkv_weight, n), at(bias, n)], [
            at(proj_weight, n), at(up_weight, n), at(down_weight, n)]

    half = pd // 2
    ins_a, ins_b = layer(0)
    low, high = call(
        functools.partial(first_kernel, pix, direct, 0),
        [*far, In(mix), In(scatter_b), In(embed_pad), In(total), *ins_a, *ins_b],
        [sds((half, d), BF16)] * 2, regrid_scratch(3 * slots // 4), flops=4e9)
    right = from_behind(low, "tile", -1)
    left = from_behind(high, "tile", 1)
    ins_a, ins_b = layer(1)
    packed = call(functools.partial(own_kernel, 1), [In(low), In(high), In(norm1_gain), at(qkv_weight, 1)],
                  [sds((pd, 3 * d), BF16)], flops=2e8)
    rows = 2 * cap
    sent = call(
        functools.partial(second_kernel, 1),
        [In(packed), In(low), In(high), *ins_a, In(left), In(right), *ins_b, In(select)],
        [sds((2, rows, d), BF16)] * chips if direct else [sds((2 * slots, d), BF16)], flops=2e9)
    one_sent = sent[0] if direct else sent
    size = cap // GROUP if direct else None
    mix_back, unembed_pad, owner = call(
        functools.partial(prep_back_kernel, size), [In(wback), In(unembed_weight.T), In(send_table)],
        [sds((slots // GROUP, pix * GROUP, 2 * pix * GROUP), BF16), sds((wide, d), BF16),
         sds((GROUP, slots), jnp.int32)], (), my, flops=2e9, after=[one_sent])

    back_scratch = [vm((2 * per, wide), F32), vm((per, wide), F32)]
    if direct:
        got = [sent[0]] + [None] * (chips - 1)
        for s in turns:
            got[s] = flip(sent[s], "tile", 2 * s)
        near_all = relay(got[:NEAR], [mix_back])
        near_pass = flip(near_all, "tile", 1)
        near = [y for i, x in enumerate(got[:NEAR]) for y in (at(x, 0), at(near_pass, i))]
    else:
        got = swap_pairs(sent, "tile").reshape(STAGES, 2 * per, d)
        near, far = [at(got, 0)], [at(got, 1)]
    prior = call(functools.partial(back_kernel, size, 0), [*near, In(unembed_pad), In(mix_back)],
                 [sds((per, wide), BF16)], back_scratch, my, flops=2e9)
    if direct:
        far_all = relay(got[NEAR:], [prior])
        far_pass = flip(far_all, "tile", 1)
        own_far = call(functools.partial(back_kernel, size, 1), [*[at(x, 0) for x in got[NEAR:]], In(unembed_pad), In(mix_back)],
                       [sds((per // 2, wide), BF16)], [vm((per, wide), F32), vm((per // 2, wide), F32)], my, flops=1e9, after=[far_all])
        far = [at(far_pass, i) for i in range(NEAR)]
    if direct:
        back_scratch = [vm((per, wide), F32), vm((per // 2, wide), F32)]
        far.append(In(own_far))
    return call(functools.partial(last_kernel, size, 2 if direct else groups), [*far, In(unembed_pad), In(mix_back), In(prior), In(owner)],
                [sds((pd, width), F32)], back_scratch, my, flops=3e9)


def solution(mesh):
    in_specs = (
        P(("groups", "tile"), None), P("tile", None), P(None, "tile"), P("tile", None),
        P(), P(), P(), P(), P(), P(), P(), P(), P(),
    )
    out_specs = P(("groups", "tile"), None)
    return jax.shard_map(body, mesh=mesh, in_specs=in_specs, out_specs=out_specs, check_vma=False)
```
